128 devices in a mesh: read: 16 (over x_lo, z, core), tm: 8 (over y, x_hi).
Axes of the slice: x: 4 (x_hi: 2, x_lo: 2; x = x_hi * 2 + x_lo), y: 4, z: 4, core: 2. Of those that a mesh axis runs over, the one named last changes fastest.
Arguments:
- student_in: bfloat16 [16, 4096, 512], P('read', 'tm'), may hold values from -6 to 6
- teacher_rows: bfloat16 [16, 4096, 768], P('read', 'tm'), may hold values from -6 to 6
- valid: int32 [16], P('read'), may hold values from 1024 to 4096, as said below
- conv_weight: bfloat16 [4, 3, 512, 512], replicated, may hold values from -0.15625 to 0.15625
- head_weight: bfloat16 [512, 5120], replicated, may hold values from -0.25 to 0.25
- teacher_head_weight: bfloat16 [768, 5120], replicated, may hold values from -0.21875 to 0.21875
Outputs:
- grad_conv: float32 [4, 3, 512, 512], P(None, None, 'read', 'tm')
- grad_head: float32 [512, 5120], P('read', 'tm')
The draws below stay inside these ranges and needn't reach their ends.
Inputs may be any that keep to these rules, and one draw needn't show every extreme that they name: One read of each draw has all 4096 frames valid.
All inputs are finite; a program needn't handle non-finite values.
Results may differ from the reference program's by a relative error of at most 0.002.
Values may be sent and summed in bfloat16 or wider, within the bound.
No kernel may reach another device: no remote copies, remote signals or barrier semaphores. Data moves between devices by JAX's collectives and lax.ppermute only.
A program may use at most 192 MiB of HBM per device.

```python
import math
import jax
import jax.numpy as jnp
from jax import lax

D = 512
V = 5120
TE = 768
LAYERS = 4
BASE_DILATION = 32
FRAMES = 4096
READS = 16


def draw_valid(key, part):
    lengths = jax.random.randint(key, (READS,), FRAMES // 4, FRAMES + 1)
    position = jax.random.randint(jax.random.fold_in(key, 7), (), 0, READS)
    return lengths.at[position].set(FRAMES).astype(jnp.int32)


def level_of(key, dims, shards, low, high):
    factor_of, own = 1.0, jax.random.fold_in(key, 6)
    for dim, shards_of in shards:
        heights = jnp.exp(jax.random.uniform(jax.random.fold_in(own, dim), (shards_of,), jnp.float32, low / len(shards), high / len(shards)))
        factor_of = factor_of * jnp.repeat(heights, dims[dim] // shards_of).reshape([-1 if axis == dim else 1 for axis in range(len(dims))])
    return factor_of


def normal_values(key, shape, deviation, bound, split=(), held_as=jnp.bfloat16):
    level = level_of(key, shape, split, -0.22, 0.18) if split else 1.0
    entries = jax.random.normal(key, shape, jnp.float32) * deviation * level
    return jnp.minimum(jnp.maximum(entries, -bound), bound).astype(held_as)


def setup_inputs(seed: int = 0) -> dict:
    keys = jax.random.split(jax.random.key(seed), 7)
    return {
        "student_in": normal_values(keys[0], (READS, FRAMES, D), 1.0, 6.0, ((0, 16), (1, 8))),
        "teacher_rows": normal_values(keys[1], (READS, FRAMES, TE), 1.0, 6.0, ((0, 16), (1, 8))),
        "valid": draw_valid(jax.random.fold_in(keys[6], 71), 0),
        "conv_weight": normal_values(keys[3], (LAYERS, 3, D, D), (3 * D) ** -0.5, 0.15625),
        "head_weight": normal_values(keys[4], (D, V), D ** -0.5, 0.25),
        "teacher_head_weight": normal_values(keys[5], (TE, V), TE ** -0.5, 0.21875),
    }


def convolved_rows(hidden, weight, receptive_reach, frames):
    padded = jnp.pad(hidden, ((receptive_reach, receptive_reach), (0, 0)))
    total = jnp.zeros((frames, weight.shape[2]), jnp.float32)
    for tap_index in range(3):
        start = tap_index * receptive_reach
        total = total + jnp.dot(padded[start:start + frames], weight[tap_index], preferred_element_type=jnp.float32)
    return (padded, total)

def one_read(student_one, teacher_one, valid_one, conv_weight, head_weight, teacher_head_weight, loss_scale):
    frames = student_one.shape[0]
    signal_frame_mask = (jnp.arange(frames) < valid_one).astype(jnp.float32)[:, None]
    hidden = student_one
    saved = []
    for layer_number in range(LAYERS):
        receptive_reach = BASE_DILATION * 2 ** layer_number
        padded, pre = convolved_rows(hidden, conv_weight[layer_number], receptive_reach, frames)
        saved.append((padded, pre, receptive_reach))
        hidden = (signal_frame_mask * (hidden.astype(jnp.float32) + jax.nn.silu(pre))).astype(jnp.bfloat16)
    student_sum = jnp.dot(hidden, head_weight, preferred_element_type=jnp.float32)
    squash = jnp.tanh(student_sum)
    student = 5.0 * squash
    teacher = 5.0 * jnp.tanh(jnp.dot(teacher_one, teacher_head_weight, preferred_element_type=jnp.float32))
    prob_teacher = jax.nn.softmax(teacher, axis=-1)
    prob_student = jax.nn.softmax(student, axis=-1)
    g_score = (loss_scale * signal_frame_mask * (prob_student - prob_teacher) * 5.0 * (1.0 - squash * squash)).astype(jnp.bfloat16)
    grad_head = jnp.dot(hidden.T, g_score, preferred_element_type=jnp.float32)
    g_hidden = jnp.dot(g_score, head_weight.T, preferred_element_type=jnp.float32)
    grads = []
    for layer_number in reversed(range(LAYERS)):
        padded, pre, receptive_reach = saved[layer_number]
        g_act = signal_frame_mask * g_hidden
        sigma = jax.nn.sigmoid(pre)
        g_pre = (g_act * sigma * (1.0 + pre * (1.0 - sigma))).astype(jnp.bfloat16)
        taps = []
        for tap_index in range(3):
            start = tap_index * receptive_reach
            taps.append(jnp.dot(padded[start:start + frames].T, g_pre, preferred_element_type=jnp.float32))
        grads.append(jnp.stack(taps))
        if layer_number > 0:
            g_padded = jnp.pad(g_pre, ((receptive_reach, receptive_reach), (0, 0)))
            total = g_act
            for tap_index in range(3):
                start = (2 - tap_index) * receptive_reach
                total = total + jnp.dot(g_padded[start:start + frames], conv_weight[layer_number, tap_index].T, preferred_element_type=jnp.float32)
            g_hidden = total
    grad_conv = jnp.stack(grads[::-1])
    return (grad_conv, grad_head)

def reference(student_in, teacher_rows, valid, conv_weight, head_weight, teacher_head_weight):
    loss_scale = V / (3.0 * math.sqrt(READS * FRAMES))

    def distill_step_read(carry, items):
        student_one, teacher_one, valid_one = items
        grad_conv, grad_head = one_read(student_one, teacher_one, valid_one, conv_weight, head_weight, teacher_head_weight, loss_scale)
        return ((carry[0] + grad_conv, carry[1] + grad_head), None)
    start = (jnp.zeros((LAYERS, 3, D, D), jnp.float32), jnp.zeros((D, V), jnp.float32))
    totals, unused = lax.scan(distill_step_read, start, (student_in, teacher_rows, valid))
    return (totals[0], totals[1])
```

```python
import math

import jax
import jax.numpy as jnp
from jax import lax
from jax.sharding import PartitionSpec as P

LAYERS = 4
BASE_DILATION = 32
AXES = ("read", "tm")
READ, TM = 16, 8
CLASSES = BASE_DILATION // TM


def device_index(x, y, z, core):
    return (((x % 2) * 4 + z) * 2 + core) * TM + y * 2 + x // 2


BITS = [(a, b, c) for a in range(2) for b in range(2) for c in range(2)]


def near_groups():
    groups = []
    for core in range(2):
        for x0, y0, z0 in BITS:
            group = [0] * 8
            for a, b, c in BITS:
                x, y, z = ((2 * o + k + core) % 4 for o, k in ((x0, a), (y0, b), (z0, c)))
                group[(x % 2) * 4 + (y % 2) * 2 + z % 2] = device_index(x, y, z, core)
            groups.append(group)
    return groups


def far_groups():
    return [
        [device_index(x + 2 * a, y + 2 * b, z + 2 * c, core) for a, b, c in BITS]
        for core in range(2)
        for x, y, z in BITS
    ]


def other_core():
    return [(d, d ^ TM) for d in range(READ * TM)]


def frame_groups():
    return [[r * TM + t for t in range(TM)] for r in range(READ)]


def exchange(x, groups):
    return lax.all_to_all(x, AXES, 0, 0, tiled=True, axis_index_groups=groups)


def encode(x):
    return (x * jnp.abs(x)).astype(jnp.bfloat16)


def decode(y):
    y = y.astype(jnp.float32)
    return y * lax.rsqrt(jnp.maximum(jnp.abs(y), 1e-37))


def by_class(x):
    frames = x.shape[0]
    row = lax.broadcasted_iota(jnp.int32, (frames, frames), 0)
    col = lax.broadcasted_iota(jnp.int32, (frames, frames), 1)
    per = frames // TM
    source = (row % per) // CLASSES * BASE_DILATION + row // per * CLASSES + row % CLASSES
    select = (col == source).astype(jnp.bfloat16)
    return jnp.dot(select, x, preferred_element_type=jnp.float32).astype(jnp.bfloat16)


def pair_sum(x, core):
    mine = lax.dynamic_index_in_dim(x, core, axis=3, keepdims=False)
    other = lax.dynamic_index_in_dim(x, 1 - core, axis=3, keepdims=False)
    return mine + decode(lax.ppermute(encode(other), AXES, other_core()))


def reduce_groups(x, groups):
    got = exchange(encode(x), groups)
    return jnp.sum(decode(got), axis=0)


def on_device(student_in, teacher_rows, valid, conv_weight, head_weight, teacher_head_weight):
    _, frames, width = student_in.shape
    scores = head_weight.shape[1]
    loss_scale = scores / (3.0 * math.sqrt(READ * TM * frames))
    core = lax.axis_index("read") % 2
    hidden = exchange(by_class(student_in[0]), frame_groups())
    teacher_in = exchange(by_class(teacher_rows[0]), frame_groups())
    row = jnp.arange(frames, dtype=jnp.int32)
    position = row // CLASSES * BASE_DILATION + lax.axis_index("tm") * CLASSES + row % CLASSES
    mask = (position < valid[0]).astype(jnp.float32)[:, None]

    saved = []
    for layer in range(LAYERS):
        reach = CLASSES * 2**layer
        padded = jnp.pad(hidden, ((reach, reach), (0, 0)))
        pre = jnp.zeros((frames, width), jnp.float32)
        for tap in range(3):
            pre = pre + jnp.dot(
                padded[tap * reach : tap * reach + frames],
                conv_weight[layer, tap],
                preferred_element_type=jnp.float32,
            )
        saved.append((padded, pre, reach))
        hidden = (mask * (hidden.astype(jnp.float32) + jax.nn.silu(pre))).astype(jnp.bfloat16)

    squash = jnp.tanh(jnp.dot(hidden, head_weight, preferred_element_type=jnp.float32))
    teacher = jnp.tanh(jnp.dot(teacher_in, teacher_head_weight, preferred_element_type=jnp.float32))
    exp_s, exp_t = jnp.exp(5.0 * squash), jnp.exp(5.0 * teacher)
    inv_s = 1.0 / jnp.sum(exp_s, axis=1, keepdims=True)
    inv_t = 1.0 / jnp.sum(exp_t, axis=1, keepdims=True)
    scale = 5.0 * loss_scale * mask
    g_score = (
        scale * (exp_s * inv_s - exp_t * inv_t) * (1.0 - squash * squash)
    ).astype(jnp.bfloat16)
    head_part = jnp.dot(hidden.T, g_score, preferred_element_type=jnp.float32)
    g_hidden = jnp.dot(g_score, head_weight.T, preferred_element_type=jnp.float32)

    head_mine = pair_sum(head_part.reshape(2, 2, 2, 2, 32, 2, 2, scores // 4), core)
    head_near = head_mine.transpose(0, 5, 2, 1, 4, 3, 6).reshape(8, 4 * 32, scores // 4)
    head_sum = reduce_groups(head_near, near_groups())

    grads = []
    for layer in reversed(range(LAYERS)):
        padded, pre, reach = saved[layer]
        g_act = mask * g_hidden
        sigma = jax.nn.sigmoid(pre)
        g_pre = (g_act * sigma * (1.0 + pre * (1.0 - sigma))).astype(jnp.bfloat16)
        grads.append(
            jnp.stack(
                [
                    jnp.dot(
                        padded[tap * reach : tap * reach + frames].T,
                        g_pre,
                        preferred_element_type=jnp.float32,
                    )
                    for tap in range(3)
                ]
            )
        )
        if layer > 0:
            g_padded = jnp.pad(g_pre, ((reach, reach), (0, 0)))
            g_hidden = g_act
            for tap in range(3):
                start = (2 - tap) * reach
                g_hidden = g_hidden + jnp.dot(
                    g_padded[start : start + frames],
                    conv_weight[layer, tap].T,
                    preferred_element_type=jnp.float32,
                )
    taps = LAYERS * 3
    conv_part = jnp.concatenate(grads[::-1])
    conv_rows = conv_part.reshape(taps, 2, 2, 2, 2, 32, 2, 2, width // 4).transpose(1, 2, 3, 4, 0, 5, 6, 7, 8)
    conv_mine = pair_sum(conv_rows, core)
    conv_near = conv_mine.transpose(0, 6, 2, 3, 1, 5, 4, 7).reshape(8, taps * 4 * 32, width // 4)
    conv_sum = reduce_groups(conv_near, near_groups())

    head_far = head_sum.reshape(2, 2, 32, 2, scores // 8).transpose(3, 1, 0, 2, 4)
    conv_far = conv_sum.reshape(taps, 2, 2, 32, 2, width // 8).transpose(4, 2, 1, 0, 3, 5)
    flat = jnp.concatenate(
        [head_far.reshape(8, -1, 128), conv_far.reshape(8, -1, 128)], axis=1
    )
    total = reduce_groups(flat, far_groups())
    cut = 32 * scores // 8 // 128
    grad_head = total[:cut].reshape(32, scores // 8)
    grad_conv = total[cut:].reshape(LAYERS, 3, 32, width // 8)
    return (grad_conv, grad_head)


def solution(mesh):
    return jax.shard_map(
        on_device,
        mesh=mesh,
        in_specs=(P("read", "tm", None), P("read", "tm", None), P("read"), P(), P(), P()),
        out_specs=(P(None, None, "read", "tm"), P("read", "tm")),
        check_vma=False,
    )
```

```python
import functools
import math

import jax
import jax.numpy as jnp
from jax import lax
from jax.experimental import pallas as pl
from jax.experimental.pallas import tpu as pltpu
from jax.sharding import PartitionSpec as P

LAYERS, TAPS = 4, 3
BASE_DILATION = 32
AXES = ("read", "tm")
READ, TM = 16, 8
CLASSES = BASE_DILATION // TM
PAD = CLASSES * 2 ** (LAYERS - 1)
BITS = [(a, b, c) for a in range(2) for b in range(2) for c in range(2)]
F32, BF16 = jnp.float32, jnp.bfloat16


def near_of(core, v):
    return (v // 2) ^ (v % 2) if core == 0 else v // 2


def far_of(core, v):
    return v // 2 if core == 0 else (v // 2) ^ (v % 2)


def high_low(core, near, far):
    return (far if core == 0 else near, near ^ far)


def device_index(x, y, z, core):
    return (((x % 2) * 4 + z) * 2 + core) * TM + y * 2 + x // 2


def groups_of(fixed, order):
    groups = {}
    for core in range(2):
        for x in range(4):
            for y in range(4):
                for z in range(4):
                    key = (core, fixed(core, x), fixed(core, y), fixed(core, z))
                    place = order(core, x) * 4 + order(core, y) * 2 + order(core, z)
                    groups.setdefault(key, [0] * 8)[place] = device_index(x, y, z, core)
    return list(groups.values())


def near_groups():
    def cube(core, v):
        return (v + core) % 4 // 2

    return groups_of(cube, near_of)


def far_groups():
    return groups_of(near_of, far_of)


def other_core():
    return [(d, d ^ TM) for d in range(READ * TM)]


def frame_groups():
    return [[r * TM + t for t in range(TM)] for r in range(READ)]


def exchange(x, groups):
    return lax.all_to_all(x, AXES, 0, 0, tiled=True, axis_index_groups=groups)


def encode(x):
    return (x * jnp.abs(x)).astype(BF16)


def decode(y):
    y = y.astype(F32)
    return y * lax.rsqrt(jnp.maximum(jnp.abs(y), 1e-37))


def low_lanes(shape):
    return lax.broadcasted_iota(jnp.int32, shape, len(shape) - 1) < 64


def dot(a, b):
    return jnp.dot(a, b, preferred_element_type=F32)


def dot_nt(a, b):
    return lax.dot_general(a, b, (((1,), (1,)), ((), ())), preferred_element_type=F32)


def params(*kinds):
    return pltpu.CompilerParams(dimension_semantics=kinds, vmem_limit_bytes=62 * 1024 * 1024)


def whole():
    return pl.BlockSpec(memory_space=pltpu.VMEM)


def frame_mask(sc_ref, frames):
    row = lax.broadcasted_iota(jnp.int32, (frames, 1), 0)
    position = row // CLASSES * BASE_DILATION + sc_ref[1] * CLASSES + row % CLASSES
    return (position < sc_ref[0]).astype(F32)


def regroup_kernel(x_ref, out_ref):
    frames = x_ref.shape[0]
    row = lax.broadcasted_iota(jnp.int32, (frames, frames), 0)
    col = lax.broadcasted_iota(jnp.int32, (frames, frames), 1)
    per = frames // TM
    source = (row % per) // CLASSES * BASE_DILATION + row // per * CLASSES + row % CLASSES
    select = jnp.where(col == source, 1.0, 0.0).astype(BF16)
    out_ref[...] = dot(select, x_ref[...]).astype(BF16)


def regroup(x):
    return pl.pallas_call(
        regroup_kernel,
        out_shape=jax.ShapeDtypeStruct(x.shape, BF16),
        in_specs=[whole()],
        out_specs=whole(),
        name="regroup",
    )(x)


def conv_kernel(sc_ref, x_ref, w_ref, saved_ref, pre_ref, last_ref, pad_s, tap_s):
    layer = pl.program_id(0)
    frames = x_ref.shape[0]

    @pl.when(layer == 0)
    def _():
        pad_s[...] = jnp.zeros_like(pad_s)
        pad_s[PAD : PAD + frames] = x_ref[...].astype(F32)

    for at in range(LAYERS):

        @pl.when(layer == at)
        def _():
            reach = CLASSES * 2**at
            tap_s[0] = pad_s[PAD - reach : PAD - reach + frames].astype(BF16)
            tap_s[1] = pad_s[PAD + reach : PAD + reach + frames].astype(BF16)

    hidden = pad_s[PAD : PAD + frames]
    middle = hidden.astype(BF16)
    saved_ref[0] = middle
    pre = dot(tap_s[0], w_ref[0, 0]) + dot(middle, w_ref[0, 1]) + dot(tap_s[1], w_ref[0, 2])
    pre_ref[0] = pre
    new = (frame_mask(sc_ref, frames) * (hidden + jax.nn.silu(pre))).astype(BF16)
    last_ref[...] = new
    pad_s[PAD : PAD + frames] = new.astype(F32)


def convolve(sc, x, weight):
    frames, width = x.shape
    one = pl.BlockSpec((1, frames, width), lambda i: (i, 0, 0))
    flat = pl.BlockSpec((frames, width), lambda i: (0, 0))
    return pl.pallas_call(
        conv_kernel,
        grid=(LAYERS,),
        in_specs=[
            pl.BlockSpec(memory_space=pltpu.SMEM),
            flat,
            pl.BlockSpec((1, TAPS, width, width), lambda i: (i, 0, 0, 0)),
        ],
        out_specs=[one, one, flat],
        out_shape=[
            jax.ShapeDtypeStruct((LAYERS, frames, width), BF16),
            jax.ShapeDtypeStruct((LAYERS, frames, width), F32),
            jax.ShapeDtypeStruct((frames, width), BF16),
        ],
        scratch_shapes=[
            pltpu.VMEM((frames + 2 * PAD, width), F32),
            pltpu.VMEM((2, frames, width), BF16),
        ],
        compiler_params=params("arbitrary"),
        cost_estimate=pl.CostEstimate(
            flops=2 * LAYERS * TAPS * frames * width * width,
            bytes_accessed=LAYERS * (TAPS * width * width * 2 + frames * width * 6),
            transcendentals=LAYERS * frames * width,
        ),
        name="convolve",
    )(sc, x, weight)


def head_kernel(scale, tiles, sc_ref, h_ref, t_ref, ws_ref, wt_ref, mine_ref, other_ref, g_ref,
                sq_s, es_s, et_s, sum_s, ht_s, gs_s, res_s):
    step = pl.program_id(0)
    frames, width = h_ref.shape
    tile = ws_ref.shape[1]
    sub = 256

    @pl.when(step == 0)
    def _():
        sum_s[...] = jnp.zeros_like(sum_s)

    @pl.when(step < tiles)
    def _():
        for c in range(tile // sub):
            cols = slice(c * sub, (c + 1) * sub)
            squash = jnp.tanh(dot(h_ref[...], ws_ref[:, cols]))
            exp_s = jnp.exp(5.0 * squash)
            sq_s[step, :, cols] = squash
            es_s[step, :, cols] = exp_s
            sum_s[0] += exp_s[:, :128] + exp_s[:, 128:]
            exp_t = jnp.exp(5.0 * jnp.tanh(dot(t_ref[...], wt_ref[:, cols])))
            et_s[step, :, cols] = exp_t
            sum_s[1] += exp_t[:, :128] + exp_t[:, 128:]

    @pl.when(step == tiles)
    def _():
        factor = scale * frame_mask(sc_ref, frames)
        for i in range(2):
            inverse = factor / jnp.sum(sum_s[i], axis=1, keepdims=True)
            sum_s[i] = jnp.broadcast_to(inverse, (frames, 128))
        ht_s[...] = h_ref[...].T
        g_ref[...] = jnp.zeros_like(g_ref)

    @pl.when(step >= tiles)
    def _():
        at = step - tiles
        for c in range(tile // 128):
            cols = slice(c * 128, (c + 1) * 128)
            squash = sq_s[at, :, cols]
            p = es_s[at, :, cols] * sum_s[0] - et_s[at, :, cols] * sum_s[1]
            gs_s[:, cols] = (p * (1.0 - squash * squash)).astype(BF16)
        res_s[...] = dot(ht_s[...], gs_s[...])
        g_ref[...] += dot_nt(gs_s[...], ws_ref[...])
        first = sc_ref[2] == 0
        half = tile // 2
        for nx, nz, fz in BITS:
            for fx in range(2):
                found = []
                for core in range(2):
                    xh, xl = high_low(core, nx, fx)
                    zh, zl = high_low(core, nz, fz)
                    r = ((xl * 4 + zh * 2 + zl) * 2 + core) * 32
                    found.append(res_s[r : r + 32, xh * half : (xh + 1) * half])
                to = slice(fx * half, (fx + 1) * half)
                mine_ref[nx, 0, nz, fz, 0, :, to] = jnp.where(first, found[0], found[1])
                other_ref[nx, 0, nz, fz, 0, :, to] = encode(jnp.where(first, found[1], found[0]))


def heads(sc, hidden, teacher_in, head_weight, teacher_head_weight, loss_scale):
    frames, width = hidden.shape
    wide = teacher_in.shape[1]
    scores = head_weight.shape[1]
    tiles = 4
    tile = scores // tiles

    def place(i, core):
        y = jnp.maximum(i - tiles, 0)
        high, low = y // 2, y % 2
        even = core == 0
        near = jnp.where(even, high ^ low, high)
        far = jnp.where(even, high, high ^ low)
        return (0, near, 0, 0, far, 0, 0)

    block = (2, 1, 2, 2, 1, 32, tile)
    shape = (2, 2, 2, 2, 2, 32, tile)
    kernel = functools.partial(head_kernel, 5.0 * loss_scale, tiles)
    big = pltpu.VMEM((tiles, frames, tile), F32)
    return pl.pallas_call(
        kernel,
        grid_spec=pltpu.PrefetchScalarGridSpec(
            num_scalar_prefetch=1,
            grid=(2 * tiles,),
            in_specs=[
                pl.BlockSpec((frames, width), lambda i, sc: (0, 0)),
                pl.BlockSpec((frames, wide), lambda i, sc: (0, 0)),
                pl.BlockSpec((width, tile), lambda i, sc: (0, i % tiles)),
                pl.BlockSpec((wide, tile), lambda i, sc: (0, jnp.minimum(i, tiles - 1))),
            ],
            out_specs=[
                pl.BlockSpec(block, lambda i, sc: place(i, sc[2])),
                pl.BlockSpec(block, lambda i, sc: place(i, 1 - sc[2])),
                pl.BlockSpec((frames, width), lambda i, sc: (0, 0)),
            ],
            scratch_shapes=[
                big,
                big,
                big,
                pltpu.VMEM((2, frames, 128), F32),
                pltpu.VMEM((width, frames), BF16),
                pltpu.VMEM((frames, tile), BF16),
                pltpu.VMEM((width, tile), F32),
            ],
        ),
        out_shape=[
            jax.ShapeDtypeStruct(shape, F32),
            jax.ShapeDtypeStruct(shape, BF16),
            jax.ShapeDtypeStruct((frames, width), F32),
        ],
        compiler_params=params("arbitrary"),
        cost_estimate=pl.CostEstimate(
            flops=2 * frames * scores * (3 * width + wide),
            bytes_accessed=scores * (6 * width + 2 * wide),
            transcendentals=4 * frames * scores,
        ),
        name="heads",
    )(sc, hidden, teacher_in, head_weight, teacher_head_weight)


def back_kernel(sc_ref, g4_ref, h_ref, pre_ref, w_ref, mine_ref, other_ref, g_s, pad_s, tap_s, ht_s, res_s):
    step = pl.program_id(0)
    frames, width = g4_ref.shape

    @pl.when(step == 0)
    def _():
        g_s[...] = g4_ref[...]
        pad_s[...] = jnp.zeros_like(pad_s)

    g_act = frame_mask(sc_ref, frames) * g_s[...]
    pre = pre_ref[0]
    sigma = jax.nn.sigmoid(pre)
    g_pre = (g_act * sigma * (1.0 + pre * (1.0 - sigma))).astype(BF16)
    pad_s[PAD : PAD + frames] = g_pre.astype(F32)
    tap_s[1] = g_pre
    for at in range(LAYERS):

        @pl.when(step == LAYERS - 1 - at)
        def _():
            reach = CLASSES * 2**at
            tap_s[0] = pad_s[PAD + reach : PAD + reach + frames].astype(BF16)
            tap_s[2] = pad_s[PAD - reach : PAD - reach + frames].astype(BF16)

    ht_s[...] = h_ref[0].T
    first = sc_ref[2] == 0
    low = low_lanes((32, 128))
    for tap in range(TAPS):
        res_s[...] = dot(ht_s[...], tap_s[tap])
        for nz, fz in ((0, 0), (0, 1), (1, 0), (1, 1)):
            for ny, fy in ((0, 0), (0, 1), (1, 0), (1, 1)):
                found = []
                for core in range(2):
                    zh, zl = high_low(core, nz, fz)
                    yh, yl = high_low(core, ny, fy)
                    cols = slice((yh * 2 + yl) * 128, (yh * 2 + yl + 1) * 128)
                    rows = [((xl * 4 + zh * 2 + zl) * 2 + core) * 32 for xl in range(2)]
                    a, b = (res_s[r : r + 32, cols] for r in rows)
                    if core == 1:
                        b = pltpu.roll(b, 64, 1)
                    found.append((jnp.where(low, a, b), jnp.where(low, b, a)))
                for nx in range(2):
                    mine = jnp.where(first, found[0][nx], found[1][nx])
                    other = jnp.where(first, found[1][nx], found[0][nx])
                    mine_ref[nx, ny, nz, tap, fz, fy] = mine
                    other_ref[nx, ny, nz, tap, fz, fy] = encode(other)

    @pl.when(step < LAYERS - 1)
    def _():
        g_s[...] = (
            g_act
            + dot_nt(tap_s[0], w_ref[0, 0])
            + dot_nt(tap_s[1], w_ref[0, 1])
            + dot_nt(tap_s[2], w_ref[0, 2])
        )


def back(sc, g4, saved, pre, weight):
    frames, width = g4.shape
    one = pl.BlockSpec((1, frames, width), lambda i: (LAYERS - 1 - i, 0, 0))
    block = (2, 2, 2, TAPS, 2, 2, 32, width // 4)
    shape = (2, 2, 2, LAYERS * TAPS, 2, 2, 32, width // 4)
    out = pl.BlockSpec(block, lambda i: (0, 0, 0, LAYERS - 1 - i, 0, 0, 0, 0))
    return pl.pallas_call(
        back_kernel,
        grid=(LAYERS,),
        in_specs=[
            pl.BlockSpec(memory_space=pltpu.SMEM),
            pl.BlockSpec((frames, width), lambda i: (0, 0)),
            one,
            one,
            pl.BlockSpec((1, TAPS, width, width), lambda i: (LAYERS - 1 - i, 0, 0, 0)),
        ],
        out_specs=[out, out],
        out_shape=[jax.ShapeDtypeStruct(shape, F32), jax.ShapeDtypeStruct(shape, BF16)],
        scratch_shapes=[
            pltpu.VMEM((frames, width), F32),
            pltpu.VMEM((frames + 2 * PAD, width), F32),
            pltpu.VMEM((TAPS, frames, width), BF16),
            pltpu.VMEM((width, frames), BF16),
            pltpu.VMEM((width, width), F32),
        ],
        compiler_params=params("arbitrary"),
        cost_estimate=pl.CostEstimate(
            flops=2 * (2 * LAYERS - 1) * TAPS * frames * width * width,
            bytes_accessed=LAYERS * (TAPS * width * width * 8 + frames * width * 6),
            transcendentals=LAYERS * frames * width,
        ),
        name="back",
    )(sc, g4, saved, pre, weight)


def total_of(ref, *at):
    total = decode(ref[(0, *at)])
    for i in range(1, 8):
        total = total + decode(ref[(i, *at)])
    return total


def head_far_kernel(got_ref, out_ref):
    half = got_ref.shape[-1] // 2
    for fz in range(2):
        for fy in range(2):
            for fx in range(2):
                for c in range(half // 128):
                    lanes = slice(fx * half + c * 128, fx * half + (c + 1) * 128)
                    total = total_of(got_ref, fz, fy, slice(None), lanes)
                    out_ref[fx * 4 + fy * 2 + fz, c * 32 : (c + 1) * 32] = encode(total)


def head_far(got):
    tile = got.shape[-1]
    return pl.pallas_call(
        head_far_kernel,
        out_shape=jax.ShapeDtypeStruct((8, 32 * tile // 256, 128), BF16),
        in_specs=[whole()],
        out_specs=whole(),
        compiler_params=params(),
        cost_estimate=pl.CostEstimate(
            flops=8 * got.size, bytes_accessed=3 * got.size, transcendentals=got.size
        ),
        name="head_far",
    )(got)


def conv_far_kernel(got_ref, head_ref, out_ref):
    cut = head_ref.shape[1]
    out_ref[:, :cut] = head_ref[...]
    low = low_lanes((32, 128))
    half = LAYERS * TAPS // 2
    for t in range(half):
        for fz in range(2):
            for fy in range(2):
                a = total_of(got_ref, t, fz, fy)
                b = total_of(got_ref, t + half, fz, fy)
                rows = slice(cut + t * 32, cut + (t + 1) * 32)
                out_ref[fy * 2 + fz, rows] = encode(jnp.where(low, a, pltpu.roll(b, 64, 1)))
                out_ref[4 + fy * 2 + fz, rows] = encode(jnp.where(low, pltpu.roll(a, 64, 1), b))


def conv_far(got, head):
    return pl.pallas_call(
        conv_far_kernel,
        out_shape=jax.ShapeDtypeStruct((8, head.shape[1] + LAYERS * TAPS * 16, 128), BF16),
        in_specs=[whole(), whole()],
        out_specs=whole(),
        compiler_params=params(),
        name="conv_far",
    )(got, head)


def finish_kernel(got_ref, conv_ref, head_ref):
    blocks = head_ref.shape[1] // 128
    for c in range(blocks):
        head_ref[:, c * 128 : (c + 1) * 128] = total_of(got_ref, slice(c * 32, (c + 1) * 32))
    half = LAYERS * TAPS // 2
    for t in range(half):
        total = total_of(got_ref, slice((blocks + t) * 32, (blocks + t + 1) * 32))
        for tap, value in ((t, total), (t + half, pltpu.roll(total, 64, 1))):
            conv_ref[tap // TAPS, tap % TAPS] = value[:, :64]


def finish(got, scores):
    return pl.pallas_call(
        finish_kernel,
        out_shape=[
            jax.ShapeDtypeStruct((LAYERS, TAPS, 32, 64), F32),
            jax.ShapeDtypeStruct((32, scores // 8), F32),
        ],
        in_specs=[whole()],
        out_specs=[whole(), whole()],
        compiler_params=params(),
        name="finish",
    )(got)


def pair_sum(mine, other):
    return encode(mine + decode(lax.ppermute(other, AXES, other_core())))


def on_device(student_in, teacher_rows, valid, conv_weight, head_weight, teacher_head_weight):
    _, frames, width = student_in.shape
    scores = head_weight.shape[1]
    loss_scale = scores / (3.0 * math.sqrt(READ * TM * frames))
    sc = jnp.stack([valid[0], lax.axis_index("tm"), lax.axis_index("read") % 2])
    regrouped = regroup(student_in[0]).reshape(TM, frames // TM, width)
    student = exchange(regrouped, frame_groups()).reshape(frames, width)
    teacher = regroup(teacher_rows[0]).reshape(TM, frames // TM, -1)
    teacher = exchange(teacher, frame_groups()).reshape(frames, -1)

    saved, pre, hidden = convolve(sc, student, conv_weight)
    mine, other, g4 = heads(sc, hidden, teacher, head_weight, teacher_head_weight, loss_scale)
    near = pair_sum(mine, other)
    near, g4 = lax.optimization_barrier((near, g4))
    head_got = exchange(near.reshape(8, 4 * 32, scores // 4), near_groups())

    mine, other = back(sc, g4, saved, pre, conv_weight)
    near = pair_sum(mine, other)
    conv_got = exchange(near.reshape(8, LAYERS * TAPS * 4 * 32, width // 4), near_groups())

    far = head_far(head_got.reshape(8, 2, 2, 32, scores // 4))
    far = conv_far(conv_got.reshape(8, LAYERS * TAPS, 2, 2, 32, width // 4), far)
    return tuple(finish(exchange(far, far_groups()), scores))


def solution(mesh):
    return jax.shard_map(
        on_device,
        mesh=mesh,
        in_specs=(P("read", "tm", None), P("read", "tm", None), P("read"), P(), P(), P()),
        out_specs=(P(None, None, "read", "tm"), P("read", "tm")),
        check_vma=False,
    )
```

```python
import functools
import math

import jax
import jax.numpy as jnp
from jax import lax
from jax.experimental import pallas as pl
from jax.experimental.pallas import tpu as pltpu
from jax.sharding import PartitionSpec as P

LAYERS, TAPS = 4, 3
BASE_DILATION = 32
AXES = ("read", "tm")
READ, TM = 16, 8
CLASSES = BASE_DILATION // TM
PAD = CLASSES * 2 ** (LAYERS - 1)
BITS = [(a, b, c) for a in range(2) for b in range(2) for c in range(2)]
F32, BF16 = jnp.float32, jnp.bfloat16


def near_of(core, v):
    return (v // 2) ^ (v % 2) if core == 0 else v // 2


def far_of(core, v):
    return v // 2 if core == 0 else (v // 2) ^ (v % 2)


def high_low(core, near, far):
    return (far if core == 0 else near, near ^ far)


def device_index(x, y, z, core):
    return (((x % 2) * 4 + z) * 2 + core) * TM + y * 2 + x // 2


def groups_of(fixed, order):
    groups = {}
    for core in range(2):
        for x in range(4):
            for y in range(4):
                for z in range(4):
                    key = (core, fixed(core, x), fixed(core, y), fixed(core, z))
                    place = order(core, x) * 4 + order(core, y) * 2 + order(core, z)
                    groups.setdefault(key, [0] * 8)[place] = device_index(x, y, z, core)
    return list(groups.values())


def near_groups():
    def cube(core, v):
        return (v + core) % 4 // 2

    return groups_of(cube, near_of)


def far_groups():
    return groups_of(near_of, far_of)


def other_core():
    return [(d, d ^ TM) for d in range(READ * TM)]


def frame_groups():
    return [[r * TM + t for t in range(TM)] for r in range(READ)]


def exchange(x, groups):
    return lax.all_to_all(x, AXES, 0, 0, tiled=True, axis_index_groups=groups)


def encode(x):
    return (x * jnp.abs(x)).astype(BF16)


def decode(y):
    y = y.astype(F32)
    return y * lax.rsqrt(jnp.maximum(jnp.abs(y), 1e-37))


def low_lanes(shape):
    return lax.broadcasted_iota(jnp.int32, shape, len(shape) - 1) < 64


def dot(a, b):
    return jnp.dot(a, b, preferred_element_type=F32)


def dot_nt(a, b):
    return lax.dot_general(a, b, (((1,), (1,)), ((), ())), preferred_element_type=F32)


def params(*kinds):
    return pltpu.CompilerParams(dimension_semantics=kinds, vmem_limit_bytes=62 * 1024 * 1024)


def whole():
    return pl.BlockSpec(memory_space=pltpu.VMEM)


def frame_mask(sc_ref, frames):
    row = lax.broadcasted_iota(jnp.int32, (frames, 1), 0)
    position = row // CLASSES * BASE_DILATION + sc_ref[1] * CLASSES + row % CLASSES
    return (position < sc_ref[0]).astype(F32)


def regroup_kernel(x_ref, out_ref):
    frames = x_ref.shape[0]
    row = lax.broadcasted_iota(jnp.int32, (frames, frames), 0)
    col = lax.broadcasted_iota(jnp.int32, (frames, frames), 1)
    per = frames // TM
    source = (row % per) // CLASSES * BASE_DILATION + row // per * CLASSES + row % CLASSES
    select = jnp.where(col == source, 1.0, 0.0).astype(BF16)
    out_ref[...] = dot(select, x_ref[...]).astype(BF16)


def regroup(x):
    return pl.pallas_call(
        regroup_kernel,
        out_shape=jax.ShapeDtypeStruct(x.shape, BF16),
        in_specs=[whole()],
        out_specs=whole(),
        name="regroup",
    )(x)


def conv_kernel(sc_ref, x_ref, w_ref, saved_ref, pre_ref, last_ref, pad_s, tap_s):
    layer = pl.program_id(0)
    frames = x_ref.shape[0]

    @pl.when(layer == 0)
    def _():
        pad_s[...] = jnp.zeros_like(pad_s)
        pad_s[PAD : PAD + frames] = x_ref[...].astype(F32)

    for at in range(LAYERS):

        @pl.when(layer == at)
        def _():
            reach = CLASSES * 2**at
            tap_s[0] = pad_s[PAD - reach : PAD - reach + frames].astype(BF16)
            tap_s[1] = pad_s[PAD + reach : PAD + reach + frames].astype(BF16)

    hidden = pad_s[PAD : PAD + frames]
    middle = hidden.astype(BF16)
    saved_ref[0] = middle
    pre = dot(tap_s[0], w_ref[0, 0]) + dot(middle, w_ref[0, 1]) + dot(tap_s[1], w_ref[0, 2])
    pre_ref[0] = pre
    new = (frame_mask(sc_ref, frames) * (hidden + jax.nn.silu(pre))).astype(BF16)
    last_ref[...] = new
    pad_s[PAD : PAD + frames] = new.astype(F32)


def convolve(sc, x, weight):
    frames, width = x.shape
    one = pl.BlockSpec((1, frames, width), lambda i: (i, 0, 0))
    flat = pl.BlockSpec((frames, width), lambda i: (0, 0))
    return pl.pallas_call(
        conv_kernel,
        grid=(LAYERS,),
        in_specs=[
            pl.BlockSpec(memory_space=pltpu.SMEM),
            flat,
            pl.BlockSpec((1, TAPS, width, width), lambda i: (i, 0, 0, 0)),
        ],
        out_specs=[one, one, flat],
        out_shape=[
            jax.ShapeDtypeStruct((LAYERS, frames, width), BF16),
            jax.ShapeDtypeStruct((LAYERS, frames, width), F32),
            jax.ShapeDtypeStruct((frames, width), BF16),
        ],
        scratch_shapes=[
            pltpu.VMEM((frames + 2 * PAD, width), F32),
            pltpu.VMEM((2, frames, width), BF16),
        ],
        compiler_params=params("arbitrary"),
        cost_estimate=pl.CostEstimate(
            flops=2 * LAYERS * TAPS * frames * width * width,
            bytes_accessed=LAYERS * (TAPS * width * width * 2 + frames * width * 6),
            transcendentals=LAYERS * frames * width,
        ),
        name="convolve",
    )(sc, x, weight)


def head_kernel(scale, tiles, sc_ref, h_ref, t_ref, ws_ref, wt_ref, mine_ref, other_ref, g_ref,
                sq_s, es_s, et_s, sum_s, ht_s, gs_s, res_s):
    step = pl.program_id(0)
    frames, width = h_ref.shape
    tile = ws_ref.shape[1]
    sub = 256

    @pl.when(step == 0)
    def _():
        sum_s[...] = jnp.zeros_like(sum_s)

    @pl.when(step < tiles)
    def _():
        for c in range(tile // sub):
            cols = slice(c * sub, (c + 1) * sub)
            squash = jnp.tanh(dot(h_ref[...], ws_ref[:, cols]))
            exp_s = jnp.exp(5.0 * squash)
            sq_s[step, :, cols] = squash
            es_s[step, :, cols] = exp_s
            sum_s[0] += exp_s[:, :128] + exp_s[:, 128:]
            exp_t = jnp.exp(5.0 * jnp.tanh(dot(t_ref[...], wt_ref[:, cols])))
            et_s[step, :, cols] = exp_t
            sum_s[1] += exp_t[:, :128] + exp_t[:, 128:]

    @pl.when(step == tiles)
    def _():
        factor = scale * frame_mask(sc_ref, frames)
        for i in range(2):
            inverse = factor / jnp.sum(sum_s[i], axis=1, keepdims=True)
            sum_s[i] = jnp.broadcast_to(inverse, (frames, 128))
        ht_s[...] = h_ref[...].T
        g_ref[...] = jnp.zeros_like(g_ref)

    @pl.when(step >= tiles)
    def _():
        at = step - tiles
        for c in range(tile // 128):
            cols = slice(c * 128, (c + 1) * 128)
            squash = sq_s[at, :, cols]
            p = es_s[at, :, cols] * sum_s[0] - et_s[at, :, cols] * sum_s[1]
            gs_s[:, cols] = (p * (1.0 - squash * squash)).astype(BF16)
        res_s[...] = dot(ht_s[...], gs_s[...])
        g_ref[...] += dot_nt(gs_s[...], ws_ref[...])
        first = sc_ref[2] == 0
        half = tile // 2
        for nx, nz, fz in BITS:
            for fx in range(2):
                found = []
                for core in range(2):
                    xh, xl = high_low(core, nx, fx)
                    zh, zl = high_low(core, nz, fz)
                    r = ((xl * 4 + zh * 2 + zl) * 2 + core) * 32
                    found.append(res_s[r : r + 32, xh * half : (xh + 1) * half])
                to = slice(fx * half, (fx + 1) * half)
                mine_ref[nx, 0, nz, fz, 0, :, to] = jnp.where(first, found[0], found[1])
                other_ref[nx, 0, nz, fz, 0, :, to] = encode(jnp.where(first, found[1], found[0]))


def heads(sc, hidden, teacher_in, head_weight, teacher_head_weight, loss_scale):
    frames, width = hidden.shape
    wide = teacher_in.shape[1]
    scores = head_weight.shape[1]
    tiles = 4
    tile = scores // tiles

    def place(i, core):
        y = jnp.maximum(i - tiles, 0)
        high, low = y // 2, y % 2
        even = core == 0
        near = jnp.where(even, high ^ low, high)
        far = jnp.where(even, high, high ^ low)
        return (0, near, 0, 0, far, 0, 0)

    block = (2, 1, 2, 2, 1, 32, tile)
    shape = (2, 2, 2, 2, 2, 32, tile)
    kernel = functools.partial(head_kernel, 5.0 * loss_scale, tiles)
    big = pltpu.VMEM((tiles, frames, tile), F32)
    return pl.pallas_call(
        kernel,
        grid_spec=pltpu.PrefetchScalarGridSpec(
            num_scalar_prefetch=1,
            grid=(2 * tiles,),
            in_specs=[
                pl.BlockSpec((frames, width), lambda i, sc: (0, 0)),
                pl.BlockSpec((frames, wide), lambda i, sc: (0, 0)),
                pl.BlockSpec((width, tile), lambda i, sc: (0, i % tiles)),
                pl.BlockSpec((wide, tile), lambda i, sc: (0, jnp.minimum(i, tiles - 1))),
            ],
            out_specs=[
                pl.BlockSpec(block, lambda i, sc: place(i, sc[2])),
                pl.BlockSpec(block, lambda i, sc: place(i, 1 - sc[2])),
                pl.BlockSpec((frames, width), lambda i, sc: (0, 0)),
            ],
            scratch_shapes=[
                big,
                big,
                big,
                pltpu.VMEM((2, frames, 128), F32),
                pltpu.VMEM((width, frames), BF16),
                pltpu.VMEM((frames, tile), BF16),
                pltpu.VMEM((width, tile), F32),
            ],
        ),
        out_shape=[
            jax.ShapeDtypeStruct(shape, F32),
            jax.ShapeDtypeStruct(shape, BF16),
            jax.ShapeDtypeStruct((frames, width), F32),
        ],
        compiler_params=params("arbitrary"),
        cost_estimate=pl.CostEstimate(
            flops=2 * frames * scores * (3 * width + wide),
            bytes_accessed=scores * (6 * width + 2 * wide),
            transcendentals=4 * frames * scores,
        ),
        name="heads",
    )(sc, hidden, teacher_in, head_weight, teacher_head_weight)


def back_kernel(top, count, sc_ref, g4_ref, h_ref, pre_ref, w_ref, *refs):
    *out_g, mine_ref, other_ref, g_s, pad_s, tap_s, ht_s, res_s = refs
    step = pl.program_id(0)
    frames, width = g4_ref.shape

    @pl.when(step == 0)
    def _():
        g_s[...] = g4_ref[...]
        pad_s[...] = jnp.zeros_like(pad_s)

    g_act = frame_mask(sc_ref, frames) * g_s[...]
    pre = pre_ref[0]
    sigma = jax.nn.sigmoid(pre)
    g_pre = (g_act * sigma * (1.0 + pre * (1.0 - sigma))).astype(BF16)
    pad_s[PAD : PAD + frames] = g_pre.astype(F32)
    tap_s[1] = g_pre
    for at in range(top, top - count, -1):

        @pl.when(step == top - at)
        def _():
            reach = CLASSES * 2**at
            tap_s[0] = pad_s[PAD + reach : PAD + reach + frames].astype(BF16)
            tap_s[2] = pad_s[PAD - reach : PAD - reach + frames].astype(BF16)

    ht_s[...] = h_ref[0].T
    first = sc_ref[2] == 0
    low = low_lanes((32, 128))
    for tap in range(TAPS):
        res_s[...] = dot(ht_s[...], tap_s[tap])
        for nz, fz in ((0, 0), (0, 1), (1, 0), (1, 1)):
            for ny, fy in ((0, 0), (0, 1), (1, 0), (1, 1)):
                found = []
                for core in range(2):
                    zh, zl = high_low(core, nz, fz)
                    yh, yl = high_low(core, ny, fy)
                    cols = slice((yh * 2 + yl) * 128, (yh * 2 + yl + 1) * 128)
                    rows = [((xl * 4 + zh * 2 + zl) * 2 + core) * 32 for xl in range(2)]
                    a, b = (res_s[r : r + 32, cols] for r in rows)
                    if core == 1:
                        b = pltpu.roll(b, 64, 1)
                    found.append((jnp.where(low, a, b), jnp.where(low, b, a)))
                for nx in range(2):
                    mine = jnp.where(first, found[0][nx], found[1][nx])
                    other = jnp.where(first, found[1][nx], found[0][nx])
                    mine_ref[nx, ny, nz, tap, fz, fy] = mine
                    other_ref[nx, ny, nz, tap, fz, fy] = encode(other)

    def through():
        return (
            g_act
            + dot_nt(tap_s[0], w_ref[0, 0])
            + dot_nt(tap_s[1], w_ref[0, 1])
            + dot_nt(tap_s[2], w_ref[0, 2])
        )

    @pl.when(step < count - 1)
    def _():
        g_s[...] = through()

    if out_g:

        @pl.when(step == count - 1)
        def _():
            out_g[0][...] = through()


def back(sc, g, saved, pre, weight, top, count):
    frames, width = g.shape
    more = top - count + 1 > 0
    one = pl.BlockSpec((1, frames, width), lambda i: (top - i, 0, 0))
    flat = pl.BlockSpec((frames, width), lambda i: (0, 0))
    block = (2, 2, 2, TAPS, 2, 2, 32, width // 4)
    shape = (2, 2, 2, count * TAPS, 2, 2, 32, width // 4)
    out = pl.BlockSpec(block, lambda i: (0, 0, 0, count - 1 - i, 0, 0, 0, 0))
    dots = 2 * count - (not more)
    return pl.pallas_call(
        functools.partial(back_kernel, top, count),
        grid=(count,),
        in_specs=[
            pl.BlockSpec(memory_space=pltpu.SMEM),
            flat,
            one,
            one,
            pl.BlockSpec((1, TAPS, width, width), lambda i: (top - i, 0, 0, 0)),
        ],
        out_specs=[flat] * more + [out, out],
        out_shape=[jax.ShapeDtypeStruct((frames, width), F32)] * more
        + [jax.ShapeDtypeStruct(shape, F32), jax.ShapeDtypeStruct(shape, BF16)],
        scratch_shapes=[
            pltpu.VMEM((frames, width), F32),
            pltpu.VMEM((frames + 2 * PAD, width), F32),
            pltpu.VMEM((TAPS, frames, width), BF16),
            pltpu.VMEM((width, frames), BF16),
            pltpu.VMEM((width, width), F32),
        ],
        compiler_params=params("arbitrary"),
        cost_estimate=pl.CostEstimate(
            flops=2 * dots * TAPS * frames * width * width,
            bytes_accessed=count * (TAPS * width * width * 5 + frames * width * 6),
            transcendentals=count * frames * width,
        ),
        name="back",
    )(sc, g, saved, pre, weight)


def pair_kernel(*refs):
    *ins, out_ref = refs
    at = 0
    for mine, other in zip(ins[::2], ins[1::2]):
        rows = mine.shape[1]
        out_ref[0, at : at + rows] = encode(mine[0] + decode(other[0]))
        at += rows


def pair_sum(pieces):
    lanes = pieces[0][0].shape[2]
    rows = sum(mine.shape[1] for mine, _ in pieces)
    specs = [
        pl.BlockSpec((1, mine.shape[1], lanes), lambda i: (i, 0, 0))
        for mine, _ in pieces
        for _ in range(2)
    ]
    return pl.pallas_call(
        pair_kernel,
        grid=(8,),
        in_specs=specs,
        out_specs=pl.BlockSpec((1, rows, lanes), lambda i: (i, 0, 0)),
        out_shape=jax.ShapeDtypeStruct((8, rows, lanes), BF16),
        compiler_params=params("arbitrary"),
        cost_estimate=pl.CostEstimate(
            flops=64 * rows * lanes, bytes_accessed=64 * rows * lanes, transcendentals=8 * rows * lanes
        ),
        name="pair_sum",
    )(*[x for piece in pieces for x in piece])


def total_of(ref, *at):
    total = decode(ref[(0, *at)])
    for i in range(1, 8):
        total = total + decode(ref[(i, *at)])
    return total


def head_far_kernel(got_ref, out_ref):
    half = got_ref.shape[-1] // 2
    for fz, fy, fx in BITS:
        for c in range(half // 128):
            lanes = slice(fx * half + c * 128, fx * half + (c + 1) * 128)
            out_ref[fx * 4 + fy * 2 + fz, c] = encode(total_of(got_ref, fz, fy, slice(None), lanes))


def head_far(got):
    tile = got.shape[-1]
    return pl.pallas_call(
        head_far_kernel,
        out_shape=jax.ShapeDtypeStruct((8, tile // 256, 32, 128), BF16),
        in_specs=[whole()],
        out_specs=whole(),
        compiler_params=params(),
        cost_estimate=pl.CostEstimate(
            flops=8 * got.size, bytes_accessed=3 * got.size, transcendentals=got.size
        ),
        name="head_far",
    )(got)


def conv_far_kernel(a_ref, b_ref, head_ref, out_ref):
    step = pl.program_id(0)
    blocks, each = head_ref.shape[1], a_ref.shape[1]
    low = low_lanes((32, 128))

    @pl.when(step == 0)
    def _():
        out_ref[:, :blocks] = head_ref[...]

    for t in range(each):
        at = blocks + step * each + t
        for fz in range(2):
            for fy in range(2):
                a = total_of(a_ref, t, fz, fy)
                b = total_of(b_ref, t, fz, fy)
                out_ref[fy * 2 + fz, at] = encode(jnp.where(low, a, pltpu.roll(b, 64, 1)))
                out_ref[4 + fy * 2 + fz, at] = encode(jnp.where(low, pltpu.roll(a, 64, 1), b))


def conv_far(got, head):
    half = LAYERS * TAPS // 2
    steps = 3
    block = (8, half // steps, 2, 2, 32, 128)
    shape = (8, head.shape[1] + half, 32, 128)
    return pl.pallas_call(
        conv_far_kernel,
        grid=(steps,),
        out_shape=jax.ShapeDtypeStruct(shape, BF16),
        in_specs=[
            pl.BlockSpec(block, lambda i: (0, i, 0, 0, 0, 0)),
            pl.BlockSpec(block, lambda i: (0, i + steps, 0, 0, 0, 0)),
            pl.BlockSpec(head.shape, lambda i: (0, 0, 0, 0)),
        ],
        out_specs=pl.BlockSpec(shape, lambda i: (0, 0, 0, 0)),
        compiler_params=params("arbitrary"),
        cost_estimate=pl.CostEstimate(
            flops=8 * got.size, bytes_accessed=3 * got.size, transcendentals=got.size
        ),
        name="conv_far",
    )(got, got, head)


def finish_kernel(got_ref, conv_ref, head_ref):
    blocks = head_ref.shape[1] // 128
    for c in range(blocks):
        head_ref[:, c * 128 : (c + 1) * 128] = total_of(got_ref, c)
    half = LAYERS * TAPS // 2
    for t in range(half):
        total = total_of(got_ref, blocks + t)
        for tap, value in ((t, total), (t + half, pltpu.roll(total, 64, 1))):
            conv_ref[tap // TAPS, tap % TAPS] = value[:, :64]


def finish(got, scores):
    return pl.pallas_call(
        finish_kernel,
        out_shape=[
            jax.ShapeDtypeStruct((LAYERS, TAPS, 32, 64), F32),
            jax.ShapeDtypeStruct((32, scores // 8), F32),
        ],
        in_specs=[whole()],
        out_specs=[whole(), whole()],
        compiler_params=params(),
        name="finish",
    )(got)


def swap(x):
    return lax.ppermute(x, AXES, other_core())


def on_device(student_in, teacher_rows, valid, conv_weight, head_weight, teacher_head_weight):
    _, frames, width = student_in.shape
    scores = head_weight.shape[1]
    loss_scale = scores / (3.0 * math.sqrt(READ * TM * frames))
    sc = jnp.stack([valid[0], lax.axis_index("tm"), lax.axis_index("read") % 2])
    regrouped = regroup(student_in[0]).reshape(TM, frames // TM, width)
    student = exchange(regrouped, frame_groups()).reshape(frames, width)
    teacher = regroup(teacher_rows[0]).reshape(TM, frames // TM, -1)
    teacher = exchange(teacher, frame_groups()).reshape(frames, -1)

    saved, pre, hidden = convolve(sc, student, conv_weight)
    mine, other, g = heads(sc, hidden, teacher, head_weight, teacher_head_weight, loss_scale)
    other = swap(other)
    g, mine_hi, other_hi = back(sc, g, saved, pre, conv_weight, LAYERS - 1, 2)
    other_hi = swap(other_hi)
    mine, other, g = lax.optimization_barrier((mine, other, g))
    shape = (8, 4 * 32, scores // 4)
    near = pair_sum([(mine.reshape(shape), other.reshape(shape))])
    near, g = lax.optimization_barrier((near, g))
    head_got = exchange(near, near_groups())

    mine_lo, other_lo = back(sc, g, saved, pre, conv_weight, LAYERS - 3, 2)
    other_lo = swap(other_lo)
    other_lo, head_got = lax.optimization_barrier((other_lo, head_got))
    shape = (8, LAYERS * TAPS * 2 * 32, width // 4)
    low = (mine_lo.reshape(shape), other_lo.reshape(shape))
    high = (mine_hi.reshape(shape), other_hi.reshape(shape))
    conv_got = exchange(pair_sum([low, high]), near_groups())

    far = head_far(head_got.reshape(8, 2, 2, 32, scores // 4))
    far = conv_far(conv_got.reshape(8, LAYERS * TAPS, 2, 2, 32, width // 4), far)
    return tuple(finish(exchange(far, far_groups()), scores))


def solution(mesh):
    return jax.shard_map(
        on_device,
        mesh=mesh,
        in_specs=(P("read", "tm", None), P("read", "tm", None), P("read"), P(), P(), P()),
        out_specs=(P(None, None, "read", "tm"), P("read", "tm")),
        check_vma=False,
    )
```

```python
import functools
import math

import jax
import jax.numpy as jnp
from jax import lax
from jax.experimental import pallas as pl
from jax.experimental.pallas import tpu as pltpu
from jax.sharding import PartitionSpec as P

LAYERS, TAPS = 4, 3
BASE_DILATION = 32
AXES = ("read", "tm")
READ, TM = 16, 8
CLASSES = BASE_DILATION // TM
PAD = CLASSES * 2 ** (LAYERS - 1)
BITS = [(a, b, c) for a in range(2) for b in range(2) for c in range(2)]
F32, BF16 = jnp.float32, jnp.bfloat16


def near_of(core, v):
    return (v // 2) ^ (v % 2) if core == 0 else v // 2


def far_of(core, v):
    return v // 2 if core == 0 else (v // 2) ^ (v % 2)


def high_low(core, near, far):
    return (far if core == 0 else near, near ^ far)


def device_index(x, y, z, core):
    return (((x % 2) * 4 + z) * 2 + core) * TM + y * 2 + x // 2


def groups_of(fixed, order):
    groups = {}
    for core in range(2):
        for x in range(4):
            for y in range(4):
                for z in range(4):
                    key = (core, fixed(core, x), fixed(core, y), fixed(core, z))
                    place = order(core, x) * 4 + order(core, y) * 2 + order(core, z)
                    groups.setdefault(key, [0] * 8)[place] = device_index(x, y, z, core)
    return list(groups.values())


def near_groups():
    def cube(core, v):
        return (v + core) % 4 // 2

    return groups_of(cube, near_of)


def far_groups():
    return groups_of(near_of, far_of)


def other_core():
    return [(d, d ^ TM) for d in range(READ * TM)]


def frame_groups():
    return [[r * TM + t for t in range(TM)] for r in range(READ)]


def exchange(x, groups):
    return lax.all_to_all(x, AXES, 0, 0, tiled=True, axis_index_groups=groups)


def encode(x):
    return (x * jnp.abs(x)).astype(BF16)


def decode(y):
    y = y.astype(F32)
    return y * lax.rsqrt(jnp.maximum(jnp.abs(y), 1e-37))


def low_lanes(shape):
    return lax.broadcasted_iota(jnp.int32, shape, len(shape) - 1) < 64


def dot(a, b):
    return jnp.dot(a, b, preferred_element_type=F32)


def dot_nt(a, b):
    return lax.dot_general(a, b, (((1,), (1,)), ((), ())), preferred_element_type=F32)


def params(*kinds):
    return pltpu.CompilerParams(dimension_semantics=kinds, vmem_limit_bytes=62 * 1024 * 1024)


def whole():
    return pl.BlockSpec(memory_space=pltpu.VMEM)


def frame_mask(sc_ref, frames):
    row = lax.broadcasted_iota(jnp.int32, (frames, 1), 0)
    position = row // CLASSES * BASE_DILATION + sc_ref[1] * CLASSES + row % CLASSES
    return (position < sc_ref[0]).astype(F32)


def regroup_kernel(x_ref, out_ref):
    frames = x_ref.shape[0]
    row = lax.broadcasted_iota(jnp.int32, (frames, frames), 0)
    col = lax.broadcasted_iota(jnp.int32, (frames, frames), 1)
    per = frames // TM
    source = (row % per) // CLASSES * BASE_DILATION + row // per * CLASSES + row % CLASSES
    select = jnp.where(col == source, 1.0, 0.0).astype(BF16)
    out_ref[...] = dot(select, x_ref[...]).astype(BF16)


def regroup(x):
    return pl.pallas_call(
        regroup_kernel,
        out_shape=jax.ShapeDtypeStruct(x.shape, BF16),
        in_specs=[whole()],
        out_specs=whole(),
        name="regroup",
    )(x)


def conv_kernel(sc_ref, x_ref, w_ref, saved_ref, pre_ref, last_ref, pad_s, tap_s):
    layer = pl.program_id(0)
    frames = x_ref.shape[0]

    @pl.when(layer == 0)
    def _():
        pad_s[...] = jnp.zeros_like(pad_s)
        pad_s[PAD : PAD + frames] = x_ref[...].astype(F32)

    for at in range(LAYERS):

        @pl.when(layer == at)
        def _():
            reach = CLASSES * 2**at
            tap_s[0] = pad_s[PAD - reach : PAD - reach + frames].astype(BF16)
            tap_s[1] = pad_s[PAD + reach : PAD + reach + frames].astype(BF16)

    hidden = pad_s[PAD : PAD + frames]
    middle = hidden.astype(BF16)
    saved_ref[0] = middle
    pre = dot(tap_s[0], w_ref[0, 0]) + dot(middle, w_ref[0, 1]) + dot(tap_s[1], w_ref[0, 2])
    pre_ref[0] = pre
    new = (frame_mask(sc_ref, frames) * (hidden + jax.nn.silu(pre))).astype(BF16)
    last_ref[...] = new
    pad_s[PAD : PAD + frames] = new.astype(F32)


def convolve(sc, x, weight):
    frames, width = x.shape
    one = pl.BlockSpec((1, frames, width), lambda i: (i, 0, 0))
    flat = pl.BlockSpec((frames, width), lambda i: (0, 0))
    return pl.pallas_call(
        conv_kernel,
        grid=(LAYERS,),
        in_specs=[
            pl.BlockSpec(memory_space=pltpu.SMEM),
            flat,
            pl.BlockSpec((1, TAPS, width, width), lambda i: (i, 0, 0, 0)),
        ],
        out_specs=[one, one, flat],
        out_shape=[
            jax.ShapeDtypeStruct((LAYERS, frames, width), BF16),
            jax.ShapeDtypeStruct((LAYERS, frames, width), F32),
            jax.ShapeDtypeStruct((frames, width), BF16),
        ],
        scratch_shapes=[
            pltpu.VMEM((frames + 2 * PAD, width), F32),
            pltpu.VMEM((2, frames, width), BF16),
        ],
        compiler_params=params("arbitrary"),
        cost_estimate=pl.CostEstimate(
            flops=2 * LAYERS * TAPS * frames * width * width,
            bytes_accessed=LAYERS * (TAPS * width * width * 2 + frames * width * 6),
            transcendentals=LAYERS * frames * width,
        ),
        name="convolve",
    )(sc, x, weight)


def split_rows(core, ht_s, mine_ref, other_ref):
    for ref, owner in ((mine_ref, core), (other_ref, 1 - core)):
        for at, (nz, fz, xl) in enumerate(BITS):
            high = jnp.where(owner == 0, fz, nz)
            row = ((xl * 4 + high * 2 + (nz ^ fz)) * 2 + owner) * 32
            ref[at * 32 : (at + 1) * 32] = ht_s[pl.ds(pl.multiple_of(row, 32), 32)]


def head_kernel(scale, tiles, sc_ref, h_ref, t_ref, ws_ref, wt_ref, score_ref, g_ref, mine_ref, other_ref,
                sq_s, es_s, et_s, sum_s, ht_s):
    step = pl.program_id(0)
    frames, width = h_ref.shape
    tile = ws_ref.shape[1]
    sub = 256

    @pl.when(step == 0)
    def _():
        sum_s[...] = jnp.zeros_like(sum_s)

    @pl.when(step < tiles)
    def _():
        for c in range(tile // sub):
            cols = slice(c * sub, (c + 1) * sub)
            squash = jnp.tanh(dot(h_ref[...], ws_ref[:, cols]))
            exp_s = jnp.exp(5.0 * squash)
            sq_s[step, :, cols] = squash
            es_s[step, :, cols] = exp_s
            sum_s[0] += exp_s[:, :128] + exp_s[:, 128:]
            exp_t = jnp.exp(5.0 * jnp.tanh(dot(t_ref[...], wt_ref[:, cols])))
            et_s[step, :, cols] = exp_t
            sum_s[1] += exp_t[:, :128] + exp_t[:, 128:]

    @pl.when(step == tiles)
    def _():
        factor = scale * frame_mask(sc_ref, frames)
        for i in range(2):
            inverse = factor / jnp.sum(sum_s[i], axis=1, keepdims=True)
            sum_s[i] = jnp.broadcast_to(inverse, (frames, 128))
        ht_s[...] = h_ref[...].T
        split_rows(sc_ref[2], ht_s, mine_ref, other_ref)
        g_ref[...] = jnp.zeros_like(g_ref)

    @pl.when(step >= tiles)
    def _():
        at = step - tiles
        for c in range(tile // 128):
            cols = slice(c * 128, (c + 1) * 128)
            squash = sq_s[at, :, cols]
            p = es_s[at, :, cols] * sum_s[0] - et_s[at, :, cols] * sum_s[1]
            score_ref[:, cols] = (p * (1.0 - squash * squash)).astype(BF16)
        g_ref[...] += dot_nt(score_ref[...], ws_ref[...])


def heads(sc, hidden, teacher_in, head_weight, teacher_head_weight, loss_scale):
    frames, width = hidden.shape
    wide = teacher_in.shape[1]
    scores = head_weight.shape[1]
    tiles = 4
    tile = scores // tiles
    big = pltpu.VMEM((tiles, frames, tile), F32)
    rows = pl.BlockSpec((width // 2, frames), lambda i: (0, 0))
    return pl.pallas_call(
        functools.partial(head_kernel, 5.0 * loss_scale, tiles),
        grid=(2 * tiles,),
        in_specs=[
            pl.BlockSpec(memory_space=pltpu.SMEM),
            pl.BlockSpec((frames, width), lambda i: (0, 0)),
            pl.BlockSpec((frames, wide), lambda i: (0, 0)),
            pl.BlockSpec((width, tile), lambda i: (0, i % tiles)),
            pl.BlockSpec((wide, tile), lambda i: (0, jnp.minimum(i, tiles - 1))),
        ],
        out_specs=[
            pl.BlockSpec((frames, tile), lambda i: (0, jnp.maximum(i - tiles, 0))),
            pl.BlockSpec((frames, width), lambda i: (0, 0)),
            rows,
            rows,
        ],
        scratch_shapes=[
            big,
            big,
            big,
            pltpu.VMEM((2, frames, 128), F32),
            pltpu.VMEM((width, frames), BF16),
        ],
        out_shape=[
            jax.ShapeDtypeStruct((frames, scores), BF16),
            jax.ShapeDtypeStruct((frames, width), F32),
            jax.ShapeDtypeStruct((width // 2, frames), BF16),
            jax.ShapeDtypeStruct((width // 2, frames), BF16),
        ],
        compiler_params=params("arbitrary"),
        cost_estimate=pl.CostEstimate(
            flops=2 * frames * scores * (2 * width + wide),
            bytes_accessed=scores * (6 * width + 2 * wide),
            transcendentals=4 * frames * scores,
        ),
        name="heads",
    )(sc, hidden, teacher_in, head_weight, teacher_head_weight)


def head_grad_kernel(sc_ref, ha_ref, hb_ref, ga_ref, gb_ref, out_ref, res_s):
    half = res_s.shape[1] // 2
    res_s[...] = dot(ha_ref[...], ga_ref[...]) + dot(hb_ref[...], gb_ref[...])
    first = sc_ref[2] == 0
    for nx, nz, fz in BITS:
        for fx in range(2):
            row = ((nz * 2 + fz) * 2 + (nx ^ fx)) * 32
            rows = slice(row, row + 32)
            value = res_s[rows, fx * half : (fx + 1) * half]
            if nx != fx:
                value = jnp.where(first, value, res_s[rows, nx * half : (nx + 1) * half])
            out_ref[nx, 0, nz, fz, 0, :, fx * half : (fx + 1) * half] = encode(value)


def head_grad(sc, h_mine, h_other, score_mine, score_other):
    rows, frames = h_mine.shape
    scores = score_mine.shape[1]
    tile = scores // 4

    def place(i, sc):
        high, low = i // 2, i % 2
        even = sc[2] == 0
        return (0, jnp.where(even, high ^ low, high), 0, 0, jnp.where(even, high, high ^ low), 0, 0)

    hidden = pl.BlockSpec((rows, frames), lambda i, sc: (0, 0))
    score = pl.BlockSpec((frames, tile), lambda i, sc: (0, i))
    return pl.pallas_call(
        head_grad_kernel,
        grid_spec=pltpu.PrefetchScalarGridSpec(
            num_scalar_prefetch=1,
            grid=(4,),
            in_specs=[hidden, hidden, score, score],
            out_specs=pl.BlockSpec((2, 1, 2, 2, 1, 32, tile), place),
            scratch_shapes=[pltpu.VMEM((rows, tile), F32)],
        ),
        out_shape=jax.ShapeDtypeStruct((2, 2, 2, 2, 2, 32, tile), BF16),
        compiler_params=params("arbitrary"),
        cost_estimate=pl.CostEstimate(
            flops=4 * rows * frames * scores,
            bytes_accessed=4 * frames * scores + 2 * rows * scores,
            transcendentals=0,
        ),
        name="head_grad",
    )(sc, h_mine, h_other, score_mine, score_other)


def back_kernel(sc_ref, g4_ref, h_ref, pre_ref, w_ref, send_ref, mine_ref, g_s, pad_s, tap_s, ht_s):
    step = pl.program_id(0)
    frames, width = g4_ref.shape

    @pl.when(step == 0)
    def _():
        g_s[...] = g4_ref[...]
        pad_s[...] = jnp.zeros_like(pad_s)

    g_act = frame_mask(sc_ref, frames) * g_s[...]
    pre = pre_ref[0]
    sigma = jax.nn.sigmoid(pre)
    g_pre = (g_act * sigma * (1.0 + pre * (1.0 - sigma))).astype(BF16)
    send_ref[0, :2] = g_pre.reshape(2, frames // 2, width)
    ht_s[...] = h_ref[0].T
    split_rows(sc_ref[2], ht_s, mine_ref.at[0], send_ref.at[0, 2])

    @pl.when(step < LAYERS - 1)
    def _():
        pad_s[PAD : PAD + frames] = g_pre.astype(F32)
        for at in range(LAYERS - 1, 0, -1):

            @pl.when(step == LAYERS - 1 - at)
            def _():
                reach = CLASSES * 2**at
                tap_s[0] = pad_s[PAD + reach : PAD + reach + frames].astype(BF16)
                tap_s[1] = pad_s[PAD - reach : PAD - reach + frames].astype(BF16)

        g_s[...] = (
            g_act
            + dot_nt(tap_s[0], w_ref[0, 0])
            + dot_nt(g_pre, w_ref[0, 1])
            + dot_nt(tap_s[1], w_ref[0, 2])
        )


def back(sc, g, saved, pre, weight):
    frames, width = g.shape

    def at(*block):
        return pl.BlockSpec((1, *block), lambda i: (LAYERS - 1 - i, *(0 for _ in block)))

    return pl.pallas_call(
        back_kernel,
        grid=(LAYERS,),
        in_specs=[
            pl.BlockSpec(memory_space=pltpu.SMEM),
            pl.BlockSpec((frames, width), lambda i: (0, 0)),
            at(frames, width),
            at(frames, width),
            pl.BlockSpec(
                (1, TAPS, width, width), lambda i: (jnp.maximum(LAYERS - 1 - i, 1), 0, 0, 0)
            ),
        ],
        out_specs=[at(3, frames // 2, width), at(width // 2, frames)],
        out_shape=[
            jax.ShapeDtypeStruct((LAYERS, 3, frames // 2, width), BF16),
            jax.ShapeDtypeStruct((LAYERS, width // 2, frames), BF16),
        ],
        scratch_shapes=[
            pltpu.VMEM((frames, width), F32),
            pltpu.VMEM((frames + 2 * PAD, width), F32),
            pltpu.VMEM((2, frames, width), BF16),
            pltpu.VMEM((width, frames), BF16),
        ],
        compiler_params=params("arbitrary"),
        cost_estimate=pl.CostEstimate(
            flops=2 * (LAYERS - 1) * TAPS * frames * width * width,
            bytes_accessed=LAYERS * (TAPS * width * width * 2 + frames * width * 10),
            transcendentals=LAYERS * frames * width,
        ),
        name="back",
    )(sc, g, saved, pre, weight)


def conv_grad_kernel(sc_ref, mine_ref, send_ref, got_ref, out_ref, pad_s, tap_s, res_s):
    step = pl.program_id(0)
    rows, frames = mine_ref.shape[1:]
    width = send_ref.shape[3]

    @pl.when(step == 0)
    def _():
        pad_s[...] = jnp.zeros_like(pad_s)

    for side, ref in enumerate((send_ref, got_ref)):
        g_pre = ref[0, :2].reshape(frames, width)
        tap_s[1, side] = g_pre
        pad_s[side, PAD : PAD + frames] = g_pre.astype(F32)
    for at in range(LAYERS):

        @pl.when(step == at)
        def _():
            reach = CLASSES * 2**at
            for side in range(2):
                tap_s[0, side] = pad_s[side, PAD + reach : PAD + reach + frames].astype(BF16)
                tap_s[2, side] = pad_s[side, PAD - reach : PAD - reach + frames].astype(BF16)

    core = sc_ref[2]
    low = low_lanes((32, 128))
    for tap in range(TAPS):
        res_s[...] = dot(mine_ref[0], tap_s[tap, 0]) + dot(got_ref[0, 2], tap_s[tap, 1])
        for nz, fz, ny in BITS:
            for fy in range(2):
                high = jnp.where(core == 0, fy, ny)
                cols = pl.ds(pl.multiple_of((high * 2 + (ny ^ fy)) * 128, 128), 128)
                row = (nz * 2 + fz) * 64
                a = res_s[row : row + 32, cols]
                b = pltpu.roll(res_s[row + 32 : row + 64, cols], 64 * core, 1)
                out_ref[0, ny, nz, tap, fz, fy] = encode(jnp.where(low, a, b))
                out_ref[1, ny, nz, tap, fz, fy] = encode(jnp.where(low, b, a))


def conv_grad(sc, mine, send, got):
    _, rows, frames = mine.shape
    width = send.shape[3]

    def at(*block):
        return pl.BlockSpec((1, *block), lambda i: (i, *(0 for _ in block)))

    return pl.pallas_call(
        conv_grad_kernel,
        grid=(LAYERS,),
        in_specs=[
            pl.BlockSpec(memory_space=pltpu.SMEM),
            at(rows, frames),
            at(3, frames // 2, width),
            at(3, frames // 2, width),
        ],
        out_specs=pl.BlockSpec(
            (2, 2, 2, TAPS, 2, 2, 32, width // 4), lambda i: (0, 0, 0, i, 0, 0, 0, 0)
        ),
        out_shape=jax.ShapeDtypeStruct((2, 2, 2, LAYERS * TAPS, 2, 2, 32, width // 4), BF16),
        scratch_shapes=[
            pltpu.VMEM((2, frames + 2 * PAD, width), F32),
            pltpu.VMEM((TAPS, 2, frames, width), BF16),
            pltpu.VMEM((rows, width), F32),
        ],
        compiler_params=params("arbitrary"),
        cost_estimate=pl.CostEstimate(
            flops=4 * LAYERS * TAPS * rows * frames * width,
            bytes_accessed=LAYERS * (7 * rows * frames * 2 + TAPS * rows * width * 2),
            transcendentals=0,
        ),
        name="conv_grad",
    )(sc, mine, send, got)


def total_of(ref, *at):
    total = decode(ref[(0, *at)])
    for i in range(1, 8):
        total = total + decode(ref[(i, *at)])
    return total


def head_far_kernel(got_ref, out_ref):
    half = got_ref.shape[-1] // 2
    for fz, fy, fx in BITS:
        for c in range(half // 128):
            lanes = slice(fx * half + c * 128, fx * half + (c + 1) * 128)
            out_ref[fx * 4 + fy * 2 + fz, c] = encode(total_of(got_ref, fz, fy, slice(None), lanes))


def head_far(got):
    tile = got.shape[-1]
    return pl.pallas_call(
        head_far_kernel,
        out_shape=jax.ShapeDtypeStruct((8, tile // 256, 32, 128), BF16),
        in_specs=[whole()],
        out_specs=whole(),
        compiler_params=params(),
        cost_estimate=pl.CostEstimate(
            flops=8 * got.size, bytes_accessed=3 * got.size, transcendentals=got.size
        ),
        name="head_far",
    )(got)


def conv_far_kernel(a_ref, b_ref, head_ref, out_ref):
    step = pl.program_id(0)
    blocks, each = head_ref.shape[1], a_ref.shape[1]
    low = low_lanes((32, 128))

    @pl.when(step == 0)
    def _():
        out_ref[:, :blocks] = head_ref[...]

    for t in range(each):
        at = blocks + step * each + t
        for fz in range(2):
            for fy in range(2):
                a = total_of(a_ref, t, fz, fy)
                b = total_of(b_ref, t, fz, fy)
                out_ref[fy * 2 + fz, at] = encode(jnp.where(low, a, pltpu.roll(b, 64, 1)))
                out_ref[4 + fy * 2 + fz, at] = encode(jnp.where(low, pltpu.roll(a, 64, 1), b))


def conv_far(got, head):
    half = LAYERS * TAPS // 2
    steps = 3
    block = (8, half // steps, 2, 2, 32, 128)
    shape = (8, head.shape[1] + half, 32, 128)
    return pl.pallas_call(
        conv_far_kernel,
        grid=(steps,),
        out_shape=jax.ShapeDtypeStruct(shape, BF16),
        in_specs=[
            pl.BlockSpec(block, lambda i: (0, i, 0, 0, 0, 0)),
            pl.BlockSpec(block, lambda i: (0, i + steps, 0, 0, 0, 0)),
            pl.BlockSpec(head.shape, lambda i: (0, 0, 0, 0)),
        ],
        out_specs=pl.BlockSpec(shape, lambda i: (0, 0, 0, 0)),
        compiler_params=params("arbitrary"),
        cost_estimate=pl.CostEstimate(
            flops=8 * got.size, bytes_accessed=3 * got.size, transcendentals=got.size
        ),
        name="conv_far",
    )(got, got, head)


def finish_kernel(got_ref, conv_ref, head_ref):
    blocks = head_ref.shape[1] // 128
    for c in range(blocks):
        head_ref[:, c * 128 : (c + 1) * 128] = total_of(got_ref, c)
    half = LAYERS * TAPS // 2
    for t in range(half):
        total = total_of(got_ref, blocks + t)
        for tap, value in ((t, total), (t + half, pltpu.roll(total, 64, 1))):
            conv_ref[tap // TAPS, tap % TAPS] = value[:, :64]


def finish(got, scores):
    return pl.pallas_call(
        finish_kernel,
        out_shape=[
            jax.ShapeDtypeStruct((LAYERS, TAPS, 32, 64), F32),
            jax.ShapeDtypeStruct((32, scores // 8), F32),
        ],
        in_specs=[whole()],
        out_specs=[whole(), whole()],
        compiler_params=params(),
        name="finish",
    )(got)


def swap(x):
    return lax.ppermute(x, AXES, other_core())


def on_device(student_in, teacher_rows, valid, conv_weight, head_weight, teacher_head_weight):
    _, frames, width = student_in.shape
    scores = head_weight.shape[1]
    loss_scale = scores / (3.0 * math.sqrt(READ * TM * frames))
    sc = jnp.stack([valid[0], lax.axis_index("tm"), lax.axis_index("read") % 2])
    regrouped = regroup(student_in[0]).reshape(TM, frames // TM, width)
    student = exchange(regrouped, frame_groups()).reshape(frames, width)
    teacher = regroup(teacher_rows[0]).reshape(TM, frames // TM, -1)
    teacher = exchange(teacher, frame_groups()).reshape(frames, -1)

    saved, pre, hidden = convolve(sc, student, conv_weight)
    score, g, h_mine, h_other = heads(
        sc, hidden, teacher, head_weight, teacher_head_weight, loss_scale
    )
    score_got, h_got = swap(score), swap(h_other)
    send, mine = back(sc, g, saved, pre, conv_weight)
    got = swap(send)
    score_got, h_got, mine = lax.optimization_barrier((score_got, h_got, mine))
    near = head_grad(sc, h_mine, h_got, score, score_got)
    near, got = lax.optimization_barrier((near, got))
    head_got = exchange(near.reshape(8, 4 * 32, scores // 4), near_groups())
    near = conv_grad(sc, mine, send, got)
    near, head_got = lax.optimization_barrier((near, head_got))
    conv_got = exchange(near.reshape(8, LAYERS * TAPS * 4 * 32, width // 4), near_groups())

    far = head_far(head_got.reshape(8, 2, 2, 32, scores // 4))
    far = conv_far(conv_got.reshape(8, LAYERS * TAPS, 2, 2, 32, width // 4), far)
    return tuple(finish(exchange(far, far_groups()), scores))


def solution(mesh):
    return jax.shard_map(
        on_device,
        mesh=mesh,
        in_specs=(P("read", "tm", None), P("read", "tm", None), P("read"), P(), P(), P()),
        out_specs=(P(None, None, "read", "tm"), P("read", "tm")),
        check_vma=False,
    )
```

```python
import functools
import math

import jax
import jax.numpy as jnp
from jax import lax
from jax.experimental import pallas as pl
from jax.experimental.pallas import tpu as pltpu
from jax.sharding import PartitionSpec as P

LAYERS, TAPS = 4, 3
BASE_DILATION = 32
AXES = ("read", "tm")
READ, TM = 16, 8
CLASSES = BASE_DILATION // TM
PAD = CLASSES * 2 ** (LAYERS - 1)
BITS = [(a, b, c) for a in range(2) for b in range(2) for c in range(2)]
F32, BF16 = jnp.float32, jnp.bfloat16


def near_of(core, v):
    return (v // 2) ^ (v % 2) if core == 0 else v // 2


def far_of(core, v):
    return v // 2 if core == 0 else (v // 2) ^ (v % 2)


def high_low(core, near, far):
    return (far if core == 0 else near, near ^ far)


def device_index(x, y, z, core):
    return (((x % 2) * 4 + z) * 2 + core) * TM + y * 2 + x // 2


def groups_of(fixed, order):
    groups = {}
    for core in range(2):
        for x in range(4):
            for y in range(4):
                for z in range(4):
                    key = (core, fixed(core, x), fixed(core, y), fixed(core, z))
                    place = order(core, x) * 4 + order(core, y) * 2 + order(core, z)
                    groups.setdefault(key, [0] * 8)[place] = device_index(x, y, z, core)
    return list(groups.values())


def near_groups():
    def cube(core, v):
        return (v + core) % 4 // 2

    return groups_of(cube, near_of)


def far_groups():
    return groups_of(near_of, far_of)


def other_core():
    return [(d, d ^ TM) for d in range(READ * TM)]


def frame_groups():
    return [[r * TM + t for t in range(TM)] for r in range(READ)]


def exchange(x, groups):
    return lax.all_to_all(x, AXES, 0, 0, tiled=True, axis_index_groups=groups)


def encode(x):
    return (x * jnp.abs(x)).astype(BF16)


def decode(y):
    y = y.astype(F32)
    return y * lax.rsqrt(jnp.maximum(jnp.abs(y), 1e-37))


def low_lanes(shape):
    return lax.broadcasted_iota(jnp.int32, shape, len(shape) - 1) < 64


def dot(a, b):
    return jnp.dot(a, b, preferred_element_type=F32)


def dot_nt(a, b):
    return lax.dot_general(a, b, (((1,), (1,)), ((), ())), preferred_element_type=F32)


def params(*kinds):
    return pltpu.CompilerParams(dimension_semantics=kinds, vmem_limit_bytes=62 * 1024 * 1024)


def whole():
    return pl.BlockSpec(memory_space=pltpu.VMEM)


def frame_mask(sc_ref, frames):
    row = lax.broadcasted_iota(jnp.int32, (frames, 1), 0)
    position = row // CLASSES * BASE_DILATION + sc_ref[1] * CLASSES + row % CLASSES
    return (position < sc_ref[0]).astype(F32)


def regroup_kernel(x_ref, out_ref):
    frames = x_ref.shape[0]
    row = lax.broadcasted_iota(jnp.int32, (frames, frames), 0)
    col = lax.broadcasted_iota(jnp.int32, (frames, frames), 1)
    per = frames // TM
    source = (row % per) // CLASSES * BASE_DILATION + row // per * CLASSES + row % CLASSES
    select = jnp.where(col == source, 1.0, 0.0).astype(BF16)
    out_ref[...] = dot(select, x_ref[...]).astype(BF16)


def regroup(x):
    return pl.pallas_call(
        regroup_kernel,
        out_shape=jax.ShapeDtypeStruct(x.shape, BF16),
        in_specs=[whole()],
        out_specs=whole(),
        name="regroup",
    )(x)


def split_rows(core, ht_s, mine_ref, other_ref):
    for ref, owner in ((mine_ref, core), (other_ref, 1 - core)):
        for at, (nz, fz, xl) in enumerate(BITS):
            high = jnp.where(owner == 0, fz, nz)
            row = ((xl * 4 + high * 2 + (nz ^ fz)) * 2 + owner) * 32
            ref[at * 32 : (at + 1) * 32] = ht_s[pl.ds(pl.multiple_of(row, 32), 32)]


def conv_kernel(sc_ref, x_ref, w_ref, saved_ref, pre_ref, last_ref, mine_ref, other_ref, pad_s, tap_s, ht_s):
    layer = pl.program_id(0)
    frames = x_ref.shape[0]

    @pl.when(layer == 0)
    def _():
        pad_s[...] = jnp.zeros_like(pad_s)
        pad_s[PAD : PAD + frames] = x_ref[...].astype(F32)

    for at in range(LAYERS):

        @pl.when(layer == at)
        def _():
            reach = CLASSES * 2**at
            tap_s[0] = pad_s[PAD - reach : PAD - reach + frames].astype(BF16)
            tap_s[1] = pad_s[PAD + reach : PAD + reach + frames].astype(BF16)

    hidden = pad_s[PAD : PAD + frames]
    middle = hidden.astype(BF16)
    saved_ref[0] = middle
    pre = dot(tap_s[0], w_ref[0, 0]) + dot(middle, w_ref[0, 1]) + dot(tap_s[1], w_ref[0, 2])
    pre_ref[0] = pre
    new = (frame_mask(sc_ref, frames) * (hidden + jax.nn.silu(pre))).astype(BF16)
    pad_s[PAD : PAD + frames] = new.astype(F32)

    @pl.when(layer == LAYERS - 1)
    def _():
        last_ref[...] = new
        ht_s[...] = new.T
        split_rows(sc_ref[2], ht_s, mine_ref, other_ref)


def convolve(sc, x, weight):
    frames, width = x.shape
    one = pl.BlockSpec((1, frames, width), lambda i: (i, 0, 0))
    flat = pl.BlockSpec((frames, width), lambda i: (0, 0))
    rows = pl.BlockSpec((width // 2, frames), lambda i: (0, 0))
    return pl.pallas_call(
        conv_kernel,
        grid=(LAYERS,),
        in_specs=[
            pl.BlockSpec(memory_space=pltpu.SMEM),
            flat,
            pl.BlockSpec((1, TAPS, width, width), lambda i: (i, 0, 0, 0)),
        ],
        out_specs=[one, one, flat, rows, rows],
        out_shape=[
            jax.ShapeDtypeStruct((LAYERS, frames, width), BF16),
            jax.ShapeDtypeStruct((LAYERS, frames, width), F32),
            jax.ShapeDtypeStruct((frames, width), BF16),
            jax.ShapeDtypeStruct((width // 2, frames), BF16),
            jax.ShapeDtypeStruct((width // 2, frames), BF16),
        ],
        scratch_shapes=[
            pltpu.VMEM((frames + 2 * PAD, width), F32),
            pltpu.VMEM((2, frames, width), BF16),
            pltpu.VMEM((width, frames), BF16),
        ],
        compiler_params=params("arbitrary"),
        cost_estimate=pl.CostEstimate(
            flops=2 * LAYERS * TAPS * frames * width * width,
            bytes_accessed=LAYERS * (TAPS * width * width * 2 + frames * width * 6),
            transcendentals=LAYERS * frames * width,
        ),
        name="convolve",
    )(sc, x, weight)


def head_kernel(scale, tiles, sc_ref, h_ref, t_ref, ws_ref, wt_ref, score_ref, g_ref,
                sq_s, es_s, et_s, sum_s):
    step = pl.program_id(0)
    frames, width = h_ref.shape
    tile = ws_ref.shape[1]
    sub = 256

    @pl.when(step == 0)
    def _():
        sum_s[...] = jnp.zeros_like(sum_s)

    @pl.when(step < tiles)
    def _():
        for c in range(tile // sub):
            cols = slice(c * sub, (c + 1) * sub)
            squash = jnp.tanh(dot(h_ref[...], ws_ref[:, cols]))
            exp_s = jnp.exp(5.0 * squash)
            sq_s[step, :, cols] = squash
            es_s[step, :, cols] = exp_s
            sum_s[0] += exp_s[:, :128] + exp_s[:, 128:]
            exp_t = jnp.exp(5.0 * jnp.tanh(dot(t_ref[...], wt_ref[:, cols])))
            et_s[step, :, cols] = exp_t
            sum_s[1] += exp_t[:, :128] + exp_t[:, 128:]

    @pl.when(step == tiles)
    def _():
        factor = scale * frame_mask(sc_ref, frames)
        for i in range(2):
            inverse = factor / jnp.sum(sum_s[i], axis=1, keepdims=True)
            sum_s[i] = jnp.broadcast_to(inverse, (frames, 128))
        g_ref[...] = jnp.zeros_like(g_ref)

    @pl.when(step >= tiles)
    def _():
        at = step - tiles
        for c in range(tile // 128):
            cols = slice(c * 128, (c + 1) * 128)
            squash = sq_s[at, :, cols]
            p = es_s[at, :, cols] * sum_s[0] - et_s[at, :, cols] * sum_s[1]
            score_ref[:, cols] = (p * (1.0 - squash * squash)).astype(BF16)
        g_ref[...] += dot_nt(score_ref[...], ws_ref[...])


def heads(sc, hidden, teacher_in, head_weight, teacher_head_weight, loss_scale):
    frames, width = hidden.shape
    wide = teacher_in.shape[1]
    scores = head_weight.shape[1]
    tiles = 4
    tile = scores // tiles
    big = pltpu.VMEM((tiles, frames, tile), F32)
    return pl.pallas_call(
        functools.partial(head_kernel, 5.0 * loss_scale, tiles),
        grid=(2 * tiles,),
        in_specs=[
            pl.BlockSpec(memory_space=pltpu.SMEM),
            pl.BlockSpec((frames, width), lambda i: (0, 0)),
            pl.BlockSpec((frames, wide), lambda i: (0, 0)),
            pl.BlockSpec((width, tile), lambda i: (0, i % tiles)),
            pl.BlockSpec((wide, tile), lambda i: (0, jnp.minimum(i, tiles - 1))),
        ],
        out_specs=[
            pl.BlockSpec((frames, tile), lambda i: (0, jnp.maximum(i - tiles, 0))),
            pl.BlockSpec((frames, width), lambda i: (0, 0)),
        ],
        scratch_shapes=[
            big,
            big,
            big,
            pltpu.VMEM((2, frames, 128), F32),
        ],
        out_shape=[
            jax.ShapeDtypeStruct((frames, scores), BF16),
            jax.ShapeDtypeStruct((frames, width), F32),
        ],
        compiler_params=params("arbitrary"),
        cost_estimate=pl.CostEstimate(
            flops=2 * frames * scores * (2 * width + wide),
            bytes_accessed=scores * (6 * width + 2 * wide),
            transcendentals=4 * frames * scores,
        ),
        name="heads",
    )(sc, hidden, teacher_in, head_weight, teacher_head_weight)


def head_grad_kernel(sc_ref, ha_ref, hb_ref, ga_ref, gb_ref, out_ref, res_s):
    half = ga_ref.shape[1] // 2
    first = sc_ref[2] == 0
    for c in range(half // 128):
        cols = [slice(x * half + c * 128, x * half + (c + 1) * 128) for x in range(2)]
        ga, gb = (jnp.concatenate([ref[:, at] for at in cols], axis=1) for ref in (ga_ref, gb_ref))
        res_s[c] = dot(ha_ref[...], ga) + dot(hb_ref[...], gb)
        for nx, nz, fz in BITS:
            for fx in range(2):
                row = ((nz * 2 + fz) * 2 + (nx ^ fx)) * 32
                rows = slice(row, row + 32)
                value = res_s[c, rows, fx * 128 : (fx + 1) * 128]
                if nx != fx:
                    value = jnp.where(first, value, res_s[c, rows, nx * 128 : (nx + 1) * 128])
                out_ref[nx, 0, nz, fz, 0, :, cols[fx]] = encode(value)


def head_grad(sc, h_mine, h_other, score_mine, score_other):
    rows, frames = h_mine.shape
    scores = score_mine.shape[1]
    tile = scores // 4

    def place(i, sc):
        high, low = i // 2, i % 2
        even = sc[2] == 0
        return (0, jnp.where(even, high ^ low, high), 0, 0, jnp.where(even, high, high ^ low), 0, 0)

    hidden = pl.BlockSpec((rows, frames), lambda i, sc: (0, 0))
    score = pl.BlockSpec((frames, tile), lambda i, sc: (0, i))
    return pl.pallas_call(
        head_grad_kernel,
        grid_spec=pltpu.PrefetchScalarGridSpec(
            num_scalar_prefetch=1,
            grid=(4,),
            in_specs=[hidden, hidden, score, score],
            out_specs=pl.BlockSpec((2, 1, 2, 2, 1, 32, tile), place),
            scratch_shapes=[pltpu.VMEM((tile // 256, rows, 256), F32)],
        ),
        out_shape=jax.ShapeDtypeStruct((2, 2, 2, 2, 2, 32, tile), BF16),
        compiler_params=params("arbitrary"),
        cost_estimate=pl.CostEstimate(
            flops=4 * rows * frames * scores,
            bytes_accessed=4 * frames * scores + 2 * rows * scores,
            transcendentals=0,
        ),
        name="head_grad",
    )(sc, h_mine, h_other, score_mine, score_other)


def back_kernel(sc_ref, g4_ref, h_ref, pre_ref, w_ref, send_ref, mine_ref, g_s, pad_s, tap_s, ht_s):
    step = pl.program_id(0)
    frames, width = g4_ref.shape

    @pl.when(step == 0)
    def _():
        g_s[...] = g4_ref[...]
        pad_s[...] = jnp.zeros_like(pad_s)

    g_act = frame_mask(sc_ref, frames) * g_s[...]
    pre = pre_ref[0]
    sigma = jax.nn.sigmoid(pre)
    g_pre = (g_act * sigma * (1.0 + pre * (1.0 - sigma))).astype(BF16)
    send_ref[0, :2] = g_pre.reshape(2, frames // 2, width)
    ht_s[...] = h_ref[0].T
    split_rows(sc_ref[2], ht_s, mine_ref.at[0], send_ref.at[0, 2])

    @pl.when(step < LAYERS - 1)
    def _():
        pad_s[PAD : PAD + frames] = g_pre.astype(F32)
        for at in range(LAYERS - 1, 0, -1):

            @pl.when(step == LAYERS - 1 - at)
            def _():
                reach = CLASSES * 2**at
                tap_s[0] = pad_s[PAD + reach : PAD + reach + frames].astype(BF16)
                tap_s[1] = pad_s[PAD - reach : PAD - reach + frames].astype(BF16)

        g_s[...] = (
            g_act
            + dot_nt(tap_s[0], w_ref[0, 0])
            + dot_nt(g_pre, w_ref[0, 1])
            + dot_nt(tap_s[1], w_ref[0, 2])
        )


def back(sc, g, saved, pre, weight):
    frames, width = g.shape

    def at(*block):
        return pl.BlockSpec((1, *block), lambda i: (LAYERS - 1 - i, *(0 for _ in block)))

    return pl.pallas_call(
        back_kernel,
        grid=(LAYERS,),
        in_specs=[
            pl.BlockSpec(memory_space=pltpu.SMEM),
            pl.BlockSpec((frames, width), lambda i: (0, 0)),
            at(frames, width),
            at(frames, width),
            pl.BlockSpec(
                (1, TAPS, width, width), lambda i: (jnp.maximum(LAYERS - 1 - i, 1), 0, 0, 0)
            ),
        ],
        out_specs=[at(3, frames // 2, width), at(width // 2, frames)],
        out_shape=[
            jax.ShapeDtypeStruct((LAYERS, 3, frames // 2, width), BF16),
            jax.ShapeDtypeStruct((LAYERS, width // 2, frames), BF16),
        ],
        scratch_shapes=[
            pltpu.VMEM((frames, width), F32),
            pltpu.VMEM((frames + 2 * PAD, width), F32),
            pltpu.VMEM((2, frames, width), BF16),
            pltpu.VMEM((width, frames), BF16),
        ],
        compiler_params=params("arbitrary"),
        cost_estimate=pl.CostEstimate(
            flops=2 * (LAYERS - 1) * TAPS * frames * width * width,
            bytes_accessed=LAYERS * (TAPS * width * width * 2 + frames * width * 10),
            transcendentals=LAYERS * frames * width,
        ),
        name="back",
    )(sc, g, saved, pre, weight)


def conv_grad_kernel(sc_ref, mine_ref, send_ref, got_ref, out_ref, pad_s, tap_s, res_s):
    step = pl.program_id(0)
    rows, frames = mine_ref.shape[1:]
    width = send_ref.shape[3]

    @pl.when(step == 0)
    def _():
        pad_s[...] = jnp.zeros_like(pad_s)

    for side, ref in enumerate((send_ref, got_ref)):
        g_pre = ref[0, :2].reshape(frames, width)
        tap_s[1, side] = g_pre
        pad_s[side, PAD : PAD + frames] = g_pre.astype(F32)
    for at in range(LAYERS):

        @pl.when(step == at)
        def _():
            reach = CLASSES * 2**at
            for side in range(2):
                tap_s[0, side] = pad_s[side, PAD + reach : PAD + reach + frames].astype(BF16)
                tap_s[2, side] = pad_s[side, PAD - reach : PAD - reach + frames].astype(BF16)

    core = sc_ref[2]
    low = low_lanes((32, 128))
    for tap in range(TAPS):
        res_s[tap] = dot(mine_ref[0], tap_s[tap, 0]) + dot(got_ref[0, 2], tap_s[tap, 1])
        for nz, fz, ny in BITS:
            for fy in range(2):
                high = jnp.where(core == 0, fy, ny)
                cols = pl.ds(pl.multiple_of((high * 2 + (ny ^ fy)) * 128, 128), 128)
                row = (nz * 2 + fz) * 64
                a = res_s[tap, row : row + 32, cols]
                b = pltpu.roll(res_s[tap, row + 32 : row + 64, cols], 64 * core, 1)
                out_ref[0, ny, nz, tap, fz, fy] = encode(jnp.where(low, a, b))
                out_ref[1, ny, nz, tap, fz, fy] = encode(jnp.where(low, b, a))


def conv_grad(sc, mine, send, got):
    _, rows, frames = mine.shape
    width = send.shape[3]

    def at(*block):
        return pl.BlockSpec((1, *block), lambda i: (i, *(0 for _ in block)))

    return pl.pallas_call(
        conv_grad_kernel,
        grid=(LAYERS,),
        in_specs=[
            pl.BlockSpec(memory_space=pltpu.SMEM),
            at(rows, frames),
            at(3, frames // 2, width),
            at(3, frames // 2, width),
        ],
        out_specs=pl.BlockSpec(
            (2, 2, 2, TAPS, 2, 2, 32, width // 4), lambda i: (0, 0, 0, i, 0, 0, 0, 0)
        ),
        out_shape=jax.ShapeDtypeStruct((2, 2, 2, LAYERS * TAPS, 2, 2, 32, width // 4), BF16),
        scratch_shapes=[
            pltpu.VMEM((2, frames + 2 * PAD, width), F32),
            pltpu.VMEM((TAPS, 2, frames, width), BF16),
            pltpu.VMEM((TAPS, rows, width), F32),
        ],
        compiler_params=params("arbitrary"),
        cost_estimate=pl.CostEstimate(
            flops=4 * LAYERS * TAPS * rows * frames * width,
            bytes_accessed=LAYERS * (7 * rows * frames * 2 + TAPS * rows * width * 2),
            transcendentals=0,
        ),
        name="conv_grad",
    )(sc, mine, send, got)


def total_of(ref, *at):
    total = decode(ref[(0, *at)])
    for i in range(1, 8):
        total = total + decode(ref[(i, *at)])
    return total


def head_far_kernel(got_ref, out_ref):
    half = got_ref.shape[-1] // 2
    for fz, fy, fx in BITS:
        for c in range(half // 128):
            lanes = slice(fx * half + c * 128, fx * half + (c + 1) * 128)
            out_ref[fx * 4 + fy * 2 + fz, c] = encode(total_of(got_ref, fz, fy, slice(None), lanes))


def head_far(got):
    tile = got.shape[-1]
    return pl.pallas_call(
        head_far_kernel,
        out_shape=jax.ShapeDtypeStruct((8, tile // 256, 32, 128), BF16),
        in_specs=[whole()],
        out_specs=whole(),
        compiler_params=params(),
        cost_estimate=pl.CostEstimate(
            flops=8 * got.size, bytes_accessed=3 * got.size, transcendentals=got.size
        ),
        name="head_far",
    )(got)


def conv_far_kernel(a_ref, b_ref, head_ref, out_ref):
    step = pl.program_id(0)
    blocks, each = head_ref.shape[1], a_ref.shape[1]
    low = low_lanes((32, 128))

    @pl.when(step == 0)
    def _():
        out_ref[:, :blocks] = head_ref[...]

    for t in range(each):
        at = blocks + step * each + t
        for fz in range(2):
            for fy in range(2):
                a = total_of(a_ref, t, fz, fy)
                b = total_of(b_ref, t, fz, fy)
                out_ref[fy * 2 + fz, at] = encode(jnp.where(low, a, pltpu.roll(b, 64, 1)))
                out_ref[4 + fy * 2 + fz, at] = encode(jnp.where(low, pltpu.roll(a, 64, 1), b))


def conv_far(got, head):
    half = LAYERS * TAPS // 2
    steps = 3
    block = (8, half // steps, 2, 2, 32, 128)
    shape = (8, head.shape[1] + half, 32, 128)
    return pl.pallas_call(
        conv_far_kernel,
        grid=(steps,),
        out_shape=jax.ShapeDtypeStruct(shape, BF16),
        in_specs=[
            pl.BlockSpec(block, lambda i: (0, i, 0, 0, 0, 0)),
            pl.BlockSpec(block, lambda i: (0, i + steps, 0, 0, 0, 0)),
            pl.BlockSpec(head.shape, lambda i: (0, 0, 0, 0)),
        ],
        out_specs=pl.BlockSpec(shape, lambda i: (0, 0, 0, 0)),
        compiler_params=params("arbitrary"),
        cost_estimate=pl.CostEstimate(
            flops=8 * got.size, bytes_accessed=3 * got.size, transcendentals=got.size
        ),
        name="conv_far",
    )(got, got, head)


def finish_kernel(got_ref, conv_ref, head_ref):
    blocks = head_ref.shape[1] // 128
    for c in range(blocks):
        head_ref[:, c * 128 : (c + 1) * 128] = total_of(got_ref, c)
    half = LAYERS * TAPS // 2
    for t in range(half):
        total = total_of(got_ref, blocks + t)
        for tap, value in ((t, total), (t + half, pltpu.roll(total, 64, 1))):
            conv_ref[tap // TAPS, tap % TAPS] = value[:, :64]


def finish(got, scores):
    return pl.pallas_call(
        finish_kernel,
        out_shape=[
            jax.ShapeDtypeStruct((LAYERS, TAPS, 32, 64), F32),
            jax.ShapeDtypeStruct((32, scores // 8), F32),
        ],
        in_specs=[whole()],
        out_specs=[whole(), whole()],
        compiler_params=params(),
        name="finish",
    )(got)


def swap(x):
    return lax.ppermute(x, AXES, other_core())


def on_device(student_in, teacher_rows, valid, conv_weight, head_weight, teacher_head_weight):
    _, frames, width = student_in.shape
    scores = head_weight.shape[1]
    loss_scale = scores / (3.0 * math.sqrt(READ * TM * frames))
    sc = jnp.stack([valid[0], lax.axis_index("tm"), lax.axis_index("read") % 2])
    regrouped = regroup(student_in[0]).reshape(TM, frames // TM, width)
    student = exchange(regrouped, frame_groups()).reshape(frames, width)
    teacher = regroup(teacher_rows[0]).reshape(TM, frames // TM, -1)
    teacher = exchange(teacher, frame_groups()).reshape(frames, -1)

    saved, pre, hidden, h_mine, h_other = convolve(sc, student, conv_weight)
    h_got, hidden = lax.optimization_barrier((swap(h_other), hidden))
    score, g = heads(sc, hidden, teacher, head_weight, teacher_head_weight, loss_scale)
    score_got = swap(score)
    send, mine = back(sc, g, saved, pre, conv_weight)
    got = swap(send)
    score_got, mine = lax.optimization_barrier((score_got, mine))
    near = head_grad(sc, h_mine, h_got, score, score_got)
    near, got = lax.optimization_barrier((near, got))
    head_got = exchange(near.reshape(8, 4 * 32, scores // 4), near_groups())
    near = conv_grad(sc, mine, send, got)
    near, head_got = lax.optimization_barrier((near, head_got))
    conv_got = exchange(near.reshape(8, LAYERS * TAPS * 4 * 32, width // 4), near_groups())

    far = head_far(head_got.reshape(8, 2, 2, 32, scores // 4))
    far = conv_far(conv_got.reshape(8, LAYERS * TAPS, 2, 2, 32, width // 4), far)
    return tuple(finish(exchange(far, far_groups()), scores))


def solution(mesh):
    return jax.shard_map(
        on_device,
        mesh=mesh,
        in_specs=(P("read", "tm", None), P("read", "tm", None), P("read"), P(), P(), P()),
        out_specs=(P(None, None, "read", "tm"), P("read", "tm")),
        check_vma=False,
    )
```

```python
import functools
import math

import jax
import jax.numpy as jnp
from jax import lax
from jax.experimental import pallas as pl
from jax.experimental.pallas import tpu as pltpu
from jax.sharding import PartitionSpec as P

LAYERS, TAPS = 4, 3
BASE_DILATION = 32
AXES = ("read", "tm")
READ, TM = 16, 8
CLASSES = BASE_DILATION // TM
PAD = CLASSES * 2 ** (LAYERS - 1)
BITS = [(a, b, c) for a in range(2) for b in range(2) for c in range(2)]
F32, BF16 = jnp.float32, jnp.bfloat16


def near_of(core, v):
    return (v // 2) ^ (v % 2) if core == 0 else v // 2


def far_of(core, v):
    return v // 2 if core == 0 else (v // 2) ^ (v % 2)


def high_low(core, near, far):
    return (far if core == 0 else near, near ^ far)


def device_index(x, y, z, core):
    return (((x % 2) * 4 + z) * 2 + core) * TM + y * 2 + x // 2


def groups_of(fixed, order):
    groups = {}
    for core in range(2):
        for x in range(4):
            for y in range(4):
                for z in range(4):
                    key = (core, fixed(core, x), fixed(core, y), fixed(core, z))
                    place = order(core, x) * 4 + order(core, y) * 2 + order(core, z)
                    groups.setdefault(key, [0] * 8)[place] = device_index(x, y, z, core)
    return list(groups.values())


def near_groups():
    def cube(core, v):
        return (v + core) % 4 // 2

    return groups_of(cube, near_of)


def far_groups():
    return groups_of(near_of, far_of)


def other_core():
    return [(d, d ^ TM) for d in range(READ * TM)]


def frame_groups():
    return [[r * TM + t for t in range(TM)] for r in range(READ)]


def exchange(x, groups):
    return lax.all_to_all(x, AXES, 0, 0, tiled=True, axis_index_groups=groups)


def encode(x):
    return (x * jnp.abs(x)).astype(BF16)


def decode(y):
    y = y.astype(F32)
    return y * lax.rsqrt(jnp.maximum(jnp.abs(y), 1e-37))


def low_lanes(shape):
    return lax.broadcasted_iota(jnp.int32, shape, len(shape) - 1) < 64


def dot(a, b):
    return jnp.dot(a, b, preferred_element_type=F32)


def dot_nt(a, b):
    return lax.dot_general(a, b, (((1,), (1,)), ((), ())), preferred_element_type=F32)


def params(mib, *kinds):
    return pltpu.CompilerParams(dimension_semantics=kinds, vmem_limit_bytes=mib * 1024 * 1024)


def whole():
    return pl.BlockSpec(memory_space=pltpu.VMEM)


def frame_mask(sc_ref, frames):
    row = lax.broadcasted_iota(jnp.int32, (frames, 1), 0)
    position = row // CLASSES * BASE_DILATION + sc_ref[1] * CLASSES + row % CLASSES
    return (position < sc_ref[0]).astype(F32)


def regroup_kernel(x_ref, out_ref):
    frames = x_ref.shape[0]
    row = lax.broadcasted_iota(jnp.int32, (frames, frames), 0)
    col = lax.broadcasted_iota(jnp.int32, (frames, frames), 1)
    per = frames // TM
    source = (row % per) // CLASSES * BASE_DILATION + row // per * CLASSES + row % CLASSES
    select = jnp.where(col == source, 1.0, 0.0).astype(BF16)
    out_ref[...] = dot(select, x_ref[...]).astype(BF16)


def regroup(x):
    return pl.pallas_call(
        regroup_kernel,
        out_shape=jax.ShapeDtypeStruct(x.shape, BF16),
        in_specs=[whole()],
        out_specs=whole(),
        compiler_params=params(5),
        name="regroup",
    )(x)


def split_rows(core, ht_s, mine_ref, other_ref):
    for ref, owner in ((mine_ref, core), (other_ref, 1 - core)):
        for at, (nz, fz, xl) in enumerate(BITS):
            high = jnp.where(owner == 0, fz, nz)
            row = ((xl * 4 + high * 2 + (nz ^ fz)) * 2 + owner) * 32
            ref[at * 32 : (at + 1) * 32] = ht_s[pl.ds(pl.multiple_of(row, 32), 32)]


def conv_kernel(sc_ref, x_ref, w_ref, saved_ref, pre_ref, last_ref, mine_ref, other_ref, pad_s, tap_s, ht_s):
    layer = pl.program_id(0)
    frames = x_ref.shape[0]

    @pl.when(layer == 0)
    def _():
        pad_s[...] = jnp.zeros_like(pad_s)
        pad_s[PAD : PAD + frames] = x_ref[...].astype(F32)

    for at in range(LAYERS):

        @pl.when(layer == at)
        def _():
            reach = CLASSES * 2**at
            tap_s[0] = pad_s[PAD - reach : PAD - reach + frames].astype(BF16)
            tap_s[1] = pad_s[PAD + reach : PAD + reach + frames].astype(BF16)

    hidden = pad_s[PAD : PAD + frames]
    middle = hidden.astype(BF16)
    saved_ref[0] = middle
    pre = dot(tap_s[0], w_ref[0, 0]) + dot(middle, w_ref[0, 1]) + dot(tap_s[1], w_ref[0, 2])
    pre_ref[0] = pre
    new = (frame_mask(sc_ref, frames) * (hidden + jax.nn.silu(pre))).astype(BF16)
    pad_s[PAD : PAD + frames] = new.astype(F32)

    @pl.when(layer == LAYERS - 1)
    def _():
        last_ref[...] = new
        ht_s[...] = new.T
        split_rows(sc_ref[2], ht_s, mine_ref, other_ref)


def convolve(sc, x, weight):
    frames, width = x.shape
    one = pl.BlockSpec((1, frames, width), lambda i: (i, 0, 0))
    flat = pl.BlockSpec((frames, width), lambda i: (0, 0))
    rows = pl.BlockSpec((width // 2, frames), lambda i: (0, 0))
    return pl.pallas_call(
        conv_kernel,
        grid=(LAYERS,),
        in_specs=[
            pl.BlockSpec(memory_space=pltpu.SMEM),
            flat,
            pl.BlockSpec((1, TAPS, width, width), lambda i: (i, 0, 0, 0)),
        ],
        out_specs=[one, one, flat, rows, rows],
        out_shape=[
            jax.ShapeDtypeStruct((LAYERS, frames, width), BF16),
            jax.ShapeDtypeStruct((LAYERS, frames, width), F32),
            jax.ShapeDtypeStruct((frames, width), BF16),
            jax.ShapeDtypeStruct((width // 2, frames), BF16),
            jax.ShapeDtypeStruct((width // 2, frames), BF16),
        ],
        scratch_shapes=[
            pltpu.VMEM((frames + 2 * PAD, width), F32),
            pltpu.VMEM((2, frames, width), BF16),
            pltpu.VMEM((width, frames), BF16),
        ],
        compiler_params=params(14, "arbitrary"),
        cost_estimate=pl.CostEstimate(
            flops=2 * LAYERS * TAPS * frames * width * width,
            bytes_accessed=LAYERS * (TAPS * width * width * 2 + frames * width * 6),
            transcendentals=LAYERS * frames * width,
        ),
        name="convolve",
    )(sc, x, weight)


def head_kernel(scale, tiles, sc_ref, h_ref, t_ref, ws_ref, wt_ref, score_ref, g_ref,
                sq_s, es_s, et_s, sum_s):
    step = pl.program_id(0)
    frames, width = h_ref.shape
    tile = ws_ref.shape[1]
    sub = 256

    @pl.when(step == 0)
    def _():
        sum_s[...] = jnp.zeros_like(sum_s)

    @pl.when(step < tiles)
    def _():
        for c in range(tile // sub):
            cols = slice(c * sub, (c + 1) * sub)
            squash = jnp.tanh(dot(h_ref[...], ws_ref[:, cols]))
            exp_s = jnp.exp(5.0 * squash)
            sq_s[step, :, cols] = squash
            es_s[step, :, cols] = exp_s
            sum_s[0] += exp_s[:, :128] + exp_s[:, 128:]
            exp_t = jnp.exp(5.0 * jnp.tanh(dot(t_ref[...], wt_ref[:, cols])))
            et_s[step, :, cols] = exp_t
            sum_s[1] += exp_t[:, :128] + exp_t[:, 128:]

    @pl.when(step == tiles)
    def _():
        factor = scale * frame_mask(sc_ref, frames)
        for i in range(2):
            inverse = factor / jnp.sum(sum_s[i], axis=1, keepdims=True)
            sum_s[i] = jnp.broadcast_to(inverse, (frames, 128))
        g_ref[...] = jnp.zeros_like(g_ref)

    @pl.when(step >= tiles)
    def _():
        at = step - tiles
        for c in range(tile // 128):
            cols = slice(c * 128, (c + 1) * 128)
            squash = sq_s[at, :, cols]
            p = es_s[at, :, cols] * sum_s[0] - et_s[at, :, cols] * sum_s[1]
            score_ref[:, cols] = (p * (1.0 - squash * squash)).astype(BF16)
        g_ref[...] += dot_nt(score_ref[...], ws_ref[...])


def heads(sc, hidden, teacher_in, head_weight, teacher_head_weight, loss_scale):
    frames, width = hidden.shape
    wide = teacher_in.shape[1]
    scores = head_weight.shape[1]
    tiles = 4
    tile = scores // tiles
    big = pltpu.VMEM((tiles, frames, tile), F32)
    return pl.pallas_call(
        functools.partial(head_kernel, 5.0 * loss_scale, tiles),
        grid=(2 * tiles,),
        in_specs=[
            pl.BlockSpec(memory_space=pltpu.SMEM),
            pl.BlockSpec((frames, width), lambda i: (0, 0)),
            pl.BlockSpec((frames, wide), lambda i: (0, 0)),
            pl.BlockSpec((width, tile), lambda i: (0, i % tiles)),
            pl.BlockSpec((wide, tile), lambda i: (0, jnp.minimum(i, tiles - 1))),
        ],
        out_specs=[
            pl.BlockSpec((frames, tile), lambda i: (0, jnp.maximum(i - tiles, 0))),
            pl.BlockSpec((frames, width), lambda i: (0, 0)),
        ],
        scratch_shapes=[
            big,
            big,
            big,
            pltpu.VMEM((2, frames, 128), F32),
        ],
        out_shape=[
            jax.ShapeDtypeStruct((frames, scores), BF16),
            jax.ShapeDtypeStruct((frames, width), F32),
        ],
        compiler_params=params(48, "arbitrary"),
        cost_estimate=pl.CostEstimate(
            flops=2 * frames * scores * (2 * width + wide),
            bytes_accessed=scores * (6 * width + 2 * wide),
            transcendentals=4 * frames * scores,
        ),
        name="heads",
    )(sc, hidden, teacher_in, head_weight, teacher_head_weight)


def head_grad_kernel(sc_ref, ha_ref, hb_ref, ga_ref, gb_ref, out_ref, res_s):
    half = ga_ref.shape[1] // 2
    first = sc_ref[2] == 0
    for c in range(half // 128):
        cols = [slice(x * half + c * 128, x * half + (c + 1) * 128) for x in range(2)]
        ga, gb = (jnp.concatenate([ref[:, at] for at in cols], axis=1) for ref in (ga_ref, gb_ref))
        res_s[c] = dot(ha_ref[...], ga) + dot(hb_ref[...], gb)
        for nx, nz, fz in BITS:
            for fx in range(2):
                row = ((nz * 2 + fz) * 2 + (nx ^ fx)) * 32
                rows = slice(row, row + 32)
                value = res_s[c, rows, fx * 128 : (fx + 1) * 128]
                if nx != fx:
                    value = jnp.where(first, value, res_s[c, rows, nx * 128 : (nx + 1) * 128])
                out_ref[nx, 0, nz, fz, 0, :, cols[fx]] = encode(value)


def head_grad(sc, h_mine, h_other, score_mine, score_other):
    rows, frames = h_mine.shape
    scores = score_mine.shape[1]
    tile = scores // 4

    def place(i, sc):
        high, low = i // 2, i % 2
        even = sc[2] == 0
        return (0, jnp.where(even, high ^ low, high), 0, 0, jnp.where(even, high, high ^ low), 0, 0)

    hidden = pl.BlockSpec((rows, frames), lambda i, sc: (0, 0))
    score = pl.BlockSpec((frames, tile), lambda i, sc: (0, i))
    return pl.pallas_call(
        head_grad_kernel,
        grid_spec=pltpu.PrefetchScalarGridSpec(
            num_scalar_prefetch=1,
            grid=(4,),
            in_specs=[hidden, hidden, score, score],
            out_specs=pl.BlockSpec((2, 1, 2, 2, 1, 32, tile), place),
            scratch_shapes=[pltpu.VMEM((tile // 256, rows, 256), F32)],
        ),
        out_shape=jax.ShapeDtypeStruct((2, 2, 2, 2, 2, 32, tile), BF16),
        compiler_params=params(13, "arbitrary"),
        cost_estimate=pl.CostEstimate(
            flops=4 * rows * frames * scores,
            bytes_accessed=4 * frames * scores + 2 * rows * scores,
            transcendentals=0,
        ),
        name="head_grad",
    )(sc, h_mine, h_other, score_mine, score_other)


def back_kernel(sc_ref, g4_ref, h_ref, pre_ref, w_ref, send_ref, mine_ref, g_s, pad_s, tap_s, ht_s):
    step = pl.program_id(0)
    frames, width = g4_ref.shape

    @pl.when(step == 0)
    def _():
        g_s[...] = g4_ref[...]
        pad_s[...] = jnp.zeros_like(pad_s)

    g_act = frame_mask(sc_ref, frames) * g_s[...]
    pre = pre_ref[0]
    sigma = jax.nn.sigmoid(pre)
    g_pre = (g_act * sigma * (1.0 + pre * (1.0 - sigma))).astype(BF16)
    send_ref[0, :2] = g_pre.reshape(2, frames // 2, width)
    ht_s[...] = h_ref[0].T
    split_rows(sc_ref[2], ht_s, mine_ref.at[0], send_ref.at[0, 2])

    @pl.when(step < LAYERS - 1)
    def _():
        pad_s[PAD : PAD + frames] = g_pre.astype(F32)
        for at in range(LAYERS - 1, 0, -1):

            @pl.when(step == LAYERS - 1 - at)
            def _():
                reach = CLASSES * 2**at
                tap_s[0] = pad_s[PAD + reach : PAD + reach + frames].astype(BF16)
                tap_s[1] = pad_s[PAD - reach : PAD - reach + frames].astype(BF16)

        g_s[...] = (
            g_act
            + dot_nt(tap_s[0], w_ref[0, 0])
            + dot_nt(g_pre, w_ref[0, 1])
            + dot_nt(tap_s[1], w_ref[0, 2])
        )


def back(sc, g, saved, pre, weight):
    frames, width = g.shape

    def at(*block):
        return pl.BlockSpec((1, *block), lambda i: (LAYERS - 1 - i, *(0 for _ in block)))

    return pl.pallas_call(
        back_kernel,
        grid=(LAYERS,),
        in_specs=[
            pl.BlockSpec(memory_space=pltpu.SMEM),
            pl.BlockSpec((frames, width), lambda i: (0, 0)),
            at(frames, width),
            at(frames, width),
            pl.BlockSpec(
                (1, TAPS, width, width), lambda i: (jnp.maximum(LAYERS - 1 - i, 1), 0, 0, 0)
            ),
        ],
        out_specs=[at(3, frames // 2, width), at(width // 2, frames)],
        out_shape=[
            jax.ShapeDtypeStruct((LAYERS, 3, frames // 2, width), BF16),
            jax.ShapeDtypeStruct((LAYERS, width // 2, frames), BF16),
        ],
        scratch_shapes=[
            pltpu.VMEM((frames, width), F32),
            pltpu.VMEM((frames + 2 * PAD, width), F32),
            pltpu.VMEM((2, frames, width), BF16),
            pltpu.VMEM((width, frames), BF16),
        ],
        compiler_params=params(16, "arbitrary"),
        cost_estimate=pl.CostEstimate(
            flops=2 * (LAYERS - 1) * TAPS * frames * width * width,
            bytes_accessed=LAYERS * (TAPS * width * width * 2 + frames * width * 10),
            transcendentals=LAYERS * frames * width,
        ),
        name="back",
    )(sc, g, saved, pre, weight)


def conv_grad_kernel(sc_ref, mine_ref, send_ref, got_ref, out_ref, pad_s, tap_s, res_s):
    step = pl.program_id(0)
    rows, frames = mine_ref.shape[1:]
    width = send_ref.shape[3]

    @pl.when(step == 0)
    def _():
        pad_s[...] = jnp.zeros_like(pad_s)

    for side, ref in enumerate((send_ref, got_ref)):
        g_pre = ref[0, :2].reshape(frames, width)
        tap_s[1, side] = g_pre
        pad_s[side, PAD : PAD + frames] = g_pre.astype(F32)
    for at in range(LAYERS):

        @pl.when(step == at)
        def _():
            reach = CLASSES * 2**at
            for side in range(2):
                tap_s[0, side] = pad_s[side, PAD + reach : PAD + reach + frames].astype(BF16)
                tap_s[2, side] = pad_s[side, PAD - reach : PAD - reach + frames].astype(BF16)

    core = sc_ref[2]
    low = low_lanes((32, 128))
    for tap in range(TAPS):
        res_s[tap] = dot(mine_ref[0], tap_s[tap, 0]) + dot(got_ref[0, 2], tap_s[tap, 1])
        for nz, fz, ny in BITS:
            for fy in range(2):
                high = jnp.where(core == 0, fy, ny)
                cols = pl.ds(pl.multiple_of((high * 2 + (ny ^ fy)) * 128, 128), 128)
                row = (nz * 2 + fz) * 64
                a = res_s[tap, row : row + 32, cols]
                b = pltpu.roll(res_s[tap, row + 32 : row + 64, cols], 64 * core, 1)
                out_ref[0, ny, nz, tap, fz, fy] = encode(jnp.where(low, a, b))
                out_ref[1, ny, nz, tap, fz, fy] = encode(jnp.where(low, b, a))


def conv_grad(sc, mine, send, got):
    _, rows, frames = mine.shape
    width = send.shape[3]

    def at(*block):
        return pl.BlockSpec((1, *block), lambda i: (i, *(0 for _ in block)))

    return pl.pallas_call(
        conv_grad_kernel,
        grid=(LAYERS,),
        in_specs=[
            pl.BlockSpec(memory_space=pltpu.SMEM),
            at(rows, frames),
            at(3, frames // 2, width),
            at(3, frames // 2, width),
        ],
        out_specs=pl.BlockSpec(
            (2, 2, 2, TAPS, 2, 2, 32, width // 4), lambda i: (0, 0, 0, i, 0, 0, 0, 0)
        ),
        out_shape=jax.ShapeDtypeStruct((2, 2, 2, LAYERS * TAPS, 2, 2, 32, width // 4), BF16),
        scratch_shapes=[
            pltpu.VMEM((2, frames + 2 * PAD, width), F32),
            pltpu.VMEM((TAPS, 2, frames, width), BF16),
            pltpu.VMEM((TAPS, rows, width), F32),
        ],
        compiler_params=params(18, "arbitrary"),
        cost_estimate=pl.CostEstimate(
            flops=4 * LAYERS * TAPS * rows * frames * width,
            bytes_accessed=LAYERS * (7 * rows * frames * 2 + TAPS * rows * width * 2),
            transcendentals=0,
        ),
        name="conv_grad",
    )(sc, mine, send, got)


def total_of(ref, *at):
    total = decode(ref[(0, *at)])
    for i in range(1, 8):
        total = total + decode(ref[(i, *at)])
    return total


def head_far_kernel(got_ref, out_ref):
    half = got_ref.shape[-1] // 2
    for fz, fy, fx in BITS:
        for c in range(half // 128):
            lanes = slice(fx * half + c * 128, fx * half + (c + 1) * 128)
            out_ref[fx * 4 + fy * 2 + fz, c] = encode(total_of(got_ref, fz, fy, slice(None), lanes))


def head_far(got):
    tile = got.shape[-1]
    return pl.pallas_call(
        head_far_kernel,
        out_shape=jax.ShapeDtypeStruct((8, tile // 256, 32, 128), BF16),
        in_specs=[whole()],
        out_specs=whole(),
        compiler_params=params(8),
        cost_estimate=pl.CostEstimate(
            flops=8 * got.size, bytes_accessed=3 * got.size, transcendentals=got.size
        ),
        name="head_far",
    )(got)


def conv_far_kernel(a_ref, b_ref, head_ref, out_ref):
    step = pl.program_id(0)
    blocks, each = head_ref.shape[1], a_ref.shape[1]
    low = low_lanes((32, 128))

    @pl.when(step == 0)
    def _():
        out_ref[:, :blocks] = head_ref[...]

    for t in range(each):
        at = blocks + step * each + t
        for fz in range(2):
            for fy in range(2):
                a = total_of(a_ref, t, fz, fy)
                b = total_of(b_ref, t, fz, fy)
                out_ref[fy * 2 + fz, at] = encode(jnp.where(low, a, pltpu.roll(b, 64, 1)))
                out_ref[4 + fy * 2 + fz, at] = encode(jnp.where(low, pltpu.roll(a, 64, 1), b))


def conv_far(got, head):
    half = LAYERS * TAPS // 2
    steps = 3
    block = (8, half // steps, 2, 2, 32, 128)
    shape = (8, head.shape[1] + half, 32, 128)
    return pl.pallas_call(
        conv_far_kernel,
        grid=(steps,),
        out_shape=jax.ShapeDtypeStruct(shape, BF16),
        in_specs=[
            pl.BlockSpec(block, lambda i: (0, i, 0, 0, 0, 0)),
            pl.BlockSpec(block, lambda i: (0, i + steps, 0, 0, 0, 0)),
            pl.BlockSpec(head.shape, lambda i: (0, 0, 0, 0)),
        ],
        out_specs=pl.BlockSpec(shape, lambda i: (0, 0, 0, 0)),
        compiler_params=params(8, "arbitrary"),
        cost_estimate=pl.CostEstimate(
            flops=8 * got.size, bytes_accessed=3 * got.size, transcendentals=got.size
        ),
        name="conv_far",
    )(got, got, head)


def finish_kernel(got_ref, conv_ref, head_ref):
    blocks = head_ref.shape[1] // 128
    for c in range(blocks):
        head_ref[:, c * 128 : (c + 1) * 128] = total_of(got_ref, c)
    half = LAYERS * TAPS // 2
    for t in range(half):
        total = total_of(got_ref, blocks + t)
        for tap, value in ((t, total), (t + half, pltpu.roll(total, 64, 1))):
            conv_ref[tap // TAPS, tap % TAPS] = value[:, :64]


def finish(got, scores):
    return pl.pallas_call(
        finish_kernel,
        out_shape=[
            jax.ShapeDtypeStruct((LAYERS, TAPS, 32, 64), F32),
            jax.ShapeDtypeStruct((32, scores // 8), F32),
        ],
        in_specs=[whole()],
        out_specs=[whole(), whole()],
        compiler_params=params(4),
        name="finish",
    )(got)


def swap(x):
    return lax.ppermute(x, AXES, other_core())


def on_device(student_in, teacher_rows, valid, conv_weight, head_weight, teacher_head_weight):
    _, frames, width = student_in.shape
    scores = head_weight.shape[1]
    loss_scale = scores / (3.0 * math.sqrt(READ * TM * frames))
    sc = jnp.stack([valid[0], lax.axis_index("tm"), lax.axis_index("read") % 2])
    regrouped = regroup(student_in[0]).reshape(TM, frames // TM, width)
    student = exchange(regrouped, frame_groups()).reshape(frames, width)
    teacher = regroup(teacher_rows[0]).reshape(TM, frames // TM, -1)
    teacher = exchange(teacher, frame_groups()).reshape(frames, -1)

    saved, pre, hidden, h_mine, h_other = convolve(sc, student, conv_weight)
    h_got, hidden = lax.optimization_barrier((swap(h_other), hidden))
    score, g = heads(sc, hidden, teacher, head_weight, teacher_head_weight, loss_scale)
    score_got = swap(score)
    send, mine = back(sc, g, saved, pre, conv_weight)
    got = swap(send)
    score_got, mine = lax.optimization_barrier((score_got, mine))
    near = head_grad(sc, h_mine, h_got, score, score_got)
    near, got = lax.optimization_barrier((near, got))
    head_got = exchange(near.reshape(8, 4 * 32, scores // 4), near_groups())
    near = conv_grad(sc, mine, send, got)
    near, head_got = lax.optimization_barrier((near, head_got))
    conv_got = exchange(near.reshape(8, LAYERS * TAPS * 4 * 32, width // 4), near_groups())

    far = head_far(head_got.reshape(8, 2, 2, 32, scores // 4))
    far = conv_far(conv_got.reshape(8, LAYERS * TAPS, 2, 2, 32, width // 4), far)
    return tuple(finish(exchange(far, far_groups()), scores))


def solution(mesh):
    return jax.shard_map(
        on_device,
        mesh=mesh,
        in_specs=(P("read", "tm", None), P("read", "tm", None), P("read"), P(), P(), P()),
        out_specs=(P(None, None, "read", "tm"), P("read", "tm")),
        check_vma=False,
    )
```

```python
import functools
import math

import jax
import jax.numpy as jnp
from jax import lax
from jax.experimental import pallas as pl
from jax.experimental.pallas import tpu as pltpu
from jax.sharding import PartitionSpec as P

LAYERS, TAPS = 4, 3
BASE_DILATION = 32
AXES = ("read", "tm")
READ, TM = 16, 8
CLASSES = BASE_DILATION // TM
PAD = CLASSES * 2 ** (LAYERS - 1)
BITS = [(a, b, c) for a in range(2) for b in range(2) for c in range(2)]
F32, BF16 = jnp.float32, jnp.bfloat16


def near_of(core, v):
    return (v // 2) ^ (v % 2) if core == 0 else v // 2


def far_of(core, v):
    return v // 2 if core == 0 else (v // 2) ^ (v % 2)


def high_low(core, near, far):
    return (far if core == 0 else near, near ^ far)


def device_index(x, y, z, core):
    return (((x % 2) * 4 + z) * 2 + core) * TM + y * 2 + x // 2


def groups_of(fixed, order):
    groups = {}
    for core in range(2):
        for x in range(4):
            for y in range(4):
                for z in range(4):
                    key = (core, fixed(core, x), fixed(core, y), fixed(core, z))
                    place = order(core, x) * 4 + order(core, y) * 2 + order(core, z)
                    groups.setdefault(key, [0] * 8)[place] = device_index(x, y, z, core)
    return list(groups.values())


def near_groups():
    def cube(core, v):
        return (v + core) % 4 // 2

    return groups_of(cube, near_of)


def far_groups():
    return groups_of(near_of, far_of)


def other_core():
    return [(d, d ^ TM) for d in range(READ * TM)]


def frame_groups():
    return [[r * TM + t for t in range(TM)] for r in range(READ)]


def exchange(x, groups):
    return lax.all_to_all(x, AXES, 0, 0, tiled=True, axis_index_groups=groups)


def encode(x):
    return (x * jnp.abs(x)).astype(BF16)


def decode(y):
    y = y.astype(F32)
    return y * lax.rsqrt(jnp.maximum(jnp.abs(y), 1e-37))


def low_lanes(shape):
    return lax.broadcasted_iota(jnp.int32, shape, len(shape) - 1) < 64


def dot(a, b):
    return jnp.dot(a, b, preferred_element_type=F32)


def dot_nt(a, b):
    return lax.dot_general(a, b, (((1,), (1,)), ((), ())), preferred_element_type=F32)


def params(mib, *kinds):
    return pltpu.CompilerParams(dimension_semantics=kinds, vmem_limit_bytes=mib * 1024 * 1024)


def whole():
    return pl.BlockSpec(memory_space=pltpu.VMEM)


def in_hbm(x):
    return pltpu.with_memory_space_constraint(x, pltpu.HBM)


AFTER = pl.BlockSpec(memory_space=pl.ANY)


def frame_mask(sc_ref, frames):
    row = lax.broadcasted_iota(jnp.int32, (frames, 1), 0)
    position = row // CLASSES * BASE_DILATION + sc_ref[1] * CLASSES + row % CLASSES
    return (position < sc_ref[0]).astype(F32)


def regroup_kernel(x_ref, out_ref):
    frames = x_ref.shape[0]
    row = lax.broadcasted_iota(jnp.int32, (frames, frames), 0)
    col = lax.broadcasted_iota(jnp.int32, (frames, frames), 1)
    per = frames // TM
    source = (row % per) // CLASSES * BASE_DILATION + row // per * CLASSES + row % CLASSES
    select = jnp.where(col == source, 1.0, 0.0).astype(BF16)
    out_ref[...] = dot(select, x_ref[...]).astype(BF16)


def regroup(x):
    return pl.pallas_call(
        regroup_kernel,
        out_shape=jax.ShapeDtypeStruct(x.shape, BF16),
        in_specs=[whole()],
        out_specs=whole(),
        compiler_params=params(5),
        name="regroup",
    )(x)


def split_rows(core, ht_s, mine_ref, other_ref):
    for ref, owner in ((mine_ref, core), (other_ref, 1 - core)):
        for at, (nz, fz, xl) in enumerate(BITS):
            high = jnp.where(owner == 0, fz, nz)
            row = ((xl * 4 + high * 2 + (nz ^ fz)) * 2 + owner) * 32
            ref[at * 32 : (at + 1) * 32] = ht_s[pl.ds(pl.multiple_of(row, 32), 32)]


def conv_kernel(sc_ref, x_ref, w_ref, saved_ref, pre_ref, last_ref, mine_ref, other_ref, pad_s, tap_s, ht_s):
    layer = pl.program_id(0)
    frames = x_ref.shape[0]

    @pl.when(layer == 0)
    def _():
        pad_s[...] = jnp.zeros_like(pad_s)
        pad_s[PAD : PAD + frames] = x_ref[...].astype(F32)

    for at in range(LAYERS):

        @pl.when(layer == at)
        def _():
            reach = CLASSES * 2**at
            tap_s[0] = pad_s[PAD - reach : PAD - reach + frames].astype(BF16)
            tap_s[1] = pad_s[PAD + reach : PAD + reach + frames].astype(BF16)

    hidden = pad_s[PAD : PAD + frames]
    middle = hidden.astype(BF16)
    saved_ref[0] = middle
    pre = dot(tap_s[0], w_ref[0, 0]) + dot(middle, w_ref[0, 1]) + dot(tap_s[1], w_ref[0, 2])
    pre_ref[0] = pre
    new = (frame_mask(sc_ref, frames) * (hidden + jax.nn.silu(pre))).astype(BF16)
    pad_s[PAD : PAD + frames] = new.astype(F32)

    @pl.when(layer == LAYERS - 1)
    def _():
        last_ref[...] = new
        ht_s[...] = new.T
        split_rows(sc_ref[2], ht_s, mine_ref, other_ref)


def convolve(sc, x, weight):
    frames, width = x.shape
    one = pl.BlockSpec((1, frames, width), lambda i: (i, 0, 0))
    flat = pl.BlockSpec((frames, width), lambda i: (0, 0))
    rows = pl.BlockSpec((width // 2, frames), lambda i: (0, 0))
    return pl.pallas_call(
        conv_kernel,
        grid=(LAYERS,),
        in_specs=[
            pl.BlockSpec(memory_space=pltpu.SMEM),
            flat,
            pl.BlockSpec((1, TAPS, width, width), lambda i: (i, 0, 0, 0)),
        ],
        out_specs=[one, one, flat, rows, rows],
        out_shape=[
            jax.ShapeDtypeStruct((LAYERS, frames, width), BF16),
            pltpu.HBM((LAYERS, frames, width), F32),
            pltpu.HBM((frames, width), BF16),
            pltpu.HBM((width // 2, frames), BF16),
            pltpu.HBM((width // 2, frames), BF16),
        ],
        scratch_shapes=[
            pltpu.VMEM((frames + 2 * PAD, width), F32),
            pltpu.VMEM((2, frames, width), BF16),
            pltpu.VMEM((width, frames), BF16),
        ],
        compiler_params=params(14, "arbitrary"),
        cost_estimate=pl.CostEstimate(
            flops=2 * LAYERS * TAPS * frames * width * width,
            bytes_accessed=LAYERS * (TAPS * width * width * 2 + frames * width * 6),
            transcendentals=LAYERS * frames * width,
        ),
        name="convolve",
    )(sc, x, in_hbm(weight))


def head_kernel(scale, tiles, sc_ref, h_ref, t_ref, ws_ref, wt_ref, _, score_ref, g_ref,
                sq_s, et_s, sum_s):
    step = pl.program_id(0)
    frames, width = h_ref.shape
    tile = ws_ref.shape[1]
    sub = 256

    @pl.when(step == 0)
    def _():
        sum_s[...] = jnp.zeros_like(sum_s)

    @pl.when(step < tiles)
    def _():
        for c in range(tile // sub):
            cols = slice(c * sub, (c + 1) * sub)
            squash = jnp.tanh(dot(h_ref[...], ws_ref[:, cols]))
            exp_s = jnp.exp(5.0 * squash)
            sq_s[step, :, cols] = squash
            sum_s[0] += exp_s[:, :128] + exp_s[:, 128:]
            exp_t = jnp.exp(5.0 * jnp.tanh(dot(t_ref[...], wt_ref[:, cols])))
            et_s[step, :, cols] = exp_t
            sum_s[1] += exp_t[:, :128] + exp_t[:, 128:]

    @pl.when(step == tiles)
    def _():
        factor = scale * frame_mask(sc_ref, frames)
        for i in range(2):
            inverse = factor / jnp.sum(sum_s[i], axis=1, keepdims=True)
            sum_s[i] = jnp.broadcast_to(inverse, (frames, 128))
        g_ref[...] = jnp.zeros_like(g_ref)

    @pl.when(step >= tiles)
    def _():
        at = step - tiles
        for c in range(tile // 128):
            cols = slice(c * 128, (c + 1) * 128)
            squash = sq_s[at, :, cols]
            p = jnp.exp(5.0 * squash) * sum_s[0] - et_s[at, :, cols] * sum_s[1]
            score_ref[:, cols] = (p * (1.0 - squash * squash)).astype(BF16)
        g_ref[...] += dot_nt(score_ref[...], ws_ref[...])


def heads(sc, hidden, teacher_in, head_weight, teacher_head_weight, after, loss_scale):
    frames, width = hidden.shape
    wide = teacher_in.shape[1]
    scores = head_weight.shape[1]
    tiles = 4
    tile = scores // tiles
    big = pltpu.VMEM((tiles, frames, tile), F32)
    return pl.pallas_call(
        functools.partial(head_kernel, 5.0 * loss_scale, tiles),
        grid=(2 * tiles,),
        in_specs=[
            pl.BlockSpec(memory_space=pltpu.SMEM),
            pl.BlockSpec((frames, width), lambda i: (0, 0)),
            pl.BlockSpec((frames, wide), lambda i: (0, 0)),
            pl.BlockSpec((width, tile), lambda i: (0, i % tiles)),
            pl.BlockSpec((wide, tile), lambda i: (0, jnp.minimum(i, tiles - 1))),
            AFTER,
        ],
        out_specs=[
            pl.BlockSpec((frames, tile), lambda i: (0, jnp.maximum(i - tiles, 0))),
            pl.BlockSpec((frames, width), lambda i: (0, 0)),
        ],
        scratch_shapes=[
            big,
            big,
            pltpu.VMEM((2, frames, 128), F32),
        ],
        out_shape=[
            jax.ShapeDtypeStruct((frames, scores), BF16),
            jax.ShapeDtypeStruct((frames, width), F32),
        ],
        compiler_params=params(37, "arbitrary"),
        cost_estimate=pl.CostEstimate(
            flops=2 * frames * scores * (2 * width + wide),
            bytes_accessed=scores * (6 * width + 2 * wide),
            transcendentals=4 * frames * scores,
        ),
        name="heads",
    )(sc, hidden, teacher_in, in_hbm(head_weight), in_hbm(teacher_head_weight), after)


def head_grad_kernel(sc_ref, ha_ref, hb_ref, ga_ref, gb_ref, _, out_ref, res_s):
    half = ga_ref.shape[1] // 2
    first = sc_ref[2] == 0
    for c in range(half // 128):
        cols = [slice(x * half + c * 128, x * half + (c + 1) * 128) for x in range(2)]
        ga, gb = (jnp.concatenate([ref[:, at] for at in cols], axis=1) for ref in (ga_ref, gb_ref))
        res_s[c] = dot(ha_ref[...], ga) + dot(hb_ref[...], gb)
        for nx, nz, fz in BITS:
            for fx in range(2):
                row = ((nz * 2 + fz) * 2 + (nx ^ fx)) * 32
                rows = slice(row, row + 32)
                value = res_s[c, rows, fx * 128 : (fx + 1) * 128]
                if nx != fx:
                    value = jnp.where(first, value, res_s[c, rows, nx * 128 : (nx + 1) * 128])
                out_ref[nx, 0, nz, fz, 0, :, cols[fx]] = encode(value)


def head_grad(sc, h_mine, h_other, score_mine, score_other, after):
    rows, frames = h_mine.shape
    scores = score_mine.shape[1]
    tile = scores // 4

    def place(i, sc):
        high, low = i // 2, i % 2
        even = sc[2] == 0
        return (0, jnp.where(even, high ^ low, high), 0, 0, jnp.where(even, high, high ^ low), 0, 0)

    hidden = pl.BlockSpec((rows, frames), lambda i, sc: (0, 0))
    score = pl.BlockSpec((frames, tile), lambda i, sc: (0, i))
    return pl.pallas_call(
        head_grad_kernel,
        grid_spec=pltpu.PrefetchScalarGridSpec(
            num_scalar_prefetch=1,
            grid=(4,),
            in_specs=[hidden, hidden, score, score, AFTER],
            out_specs=pl.BlockSpec((2, 1, 2, 2, 1, 32, tile), place),
            scratch_shapes=[pltpu.VMEM((tile // 256, rows, 256), F32)],
        ),
        out_shape=jax.ShapeDtypeStruct((2, 2, 2, 2, 2, 32, tile), BF16),
        compiler_params=params(13, "arbitrary"),
        cost_estimate=pl.CostEstimate(
            flops=4 * rows * frames * scores,
            bytes_accessed=4 * frames * scores + 2 * rows * scores,
            transcendentals=0,
        ),
        name="head_grad",
    )(sc, h_mine, h_other, score_mine, score_other, in_hbm(after))


def back_kernel(sc_ref, g4_ref, h_ref, pre_ref, w_ref, send_ref, mine_ref, g_s, pad_s, tap_s, ht_s):
    step = pl.program_id(0)
    frames, width = g4_ref.shape

    @pl.when(step == 0)
    def _():
        g_s[...] = g4_ref[...]
        pad_s[...] = jnp.zeros_like(pad_s)

    g_act = frame_mask(sc_ref, frames) * g_s[...]
    pre = pre_ref[0]
    sigma = jax.nn.sigmoid(pre)
    g_pre = (g_act * sigma * (1.0 + pre * (1.0 - sigma))).astype(BF16)
    send_ref[0, :2] = g_pre.reshape(2, frames // 2, width)
    ht_s[...] = h_ref[0].T
    split_rows(sc_ref[2], ht_s, mine_ref.at[0], send_ref.at[0, 2])

    @pl.when(step < LAYERS - 1)
    def _():
        pad_s[PAD : PAD + frames] = g_pre.astype(F32)
        for at in range(LAYERS - 1, 0, -1):

            @pl.when(step == LAYERS - 1 - at)
            def _():
                reach = CLASSES * 2**at
                tap_s[0] = pad_s[PAD + reach : PAD + reach + frames].astype(BF16)
                tap_s[1] = pad_s[PAD - reach : PAD - reach + frames].astype(BF16)

        g_s[...] = (
            g_act
            + dot_nt(tap_s[0], w_ref[0, 0])
            + dot_nt(g_pre, w_ref[0, 1])
            + dot_nt(tap_s[1], w_ref[0, 2])
        )


def back(sc, g, saved, pre, weight):
    frames, width = g.shape

    def at(*block):
        return pl.BlockSpec((1, *block), lambda i: (LAYERS - 1 - i, *(0 for _ in block)))

    return pl.pallas_call(
        back_kernel,
        grid=(LAYERS,),
        in_specs=[
            pl.BlockSpec(memory_space=pltpu.SMEM),
            pl.BlockSpec((frames, width), lambda i: (0, 0)),
            at(frames, width),
            at(frames, width),
            pl.BlockSpec(
                (1, TAPS, width, width), lambda i: (jnp.maximum(LAYERS - 1 - i, 1), 0, 0, 0)
            ),
        ],
        out_specs=[at(3, frames // 2, width), at(width // 2, frames)],
        out_shape=[
            jax.ShapeDtypeStruct((LAYERS, 3, frames // 2, width), BF16),
            pltpu.HBM((LAYERS, width // 2, frames), BF16),
        ],
        scratch_shapes=[
            pltpu.VMEM((frames, width), F32),
            pltpu.VMEM((frames + 2 * PAD, width), F32),
            pltpu.VMEM((2, frames, width), BF16),
            pltpu.VMEM((width, frames), BF16),
        ],
        compiler_params=params(16, "arbitrary"),
        cost_estimate=pl.CostEstimate(
            flops=2 * (LAYERS - 1) * TAPS * frames * width * width,
            bytes_accessed=LAYERS * (TAPS * width * width * 2 + frames * width * 10),
            transcendentals=LAYERS * frames * width,
        ),
        name="back",
    )(sc, g, saved, pre, weight)


def conv_grad_kernel(sc_ref, mine_ref, send_ref, got_ref, _, out_ref, pad_s, tap_s, res_s):
    step = pl.program_id(0)
    rows, frames = mine_ref.shape[1:]
    width = send_ref.shape[3]

    @pl.when(step == 0)
    def _():
        pad_s[...] = jnp.zeros_like(pad_s)

    for side, ref in enumerate((send_ref, got_ref)):
        g_pre = ref[0, :2].reshape(frames, width)
        tap_s[1, side] = g_pre
        pad_s[side, PAD : PAD + frames] = g_pre.astype(F32)
    for at in range(LAYERS):

        @pl.when(step == at)
        def _():
            reach = CLASSES * 2**at
            for side in range(2):
                tap_s[0, side] = pad_s[side, PAD + reach : PAD + reach + frames].astype(BF16)
                tap_s[2, side] = pad_s[side, PAD - reach : PAD - reach + frames].astype(BF16)

    core = sc_ref[2]
    low = low_lanes((32, 128))
    for tap in range(TAPS):
        res_s[tap] = dot(mine_ref[0], tap_s[tap, 0]) + dot(got_ref[0, 2], tap_s[tap, 1])
        for nz, fz, ny in BITS:
            for fy in range(2):
                high = jnp.where(core == 0, fy, ny)
                cols = pl.ds(pl.multiple_of((high * 2 + (ny ^ fy)) * 128, 128), 128)
                row = (nz * 2 + fz) * 64
                a = res_s[tap, row : row + 32, cols]
                b = pltpu.roll(res_s[tap, row + 32 : row + 64, cols], 64 * core, 1)
                out_ref[0, ny, nz, tap, fz, fy] = encode(jnp.where(low, a, b))
                out_ref[1, ny, nz, tap, fz, fy] = encode(jnp.where(low, b, a))


def conv_grad(sc, mine, send, got, after):
    _, rows, frames = mine.shape
    width = send.shape[3]

    def at(*block):
        return pl.BlockSpec((1, *block), lambda i: (i, *(0 for _ in block)))

    return pl.pallas_call(
        conv_grad_kernel,
        grid=(LAYERS,),
        in_specs=[
            pl.BlockSpec(memory_space=pltpu.SMEM),
            at(rows, frames),
            at(3, frames // 2, width),
            at(3, frames // 2, width),
            AFTER,
        ],
        out_specs=pl.BlockSpec(
            (2, 2, 2, TAPS, 2, 2, 32, width // 4), lambda i: (0, 0, 0, i, 0, 0, 0, 0)
        ),
        out_shape=pltpu.HBM((2, 2, 2, LAYERS * TAPS, 2, 2, 32, width // 4), BF16),
        scratch_shapes=[
            pltpu.VMEM((2, frames + 2 * PAD, width), F32),
            pltpu.VMEM((TAPS, 2, frames, width), BF16),
            pltpu.VMEM((TAPS, rows, width), F32),
        ],
        compiler_params=params(18, "arbitrary"),
        cost_estimate=pl.CostEstimate(
            flops=4 * LAYERS * TAPS * rows * frames * width,
            bytes_accessed=LAYERS * (7 * rows * frames * 2 + TAPS * rows * width * 2),
            transcendentals=0,
        ),
        name="conv_grad",
    )(sc, mine, send, got, in_hbm(after))


def total_of(ref, *at):
    total = decode(ref[(0, *at)])
    for i in range(1, 8):
        total = total + decode(ref[(i, *at)])
    return total


def head_far_kernel(got_ref, out_ref):
    half = got_ref.shape[-1] // 2
    for fz, fy, fx in BITS:
        for c in range(half // 128):
            lanes = slice(fx * half + c * 128, fx * half + (c + 1) * 128)
            out_ref[fx * 4 + fy * 2 + fz, c] = encode(total_of(got_ref, fz, fy, slice(None), lanes))


def head_far(got):
    tile = got.shape[-1]
    return pl.pallas_call(
        head_far_kernel,
        out_shape=jax.ShapeDtypeStruct((8, tile // 256, 32, 128), BF16),
        in_specs=[whole()],
        out_specs=whole(),
        compiler_params=params(8),
        cost_estimate=pl.CostEstimate(
            flops=8 * got.size, bytes_accessed=3 * got.size, transcendentals=got.size
        ),
        name="head_far",
    )(in_hbm(got))


def conv_far_kernel(a_ref, b_ref, head_ref, out_ref):
    step = pl.program_id(0)
    blocks, each = head_ref.shape[1], a_ref.shape[1]
    low = low_lanes((32, 128))

    @pl.when(step == 0)
    def _():
        out_ref[:, :blocks] = head_ref[...]

    for t in range(each):
        at = blocks + step * each + t
        for fz in range(2):
            for fy in range(2):
                a = total_of(a_ref, t, fz, fy)
                b = total_of(b_ref, t, fz, fy)
                out_ref[fy * 2 + fz, at] = encode(jnp.where(low, a, pltpu.roll(b, 64, 1)))
                out_ref[4 + fy * 2 + fz, at] = encode(jnp.where(low, pltpu.roll(a, 64, 1), b))


def conv_far(got, head):
    half = LAYERS * TAPS // 2
    steps = 3
    block = (8, half // steps, 2, 2, 32, 128)
    shape = (8, head.shape[1] + half, 32, 128)
    return pl.pallas_call(
        conv_far_kernel,
        grid=(steps,),
        out_shape=jax.ShapeDtypeStruct(shape, BF16),
        in_specs=[
            pl.BlockSpec(block, lambda i: (0, i, 0, 0, 0, 0)),
            pl.BlockSpec(block, lambda i: (0, i + steps, 0, 0, 0, 0)),
            pl.BlockSpec(head.shape, lambda i: (0, 0, 0, 0)),
        ],
        out_specs=pl.BlockSpec(shape, lambda i: (0, 0, 0, 0)),
        compiler_params=params(8, "arbitrary"),
        cost_estimate=pl.CostEstimate(
            flops=8 * got.size, bytes_accessed=3 * got.size, transcendentals=got.size
        ),
        name="conv_far",
    )(got, got, head)


def finish_kernel(got_ref, conv_ref, head_ref):
    blocks = head_ref.shape[1] // 128
    for c in range(blocks):
        head_ref[:, c * 128 : (c + 1) * 128] = total_of(got_ref, c)
    half = LAYERS * TAPS // 2
    for t in range(half):
        total = total_of(got_ref, blocks + t)
        for tap, value in ((t, total), (t + half, pltpu.roll(total, 64, 1))):
            conv_ref[tap // TAPS, tap % TAPS] = value[:, :64]


def finish(got, scores):
    return pl.pallas_call(
        finish_kernel,
        out_shape=[
            jax.ShapeDtypeStruct((LAYERS, TAPS, 32, 64), F32),
            jax.ShapeDtypeStruct((32, scores // 8), F32),
        ],
        in_specs=[whole()],
        out_specs=[whole(), whole()],
        compiler_params=params(4),
        name="finish",
    )(got)


def swap(x):
    return lax.ppermute(x, AXES, other_core())


def on_device(student_in, teacher_rows, valid, conv_weight, head_weight, teacher_head_weight):
    _, frames, width = student_in.shape
    scores = head_weight.shape[1]
    loss_scale = scores / (3.0 * math.sqrt(READ * TM * frames))
    sc = jnp.stack([valid[0], lax.axis_index("tm"), lax.axis_index("read") % 2])
    regrouped = regroup(student_in[0]).reshape(TM, frames // TM, width)
    student = exchange(regrouped, frame_groups()).reshape(frames, width)
    teacher = regroup(teacher_rows[0]).reshape(TM, frames // TM, -1)
    teacher = exchange(teacher, frame_groups()).reshape(frames, -1)

    saved, pre, hidden, h_mine, h_other = convolve(sc, student, conv_weight)
    h_got = swap(h_other)
    score, g = heads(
        sc, hidden, teacher, head_weight, teacher_head_weight, h_got, loss_scale
    )
    score_got = swap(score)
    send, mine = back(sc, g, saved, pre, conv_weight)
    got = swap(send)
    near = head_grad(sc, h_mine, h_got, score, score_got, mine)
    head_got = exchange(near.reshape(8, 4 * 32, scores // 4), near_groups())
    near = conv_grad(sc, mine, send, got, near)
    conv_got = exchange(near.reshape(8, LAYERS * TAPS * 4 * 32, width // 4), near_groups())

    far = head_far(head_got.reshape(8, 2, 2, 32, scores // 4))
    far = conv_far(conv_got.reshape(8, LAYERS * TAPS, 2, 2, 32, width // 4), far)
    return tuple(finish(exchange(far, far_groups()), scores))


def solution(mesh):
    return jax.shard_map(
        on_device,
        mesh=mesh,
        in_specs=(P("read", "tm", None), P("read", "tm", None), P("read"), P(), P(), P()),
        out_specs=(P(None, None, "read", "tm"), P("read", "tm")),
        check_vma=False,
    )
```

```python
import functools
import math

import jax
import jax.numpy as jnp
from jax import lax
from jax.experimental import pallas as pl
from jax.experimental.pallas import tpu as pltpu
from jax.sharding import PartitionSpec as P

LAYERS, TAPS = 4, 3
BASE_DILATION = 32
AXES = ("read", "tm")
READ, TM = 16, 8
CLASSES = BASE_DILATION // TM
PAD = CLASSES * 2 ** (LAYERS - 1)
BITS = [(a, b, c) for a in range(2) for b in range(2) for c in range(2)]
F32, BF16 = jnp.float32, jnp.bfloat16


def near_of(core, v):
    return (v // 2) ^ (v % 2) if core == 0 else v // 2


def far_of(core, v):
    return v // 2 if core == 0 else (v // 2) ^ (v % 2)


def high_low(core, near, far):
    return (far if core == 0 else near, near ^ far)


def device_index(x, y, z, core):
    return (((x % 2) * 4 + z) * 2 + core) * TM + y * 2 + x // 2


def groups_of(fixed, order):
    groups = {}
    for core in range(2):
        for x in range(4):
            for y in range(4):
                for z in range(4):
                    key = (core, fixed(core, x), fixed(core, y), fixed(core, z))
                    place = order(core, x) * 4 + order(core, y) * 2 + order(core, z)
                    groups.setdefault(key, [0] * 8)[place] = device_index(x, y, z, core)
    return list(groups.values())


def near_groups():
    def cube(core, v):
        return (v + core) % 4 // 2

    return groups_of(cube, near_of)


def near_swap(x, bits):
    pairs = [(group[i], group[i ^ bits]) for group in near_groups() for i in range(8)]
    return lax.ppermute(x, AXES, pairs)


def far_groups():
    return groups_of(near_of, far_of)


def other_core():
    return [(d, d ^ TM) for d in range(READ * TM)]


def frame_groups():
    return [[r * TM + t for t in range(TM)] for r in range(READ)]


def exchange(x, groups):
    return lax.all_to_all(x, AXES, 0, 0, tiled=True, axis_index_groups=groups)


def encode(x):
    return (x * jnp.abs(x)).astype(BF16)


def decode(y):
    y = y.astype(F32)
    return y * lax.rsqrt(jnp.maximum(jnp.abs(y), 1e-37))


def low_lanes(shape):
    return lax.broadcasted_iota(jnp.int32, shape, len(shape) - 1) < 64


def dot(a, b):
    return jnp.dot(a, b, preferred_element_type=F32)


def dot_nt(a, b):
    return lax.dot_general(a, b, (((1,), (1,)), ((), ())), preferred_element_type=F32)


def params(mib, *kinds):
    return pltpu.CompilerParams(dimension_semantics=kinds, vmem_limit_bytes=mib * 1024 * 1024)


def whole():
    return pl.BlockSpec(memory_space=pltpu.VMEM)


def in_hbm(x):
    return pltpu.with_memory_space_constraint(x, pltpu.HBM)


AFTER = pl.BlockSpec(memory_space=pl.ANY)


def frame_mask(sc_ref, frames):
    row = lax.broadcasted_iota(jnp.int32, (frames, 1), 0)
    position = row // CLASSES * BASE_DILATION + sc_ref[1] * CLASSES + row % CLASSES
    return (position < sc_ref[0]).astype(F32)


def regroup_kernel(x_ref, out_ref):
    frames = x_ref.shape[0]
    row = lax.broadcasted_iota(jnp.int32, (frames, frames), 0)
    col = lax.broadcasted_iota(jnp.int32, (frames, frames), 1)
    per = frames // TM
    source = (row % per) // CLASSES * BASE_DILATION + row // per * CLASSES + row % CLASSES
    select = jnp.where(col == source, 1.0, 0.0).astype(BF16)
    out_ref[...] = dot(select, x_ref[...]).astype(BF16)


def regroup(x):
    return pl.pallas_call(
        regroup_kernel,
        out_shape=jax.ShapeDtypeStruct(x.shape, BF16),
        in_specs=[whole()],
        out_specs=whole(),
        compiler_params=params(5),
        name="regroup",
    )(x)


def split_rows(core, ht_s, mine_ref, other_ref):
    for ref, owner in ((mine_ref, core), (other_ref, 1 - core)):
        for at, (nz, fz, xl) in enumerate(BITS):
            high = jnp.where(owner == 0, fz, nz)
            row = ((xl * 4 + high * 2 + (nz ^ fz)) * 2 + owner) * 32
            ref[at * 32 : (at + 1) * 32] = ht_s[pl.ds(pl.multiple_of(row, 32), 32)]


def conv_kernel(sc_ref, x_ref, w_ref, saved_ref, pre_ref, last_ref, mine_ref, other_ref, pad_s, tap_s, ht_s):
    layer = pl.program_id(0)
    frames = x_ref.shape[0]

    @pl.when(layer == 0)
    def _():
        pad_s[...] = jnp.zeros_like(pad_s)
        pad_s[PAD : PAD + frames] = x_ref[...].astype(F32)

    for at in range(LAYERS):

        @pl.when(layer == at)
        def _():
            reach = CLASSES * 2**at
            tap_s[0] = pad_s[PAD - reach : PAD - reach + frames].astype(BF16)
            tap_s[1] = pad_s[PAD + reach : PAD + reach + frames].astype(BF16)

    hidden = pad_s[PAD : PAD + frames]
    middle = hidden.astype(BF16)
    saved_ref[0] = middle
    pre = dot(tap_s[0], w_ref[0, 0]) + dot(middle, w_ref[0, 1]) + dot(tap_s[1], w_ref[0, 2])
    pre_ref[0] = pre
    new = (frame_mask(sc_ref, frames) * (hidden + jax.nn.silu(pre))).astype(BF16)
    pad_s[PAD : PAD + frames] = new.astype(F32)

    @pl.when(layer == LAYERS - 1)
    def _():
        last_ref[...] = new
        ht_s[...] = new.T
        split_rows(sc_ref[2], ht_s, mine_ref, other_ref)


def convolve(sc, x, weight):
    frames, width = x.shape
    one = pl.BlockSpec((1, frames, width), lambda i: (i, 0, 0))
    flat = pl.BlockSpec((frames, width), lambda i: (0, 0))
    rows = pl.BlockSpec((width // 2, frames), lambda i: (0, 0))
    return pl.pallas_call(
        conv_kernel,
        grid=(LAYERS,),
        in_specs=[
            pl.BlockSpec(memory_space=pltpu.SMEM),
            flat,
            pl.BlockSpec((1, TAPS, width, width), lambda i: (i, 0, 0, 0)),
        ],
        out_specs=[one, one, flat, rows, rows],
        out_shape=[
            jax.ShapeDtypeStruct((LAYERS, frames, width), BF16),
            pltpu.HBM((LAYERS, frames, width), F32),
            pltpu.HBM((frames, width), BF16),
            pltpu.HBM((width // 2, frames), BF16),
            pltpu.HBM((width // 2, frames), BF16),
        ],
        scratch_shapes=[
            pltpu.VMEM((frames + 2 * PAD, width), F32),
            pltpu.VMEM((2, frames, width), BF16),
            pltpu.VMEM((width, frames), BF16),
        ],
        compiler_params=params(14, "arbitrary"),
        cost_estimate=pl.CostEstimate(
            flops=2 * LAYERS * TAPS * frames * width * width,
            bytes_accessed=LAYERS * (TAPS * width * width * 2 + frames * width * 6),
            transcendentals=LAYERS * frames * width,
        ),
        name="convolve",
    )(sc, x, in_hbm(weight))


def head_kernel(scale, tiles, sc_ref, h_ref, t_ref, ws_ref, wt_ref, _, score_ref, g_ref,
                sq_s, et_s, sum_s):
    step = pl.program_id(0)
    frames, width = h_ref.shape
    tile = ws_ref.shape[1]
    sub = 256

    @pl.when(step == 0)
    def _():
        sum_s[...] = jnp.zeros_like(sum_s)

    @pl.when(step < tiles)
    def _():
        for c in range(tile // sub):
            cols = slice(c * sub, (c + 1) * sub)
            squash = jnp.tanh(dot(h_ref[...], ws_ref[:, cols]))
            exp_s = jnp.exp(5.0 * squash)
            sq_s[step, :, cols] = squash
            sum_s[0] += exp_s[:, :128] + exp_s[:, 128:]
            exp_t = jnp.exp(5.0 * jnp.tanh(dot(t_ref[...], wt_ref[:, cols])))
            et_s[step, :, cols] = exp_t
            sum_s[1] += exp_t[:, :128] + exp_t[:, 128:]

    @pl.when(step == tiles)
    def _():
        factor = scale * frame_mask(sc_ref, frames)
        for i in range(2):
            inverse = factor / jnp.sum(sum_s[i], axis=1, keepdims=True)
            sum_s[i] = jnp.broadcast_to(inverse, (frames, 128))
        g_ref[...] = jnp.zeros_like(g_ref)

    @pl.when(step >= tiles)
    def _():
        at = step - tiles
        for c in range(tile // 128):
            cols = slice(c * 128, (c + 1) * 128)
            squash = sq_s[at, :, cols]
            p = jnp.exp(5.0 * squash) * sum_s[0] - et_s[at, :, cols] * sum_s[1]
            score_ref[:, cols] = (p * (1.0 - squash * squash)).astype(BF16)
        g_ref[...] += dot_nt(score_ref[...], ws_ref[...])


def heads(sc, hidden, teacher_in, head_weight, teacher_head_weight, after, loss_scale):
    frames, width = hidden.shape
    wide = teacher_in.shape[1]
    scores = head_weight.shape[1]
    tiles = 4
    tile = scores // tiles
    big = pltpu.VMEM((tiles, frames, tile), F32)
    return pl.pallas_call(
        functools.partial(head_kernel, 5.0 * loss_scale, tiles),
        grid=(2 * tiles,),
        in_specs=[
            pl.BlockSpec(memory_space=pltpu.SMEM),
            pl.BlockSpec((frames, width), lambda i: (0, 0)),
            pl.BlockSpec((frames, wide), lambda i: (0, 0)),
            pl.BlockSpec((width, tile), lambda i: (0, i % tiles)),
            pl.BlockSpec((wide, tile), lambda i: (0, jnp.minimum(i, tiles - 1))),
            AFTER,
        ],
        out_specs=[
            pl.BlockSpec((frames, tile), lambda i: (0, jnp.maximum(i - tiles, 0))),
            pl.BlockSpec((frames, width), lambda i: (0, 0)),
        ],
        scratch_shapes=[
            big,
            big,
            pltpu.VMEM((2, frames, 128), F32),
        ],
        out_shape=[
            jax.ShapeDtypeStruct((frames, scores), BF16),
            jax.ShapeDtypeStruct((frames, width), F32),
        ],
        compiler_params=params(37, "arbitrary"),
        cost_estimate=pl.CostEstimate(
            flops=2 * frames * scores * (2 * width + wide),
            bytes_accessed=scores * (6 * width + 2 * wide),
            transcendentals=4 * frames * scores,
        ),
        name="heads",
    )(sc, hidden, teacher_in, in_hbm(head_weight), in_hbm(teacher_head_weight), after)


def head_grad_kernel(sc_ref, ha_ref, hb_ref, ga_ref, gb_ref, _, out_ref, res_s):
    half = ga_ref.shape[1] // 2
    first = sc_ref[2] == 0
    for c in range(half // 128):
        cols = [slice(x * half + c * 128, x * half + (c + 1) * 128) for x in range(2)]
        ga, gb = (jnp.concatenate([ref[:, at] for at in cols], axis=1) for ref in (ga_ref, gb_ref))
        res_s[c] = dot(ha_ref[...], ga) + dot(hb_ref[...], gb)
        for nx, nz, fz in BITS:
            for fx in range(2):
                row = ((nz * 2 + fz) * 2 + (nx ^ fx)) * 32
                rows = slice(row, row + 32)
                value = res_s[c, rows, fx * 128 : (fx + 1) * 128]
                if nx != fx:
                    value = jnp.where(first, value, res_s[c, rows, nx * 128 : (nx + 1) * 128])
                out_ref[nx, 0, nz, fz, 0, :, cols[fx]] = encode(value)


def head_grad(sc, h_mine, h_other, score_mine, score_other, after):
    rows, frames = h_mine.shape
    scores = score_mine.shape[1]
    tile = scores // 4

    def place(i, sc):
        high, low = i // 2, i % 2
        even = sc[2] == 0
        return (0, jnp.where(even, high ^ low, high), 0, 0, jnp.where(even, high, high ^ low), 0, 0)

    hidden = pl.BlockSpec((rows, frames), lambda i, sc: (0, 0))
    score = pl.BlockSpec((frames, tile), lambda i, sc: (0, i))
    return pl.pallas_call(
        head_grad_kernel,
        grid_spec=pltpu.PrefetchScalarGridSpec(
            num_scalar_prefetch=1,
            grid=(4,),
            in_specs=[hidden, hidden, score, score, AFTER],
            out_specs=pl.BlockSpec((2, 1, 2, 2, 1, 32, tile), place),
            scratch_shapes=[pltpu.VMEM((tile // 256, rows, 256), F32)],
        ),
        out_shape=jax.ShapeDtypeStruct((2, 2, 2, 2, 2, 32, tile), BF16),
        compiler_params=params(13, "arbitrary"),
        cost_estimate=pl.CostEstimate(
            flops=4 * rows * frames * scores,
            bytes_accessed=4 * frames * scores + 2 * rows * scores,
            transcendentals=0,
        ),
        name="head_grad",
    )(sc, h_mine, h_other, score_mine, score_other, in_hbm(after))


def back_kernel(sc_ref, g4_ref, h_ref, pre_ref, w_ref, send_ref, mine_ref, g_s, pad_s, tap_s, ht_s):
    step = pl.program_id(0)
    frames, width = g4_ref.shape

    @pl.when(step == 0)
    def _():
        g_s[...] = g4_ref[...]
        pad_s[...] = jnp.zeros_like(pad_s)

    g_act = frame_mask(sc_ref, frames) * g_s[...]
    pre = pre_ref[0]
    sigma = jax.nn.sigmoid(pre)
    g_pre = (g_act * sigma * (1.0 + pre * (1.0 - sigma))).astype(BF16)
    send_ref[0, :2] = g_pre.reshape(2, frames // 2, width)
    ht_s[...] = h_ref[0].T
    split_rows(sc_ref[2], ht_s, mine_ref.at[0], send_ref.at[0, 2])

    @pl.when(step < LAYERS - 1)
    def _():
        pad_s[PAD : PAD + frames] = g_pre.astype(F32)
        for at in range(LAYERS - 1, 0, -1):

            @pl.when(step == LAYERS - 1 - at)
            def _():
                reach = CLASSES * 2**at
                tap_s[0] = pad_s[PAD + reach : PAD + reach + frames].astype(BF16)
                tap_s[1] = pad_s[PAD - reach : PAD - reach + frames].astype(BF16)

        g_s[...] = (
            g_act
            + dot_nt(tap_s[0], w_ref[0, 0])
            + dot_nt(g_pre, w_ref[0, 1])
            + dot_nt(tap_s[1], w_ref[0, 2])
        )


def back(sc, g, saved, pre, weight):
    frames, width = g.shape

    def at(*block):
        return pl.BlockSpec((1, *block), lambda i: (LAYERS - 1 - i, *(0 for _ in block)))

    return pl.pallas_call(
        back_kernel,
        grid=(LAYERS,),
        in_specs=[
            pl.BlockSpec(memory_space=pltpu.SMEM),
            pl.BlockSpec((frames, width), lambda i: (0, 0)),
            at(frames, width),
            at(frames, width),
            pl.BlockSpec(
                (1, TAPS, width, width), lambda i: (jnp.maximum(LAYERS - 1 - i, 1), 0, 0, 0)
            ),
        ],
        out_specs=[at(3, frames // 2, width), at(width // 2, frames)],
        out_shape=[
            jax.ShapeDtypeStruct((LAYERS, 3, frames // 2, width), BF16),
            pltpu.HBM((LAYERS, width // 2, frames), BF16),
        ],
        scratch_shapes=[
            pltpu.VMEM((frames, width), F32),
            pltpu.VMEM((frames + 2 * PAD, width), F32),
            pltpu.VMEM((2, frames, width), BF16),
            pltpu.VMEM((width, frames), BF16),
        ],
        compiler_params=params(16, "arbitrary"),
        cost_estimate=pl.CostEstimate(
            flops=2 * (LAYERS - 1) * TAPS * frames * width * width,
            bytes_accessed=LAYERS * (TAPS * width * width * 2 + frames * width * 10),
            transcendentals=LAYERS * frames * width,
        ),
        name="back",
    )(sc, g, saved, pre, weight)


def conv_grad_kernel(sc_ref, mine_ref, send_ref, got_ref, _, *refs):
    outs, (pad_s, tap_s, res_s) = refs[:8], refs[8:]
    step = pl.program_id(0)
    rows, frames = mine_ref.shape[1:]
    width = send_ref.shape[3]

    @pl.when(step == 0)
    def _():
        pad_s[...] = jnp.zeros_like(pad_s)

    for side, ref in enumerate((send_ref, got_ref)):
        g_pre = ref[0, :2].reshape(frames, width)
        tap_s[1, side] = g_pre
        pad_s[side, PAD : PAD + frames] = g_pre.astype(F32)
    for at in range(LAYERS):

        @pl.when(step == at)
        def _():
            reach = CLASSES * 2**at
            for side in range(2):
                tap_s[0, side] = pad_s[side, PAD + reach : PAD + reach + frames].astype(BF16)
                tap_s[2, side] = pad_s[side, PAD - reach : PAD - reach + frames].astype(BF16)

    core, mx, my, mz = (sc_ref[i] for i in range(2, 6))
    side = lax.broadcasted_iota(jnp.int32, (32, 128), 1) // 64
    straight, crossed = side == mx, side != mx
    for tap in range(TAPS):
        res_s[tap] = dot(mine_ref[0], tap_s[tap, 0]) + dot(got_ref[0, 2], tap_s[tap, 1])
        for dy, dz, fz in BITS:
            for fy in range(2):
                ny, nz = my ^ dy, mz ^ dz
                high = jnp.where(core == 0, fy, ny)
                cols = pl.ds(pl.multiple_of((high * 2 + (ny ^ fy)) * 128, 128), 128)
                row = pl.multiple_of((nz * 2 + fz) * 64, 64)
                a = res_s[tap, pl.ds(row, 32), cols]
                b = pltpu.roll(res_s[tap, pl.ds(row + 32, 32), cols], 64 * core, 1)
                outs[dy * 2 + dz][tap, fz, fy] = encode(jnp.where(straight, a, b))
                outs[4 + dy * 2 + dz][tap, fz, fy] = encode(jnp.where(crossed, a, b))


def conv_grad(sc, mine, send, got, after):
    _, rows, frames = mine.shape
    width = send.shape[3]

    def at(*block):
        return pl.BlockSpec((1, *block), lambda i: (i, *(0 for _ in block)))

    out = pl.BlockSpec((TAPS, 2, 2, 32, width // 4), lambda i: (i, 0, 0, 0, 0))
    return pl.pallas_call(
        conv_grad_kernel,
        grid=(LAYERS,),
        in_specs=[
            pl.BlockSpec(memory_space=pltpu.SMEM),
            at(rows, frames),
            at(3, frames // 2, width),
            at(3, frames // 2, width),
            AFTER,
        ],
        out_specs=[out] * 8,
        out_shape=[jax.ShapeDtypeStruct((LAYERS * TAPS, 2, 2, 32, width // 4), BF16)] * 8,
        scratch_shapes=[
            pltpu.VMEM((2, frames + 2 * PAD, width), F32),
            pltpu.VMEM((TAPS, 2, frames, width), BF16),
            pltpu.VMEM((TAPS, rows, width), F32),
        ],
        compiler_params=params(18, "arbitrary"),
        cost_estimate=pl.CostEstimate(
            flops=4 * LAYERS * TAPS * rows * frames * width,
            bytes_accessed=LAYERS * (7 * rows * frames * 2 + TAPS * rows * width * 2),
            transcendentals=0,
        ),
        name="conv_grad",
    )(sc, mine, send, got, in_hbm(after))


def total_of(ref, *at):
    total = decode(ref[(0, *at)])
    for i in range(1, 8):
        total = total + decode(ref[(i, *at)])
    return total


def head_far_kernel(got_ref, out_ref):
    half = got_ref.shape[-1] // 2
    for fz, fy, fx in BITS:
        for c in range(half // 128):
            lanes = slice(fx * half + c * 128, fx * half + (c + 1) * 128)
            out_ref[fx * 4 + fy * 2 + fz, c] = encode(total_of(got_ref, fz, fy, slice(None), lanes))


def head_far(got):
    tile = got.shape[-1]
    return pl.pallas_call(
        head_far_kernel,
        out_shape=jax.ShapeDtypeStruct((8, tile // 256, 32, 128), BF16),
        in_specs=[whole()],
        out_specs=whole(),
        compiler_params=params(8),
        cost_estimate=pl.CostEstimate(
            flops=8 * got.size, bytes_accessed=3 * got.size, transcendentals=got.size
        ),
        name="head_far",
    )(in_hbm(got))


def conv_far_kernel(*refs):
    first, second, (head_ref, out_ref) = refs[:8], refs[8:16], refs[16:]
    step = pl.program_id(0)
    blocks, each = head_ref.shape[1], first[0].shape[0]
    low = low_lanes((32, 128))

    @pl.when(step == 0)
    def _():
        out_ref[:, :blocks] = head_ref[...]

    for t in range(each):
        at = blocks + step * each + t
        for fz in range(2):
            for fy in range(2):
                a = sum(decode(ref[t, fz, fy]) for ref in first)
                b = sum(decode(ref[t, fz, fy]) for ref in second)
                out_ref[fy * 2 + fz, at] = encode(jnp.where(low, a, pltpu.roll(b, 64, 1)))
                out_ref[4 + fy * 2 + fz, at] = encode(jnp.where(low, pltpu.roll(a, 64, 1), b))


def conv_far(got, head):
    half = LAYERS * TAPS // 2
    steps = 3
    block = (half // steps, 2, 2, 32, 128)
    shape = (8, head.shape[1] + half, 32, 128)
    size = 8 * got[0].size
    return pl.pallas_call(
        conv_far_kernel,
        grid=(steps,),
        out_shape=jax.ShapeDtypeStruct(shape, BF16),
        in_specs=[pl.BlockSpec(block, lambda i: (i, 0, 0, 0, 0))] * 8
        + [pl.BlockSpec(block, lambda i: (i + steps, 0, 0, 0, 0))] * 8
        + [pl.BlockSpec(head.shape, lambda i: (0, 0, 0, 0))],
        out_specs=pl.BlockSpec(shape, lambda i: (0, 0, 0, 0)),
        compiler_params=params(8, "arbitrary"),
        cost_estimate=pl.CostEstimate(
            flops=8 * size, bytes_accessed=3 * size, transcendentals=size
        ),
        name="conv_far",
    )(*got, *got, head)


def finish_kernel(got_ref, conv_ref, head_ref):
    blocks = head_ref.shape[1] // 128
    for c in range(blocks):
        head_ref[:, c * 128 : (c + 1) * 128] = total_of(got_ref, c)
    half = LAYERS * TAPS // 2
    for t in range(half):
        total = total_of(got_ref, blocks + t)
        for tap, value in ((t, total), (t + half, pltpu.roll(total, 64, 1))):
            conv_ref[tap // TAPS, tap % TAPS] = value[:, :64]


def finish(got, scores):
    return pl.pallas_call(
        finish_kernel,
        out_shape=[
            jax.ShapeDtypeStruct((LAYERS, TAPS, 32, 64), F32),
            jax.ShapeDtypeStruct((32, scores // 8), F32),
        ],
        in_specs=[whole()],
        out_specs=[whole(), whole()],
        compiler_params=params(4),
        name="finish",
    )(got)


def swap(x):
    return lax.ppermute(x, AXES, other_core())


def on_device(student_in, teacher_rows, valid, conv_weight, head_weight, teacher_head_weight):
    _, frames, width = student_in.shape
    scores = head_weight.shape[1]
    loss_scale = scores / (3.0 * math.sqrt(READ * TM * frames))
    read, tm = (lax.axis_index(axis) for axis in AXES)
    core = read % 2
    even = 1 - core
    near_bits = (
        tm % 2 ^ read // 8 * even,
        tm // 4 ^ tm // 2 % 2 * even,
        read // 4 % 2 ^ read // 2 % 2 * even,
    )
    sc = jnp.stack([valid[0], tm, core, *near_bits])
    regrouped = regroup(student_in[0]).reshape(TM, frames // TM, width)
    student = exchange(regrouped, frame_groups()).reshape(frames, width)
    teacher = regroup(teacher_rows[0]).reshape(TM, frames // TM, -1)
    teacher = exchange(teacher, frame_groups()).reshape(frames, -1)

    saved, pre, hidden, h_mine, h_other = convolve(sc, student, conv_weight)
    h_got = swap(h_other)
    score, g = heads(
        sc, hidden, teacher, head_weight, teacher_head_weight, h_got, loss_scale
    )
    score_got = swap(score)
    send, mine = back(sc, g, saved, pre, conv_weight)
    got = swap(send)
    near = head_grad(sc, h_mine, h_got, score, score_got, mine)
    head_got = exchange(near.reshape(8, 4 * 32, scores // 4), near_groups())
    parts = conv_grad(sc, mine, send, got, near)
    conv_got = [parts[0]] + [near_swap(parts[i], i) for i in range(1, 8)]

    far = head_far(head_got.reshape(8, 2, 2, 32, scores // 4))
    far = conv_far(conv_got, far)
    return tuple(finish(exchange(far, far_groups()), scores))


def solution(mesh):
    return jax.shard_map(
        on_device,
        mesh=mesh,
        in_specs=(P("read", "tm", None), P("read", "tm", None), P("read"), P(), P(), P()),
        out_specs=(P(None, None, "read", "tm"), P("read", "tm")),
        check_vma=False,
    )
```

```python
import functools
import math

import jax
import jax.numpy as jnp
from jax import lax
from jax.experimental import pallas as pl
from jax.experimental.pallas import tpu as pltpu
from jax.sharding import PartitionSpec as P

LAYERS, TAPS = 4, 3
BASE_DILATION = 32
AXES = ("read", "tm")
READ, TM = 16, 8
CLASSES = BASE_DILATION // TM
PAD = CLASSES * 2 ** (LAYERS - 1)
BITS = [(a, b, c) for a in range(2) for b in range(2) for c in range(2)]
F32, BF16 = jnp.float32, jnp.bfloat16


def near_of(core, v):
    return (v // 2) ^ (v % 2) if core == 0 else v // 2


def far_of(core, v):
    return v // 2 if core == 0 else (v // 2) ^ (v % 2)


def high_low(core, near, far):
    return (far if core == 0 else near, near ^ far)


def device_index(x, y, z, core):
    return (((x % 2) * 4 + z) * 2 + core) * TM + y * 2 + x // 2


def groups_of(fixed, order):
    groups = {}
    for core in range(2):
        for x in range(4):
            for y in range(4):
                for z in range(4):
                    key = (core, fixed(core, x), fixed(core, y), fixed(core, z))
                    place = order(core, x) * 4 + order(core, y) * 2 + order(core, z)
                    groups.setdefault(key, [0] * 8)[place] = device_index(x, y, z, core)
    return list(groups.values())


def near_groups():
    def cube(core, v):
        return (v + core) % 4 // 2

    return groups_of(cube, near_of)


def near_swap(x, bits):
    pairs = [(group[i], group[i ^ bits]) for group in near_groups() for i in range(8)]
    return lax.ppermute(x, AXES, pairs)


def far_groups():
    return groups_of(near_of, far_of)


def other_core():
    return [(d, d ^ TM) for d in range(READ * TM)]


def frame_groups():
    return [[r * TM + t for t in range(TM)] for r in range(READ)]


def exchange(x, groups):
    return lax.all_to_all(x, AXES, 0, 0, tiled=True, axis_index_groups=groups)


def encode(x):
    return (x * jnp.abs(x)).astype(BF16)


def decode(y):
    y = y.astype(F32)
    return y * lax.rsqrt(jnp.maximum(jnp.abs(y), 1e-37))


def low_lanes(shape):
    return lax.broadcasted_iota(jnp.int32, shape, len(shape) - 1) < 64


def dot(a, b):
    return jnp.dot(a, b, preferred_element_type=F32)


def dot_nt(a, b):
    return lax.dot_general(a, b, (((1,), (1,)), ((), ())), preferred_element_type=F32)


def params(mib, *kinds):
    return pltpu.CompilerParams(dimension_semantics=kinds, vmem_limit_bytes=mib * 1024 * 1024)


def whole():
    return pl.BlockSpec(memory_space=pltpu.VMEM)


def in_hbm(x):
    return pltpu.with_memory_space_constraint(x, pltpu.HBM)


AFTER = pl.BlockSpec(memory_space=pl.ANY)


def frame_mask(sc_ref, frames):
    row = lax.broadcasted_iota(jnp.int32, (frames, 1), 0)
    position = row // CLASSES * BASE_DILATION + sc_ref[1] * CLASSES + row % CLASSES
    return (position < sc_ref[0]).astype(F32)


def regroup_kernel(x_ref, out_ref, select_s):
    frames = x_ref.shape[0]

    @pl.when(pl.program_id(0) == 0)
    def _():
        row = lax.broadcasted_iota(jnp.int32, (frames, frames), 0)
        col = lax.broadcasted_iota(jnp.int32, (frames, frames), 1)
        per = frames // TM
        source = (row % per) // CLASSES * BASE_DILATION + row // per * CLASSES + row % CLASSES
        select_s[...] = jnp.where(col == source, 1.0, 0.0).astype(BF16)

    out_ref[...] = dot(select_s[...], x_ref[...]).astype(BF16)


def regroup(x):
    frames, width = x.shape
    block = pl.BlockSpec((frames, 256), lambda i: (0, i))
    return pl.pallas_call(
        regroup_kernel,
        grid=(width // 256,),
        out_shape=jax.ShapeDtypeStruct(x.shape, BF16),
        in_specs=[block],
        out_specs=block,
        scratch_shapes=[pltpu.VMEM((frames, frames), BF16)],
        compiler_params=params(5, "arbitrary"),
        name="regroup",
    )(in_hbm(x))


def split_rows(core, ht_s, mine_ref, other_ref):
    for ref, owner in ((mine_ref, core), (other_ref, 1 - core)):
        for at, (nz, fz, xl) in enumerate(BITS):
            high = jnp.where(owner == 0, fz, nz)
            row = ((xl * 4 + high * 2 + (nz ^ fz)) * 2 + owner) * 32
            ref[at * 32 : (at + 1) * 32] = ht_s[pl.ds(pl.multiple_of(row, 32), 32)]


def conv_kernel(sc_ref, x_ref, w_ref, saved_ref, pre_ref, last_ref, mine_ref, other_ref, pad_s, tap_s, ht_s):
    layer = pl.program_id(0)
    frames = x_ref.shape[0]

    @pl.when(layer == 0)
    def _():
        pad_s[...] = jnp.zeros_like(pad_s)
        pad_s[PAD : PAD + frames] = x_ref[...].astype(F32)

    for at in range(LAYERS):

        @pl.when(layer == at)
        def _():
            reach = CLASSES * 2**at
            tap_s[0] = pad_s[PAD - reach : PAD - reach + frames].astype(BF16)
            tap_s[1] = pad_s[PAD + reach : PAD + reach + frames].astype(BF16)

    hidden = pad_s[PAD : PAD + frames]
    middle = hidden.astype(BF16)
    saved_ref[0] = middle
    pre = dot(tap_s[0], w_ref[0, 0]) + dot(middle, w_ref[0, 1]) + dot(tap_s[1], w_ref[0, 2])
    pre_ref[0] = pre
    new = (frame_mask(sc_ref, frames) * (hidden + jax.nn.silu(pre))).astype(BF16)
    pad_s[PAD : PAD + frames] = new.astype(F32)

    @pl.when(layer == LAYERS - 1)
    def _():
        last_ref[...] = new
        ht_s[...] = new.T
        split_rows(sc_ref[2], ht_s, mine_ref, other_ref)


def convolve(sc, x, weight):
    frames, width = x.shape
    one = pl.BlockSpec((1, frames, width), lambda i: (i, 0, 0))
    flat = pl.BlockSpec((frames, width), lambda i: (0, 0))
    rows = pl.BlockSpec((width // 2, frames), lambda i: (0, 0))
    return pl.pallas_call(
        conv_kernel,
        grid=(LAYERS,),
        in_specs=[
            pl.BlockSpec(memory_space=pltpu.SMEM),
            flat,
            pl.BlockSpec((1, TAPS, width, width), lambda i: (i, 0, 0, 0)),
        ],
        out_specs=[one, one, flat, rows, rows],
        out_shape=[
            jax.ShapeDtypeStruct((LAYERS, frames, width), BF16),
            pltpu.HBM((LAYERS, frames, width), F32),
            pltpu.HBM((frames, width), BF16),
            pltpu.HBM((width // 2, frames), BF16),
            pltpu.HBM((width // 2, frames), BF16),
        ],
        scratch_shapes=[
            pltpu.VMEM((frames + 2 * PAD, width), F32),
            pltpu.VMEM((2, frames, width), BF16),
            pltpu.VMEM((width, frames), BF16),
        ],
        compiler_params=params(14, "arbitrary"),
        cost_estimate=pl.CostEstimate(
            flops=2 * LAYERS * TAPS * frames * width * width,
            bytes_accessed=LAYERS * (TAPS * width * width * 2 + frames * width * 6),
            transcendentals=LAYERS * frames * width,
        ),
        name="convolve",
    )(sc, x, in_hbm(weight))


def head_kernel(scale, tiles, sc_ref, h_ref, t_ref, ws_ref, wt_ref, _, score_ref, g_ref,
                sq_s, et_s, sum_s):
    step = pl.program_id(0)
    frames, width = h_ref.shape
    tile = ws_ref.shape[1]
    sub = 256

    @pl.when(step == 0)
    def _():
        sum_s[...] = jnp.zeros_like(sum_s)

    @pl.when(step < tiles)
    def _():
        for c in range(tile // sub):
            cols = slice(c * sub, (c + 1) * sub)
            squash = jnp.tanh(dot(h_ref[...], ws_ref[:, cols]))
            exp_s = jnp.exp(5.0 * squash)
            sq_s[step, :, cols] = squash
            sum_s[0] += exp_s[:, :128] + exp_s[:, 128:]
            exp_t = jnp.exp(5.0 * jnp.tanh(dot(t_ref[...], wt_ref[:, cols])))
            et_s[step, :, cols] = exp_t
            sum_s[1] += exp_t[:, :128] + exp_t[:, 128:]

    @pl.when(step == tiles)
    def _():
        factor = scale * frame_mask(sc_ref, frames)
        for i in range(2):
            inverse = factor / jnp.sum(sum_s[i], axis=1, keepdims=True)
            sum_s[i] = jnp.broadcast_to(inverse, (frames, 128))
        g_ref[...] = jnp.zeros_like(g_ref)

    @pl.when(step >= tiles)
    def _():
        at = step - tiles
        for c in range(tile // 128):
            cols = slice(c * 128, (c + 1) * 128)
            squash = sq_s[at, :, cols]
            p = jnp.exp(5.0 * squash) * sum_s[0] - et_s[at, :, cols] * sum_s[1]
            score_ref[:, cols] = (p * (1.0 - squash * squash)).astype(BF16)
        g_ref[...] += dot_nt(score_ref[...], ws_ref[...])


def heads(sc, hidden, teacher_in, head_weight, teacher_head_weight, after, loss_scale):
    frames, width = hidden.shape
    wide = teacher_in.shape[1]
    scores = head_weight.shape[1]
    tiles = 4
    tile = scores // tiles
    big = pltpu.VMEM((tiles, frames, tile), F32)
    return pl.pallas_call(
        functools.partial(head_kernel, 5.0 * loss_scale, tiles),
        grid=(2 * tiles,),
        in_specs=[
            pl.BlockSpec(memory_space=pltpu.SMEM),
            pl.BlockSpec((frames, width), lambda i: (0, 0)),
            pl.BlockSpec((frames, wide), lambda i: (0, 0)),
            pl.BlockSpec((width, tile), lambda i: (0, i % tiles)),
            pl.BlockSpec((wide, tile), lambda i: (0, jnp.minimum(i, tiles - 1))),
            AFTER,
        ],
        out_specs=[
            pl.BlockSpec((frames, tile), lambda i: (0, jnp.maximum(i - tiles, 0))),
            pl.BlockSpec((frames, width), lambda i: (0, 0)),
        ],
        scratch_shapes=[
            big,
            big,
            pltpu.VMEM((2, frames, 128), F32),
        ],
        out_shape=[
            jax.ShapeDtypeStruct((frames, scores), BF16),
            jax.ShapeDtypeStruct((frames, width), F32),
        ],
        compiler_params=params(37, "arbitrary"),
        cost_estimate=pl.CostEstimate(
            flops=2 * frames * scores * (2 * width + wide),
            bytes_accessed=scores * (6 * width + 2 * wide),
            transcendentals=4 * frames * scores,
        ),
        name="heads",
    )(sc, in_hbm(hidden), teacher_in, in_hbm(head_weight), in_hbm(teacher_head_weight), after)


def head_grad_kernel(sc_ref, ha_ref, hb_ref, ga_ref, gb_ref, _, out_ref, res_s):
    half = ga_ref.shape[1] // 2
    first = sc_ref[2] == 0
    for c in range(half // 128):
        cols = [slice(x * half + c * 128, x * half + (c + 1) * 128) for x in range(2)]
        ga, gb = (jnp.concatenate([ref[:, at] for at in cols], axis=1) for ref in (ga_ref, gb_ref))
        res_s[c] = dot(ha_ref[...], ga) + dot(hb_ref[...], gb)
        for nx, nz, fz in BITS:
            for fx in range(2):
                row = ((nz * 2 + fz) * 2 + (nx ^ fx)) * 32
                rows = slice(row, row + 32)
                value = res_s[c, rows, fx * 128 : (fx + 1) * 128]
                if nx != fx:
                    value = jnp.where(first, value, res_s[c, rows, nx * 128 : (nx + 1) * 128])
                out_ref[nx, 0, nz, fz, 0, :, cols[fx]] = encode(value)


def head_grad(sc, h_mine, h_other, score_mine, score_other, after):
    rows, frames = h_mine.shape
    scores = score_mine.shape[1]
    tile = scores // 4

    def place(i, sc):
        high, low = i // 2, i % 2
        even = sc[2] == 0
        return (0, jnp.where(even, high ^ low, high), 0, 0, jnp.where(even, high, high ^ low), 0, 0)

    hidden = pl.BlockSpec((rows, frames), lambda i, sc: (0, 0))
    score = pl.BlockSpec((frames, tile), lambda i, sc: (0, i))
    return pl.pallas_call(
        head_grad_kernel,
        grid_spec=pltpu.PrefetchScalarGridSpec(
            num_scalar_prefetch=1,
            grid=(4,),
            in_specs=[hidden, hidden, score, score, AFTER],
            out_specs=pl.BlockSpec((2, 1, 2, 2, 1, 32, tile), place),
            scratch_shapes=[pltpu.VMEM((tile // 256, rows, 256), F32)],
        ),
        out_shape=jax.ShapeDtypeStruct((2, 2, 2, 2, 2, 32, tile), BF16),
        compiler_params=params(13, "arbitrary"),
        cost_estimate=pl.CostEstimate(
            flops=4 * rows * frames * scores,
            bytes_accessed=4 * frames * scores + 2 * rows * scores,
            transcendentals=0,
        ),
        name="head_grad",
    )(sc, h_mine, h_other, score_mine, score_other, in_hbm(after))


def back_kernel(sc_ref, g4_ref, h_ref, pre_ref, w_ref, send_ref, mine_ref, g_s, pad_s, tap_s, ht_s):
    step = pl.program_id(0)
    frames, width = g4_ref.shape

    @pl.when(step == 0)
    def _():
        g_s[...] = g4_ref[...]
        pad_s[...] = jnp.zeros_like(pad_s)

    g_act = frame_mask(sc_ref, frames) * g_s[...]
    pre = pre_ref[0]
    sigma = jax.nn.sigmoid(pre)
    g_pre = (g_act * sigma * (1.0 + pre * (1.0 - sigma))).astype(BF16)
    send_ref[0, :2] = g_pre.reshape(2, frames // 2, width)
    ht_s[...] = h_ref[0].T
    split_rows(sc_ref[2], ht_s, mine_ref.at[0], send_ref.at[0, 2])

    @pl.when(step < LAYERS - 1)
    def _():
        pad_s[PAD : PAD + frames] = g_pre.astype(F32)
        for at in range(LAYERS - 1, 0, -1):

            @pl.when(step == LAYERS - 1 - at)
            def _():
                reach = CLASSES * 2**at
                tap_s[0] = pad_s[PAD + reach : PAD + reach + frames].astype(BF16)
                tap_s[1] = pad_s[PAD - reach : PAD - reach + frames].astype(BF16)

        g_s[...] = (
            g_act
            + dot_nt(tap_s[0], w_ref[0, 0])
            + dot_nt(g_pre, w_ref[0, 1])
            + dot_nt(tap_s[1], w_ref[0, 2])
        )


def back(sc, g, saved, pre, weight):
    frames, width = g.shape

    def at(*block):
        return pl.BlockSpec((1, *block), lambda i: (LAYERS - 1 - i, *(0 for _ in block)))

    return pl.pallas_call(
        back_kernel,
        grid=(LAYERS,),
        in_specs=[
            pl.BlockSpec(memory_space=pltpu.SMEM),
            pl.BlockSpec((frames, width), lambda i: (0, 0)),
            at(frames, width),
            at(frames, width),
            pl.BlockSpec(
                (1, TAPS, width, width), lambda i: (jnp.maximum(LAYERS - 1 - i, 1), 0, 0, 0)
            ),
        ],
        out_specs=[at(3, frames // 2, width), at(width // 2, frames)],
        out_shape=[
            jax.ShapeDtypeStruct((LAYERS, 3, frames // 2, width), BF16),
            pltpu.HBM((LAYERS, width // 2, frames), BF16),
        ],
        scratch_shapes=[
            pltpu.VMEM((frames, width), F32),
            pltpu.VMEM((frames + 2 * PAD, width), F32),
            pltpu.VMEM((2, frames, width), BF16),
            pltpu.VMEM((width, frames), BF16),
        ],
        compiler_params=params(16, "arbitrary"),
        cost_estimate=pl.CostEstimate(
            flops=2 * (LAYERS - 1) * TAPS * frames * width * width,
            bytes_accessed=LAYERS * (TAPS * width * width * 2 + frames * width * 10),
            transcendentals=LAYERS * frames * width,
        ),
        name="back",
    )(sc, g, saved, pre, weight)


def conv_grad_kernel(sc_ref, mine_ref, send_ref, got_ref, _, *refs):
    outs, (pad_s, tap_s, res_s) = refs[:8], refs[8:]
    step = pl.program_id(0)
    rows, frames = mine_ref.shape[1:]
    width = send_ref.shape[3]

    @pl.when(step == 0)
    def _():
        pad_s[...] = jnp.zeros_like(pad_s)

    for side, ref in enumerate((send_ref, got_ref)):
        g_pre = ref[0, :2].reshape(frames, width)
        tap_s[1, side] = g_pre
        pad_s[side, PAD : PAD + frames] = g_pre.astype(F32)
    for at in range(LAYERS):

        @pl.when(step == at)
        def _():
            reach = CLASSES * 2**at
            for side in range(2):
                tap_s[0, side] = pad_s[side, PAD + reach : PAD + reach + frames].astype(BF16)
                tap_s[2, side] = pad_s[side, PAD - reach : PAD - reach + frames].astype(BF16)

    core, mx, my, mz = (sc_ref[i] for i in range(2, 6))
    side = lax.broadcasted_iota(jnp.int32, (32, 128), 1) // 64
    straight, crossed = side == mx, side != mx
    for tap in range(TAPS):
        res_s[tap] = dot(mine_ref[0], tap_s[tap, 0]) + dot(got_ref[0, 2], tap_s[tap, 1])
        for dy, dz, fz in BITS:
            for fy in range(2):
                ny, nz = my ^ dy, mz ^ dz
                high = jnp.where(core == 0, fy, ny)
                cols = pl.ds(pl.multiple_of((high * 2 + (ny ^ fy)) * 128, 128), 128)
                row = pl.multiple_of((nz * 2 + fz) * 64, 64)
                a = res_s[tap, pl.ds(row, 32), cols]
                b = pltpu.roll(res_s[tap, pl.ds(row + 32, 32), cols], 64 * core, 1)
                outs[dy * 2 + dz][tap, fz, fy] = encode(jnp.where(straight, a, b))
                outs[4 + dy * 2 + dz][tap, fz, fy] = encode(jnp.where(crossed, a, b))


def conv_grad(sc, mine, send, got, after):
    _, rows, frames = mine.shape
    width = send.shape[3]

    def at(*block):
        return pl.BlockSpec((1, *block), lambda i: (i, *(0 for _ in block)))

    out = pl.BlockSpec((TAPS, 2, 2, 32, width // 4), lambda i: (i, 0, 0, 0, 0))
    return pl.pallas_call(
        conv_grad_kernel,
        grid=(LAYERS,),
        in_specs=[
            pl.BlockSpec(memory_space=pltpu.SMEM),
            at(rows, frames),
            at(3, frames // 2, width),
            at(3, frames // 2, width),
            AFTER,
        ],
        out_specs=[out] * 8,
        out_shape=[jax.ShapeDtypeStruct((LAYERS * TAPS, 2, 2, 32, width // 4), BF16)] * 8,
        scratch_shapes=[
            pltpu.VMEM((2, frames + 2 * PAD, width), F32),
            pltpu.VMEM((TAPS, 2, frames, width), BF16),
            pltpu.VMEM((TAPS, rows, width), F32),
        ],
        compiler_params=params(18, "arbitrary"),
        cost_estimate=pl.CostEstimate(
            flops=4 * LAYERS * TAPS * rows * frames * width,
            bytes_accessed=LAYERS * (7 * rows * frames * 2 + TAPS * rows * width * 2),
            transcendentals=0,
        ),
        name="conv_grad",
    )(sc, mine, send, got, in_hbm(after))


def total_of(ref, *at):
    total = decode(ref[(0, *at)])
    for i in range(1, 8):
        total = total + decode(ref[(i, *at)])
    return total


def head_far_kernel(got_ref, out_ref):
    half = got_ref.shape[-1] // 2
    for fz, fy, fx in BITS:
        for c in range(half // 128):
            lanes = slice(fx * half + c * 128, fx * half + (c + 1) * 128)
            out_ref[fx * 4 + fy * 2 + fz, c] = encode(total_of(got_ref, fz, fy, slice(None), lanes))


def head_far(got):
    tile = got.shape[-1]
    return pl.pallas_call(
        head_far_kernel,
        out_shape=jax.ShapeDtypeStruct((8, tile // 256, 32, 128), BF16),
        in_specs=[whole()],
        out_specs=whole(),
        compiler_params=params(8),
        cost_estimate=pl.CostEstimate(
            flops=8 * got.size, bytes_accessed=3 * got.size, transcendentals=got.size
        ),
        name="head_far",
    )(in_hbm(got))


def conv_far_kernel(*refs):
    first, second, (head_ref, out_ref) = refs[:8], refs[8:16], refs[16:]
    step = pl.program_id(0)
    blocks, each = head_ref.shape[1], first[0].shape[0]
    low = low_lanes((32, 128))

    @pl.when(step == 0)
    def _():
        out_ref[:, :blocks] = head_ref[...]

    for t in range(each):
        at = blocks + step * each + t
        for fz in range(2):
            for fy in range(2):
                a = sum(decode(ref[t, fz, fy]) for ref in first)
                b = sum(decode(ref[t, fz, fy]) for ref in second)
                out_ref[fy * 2 + fz, at] = encode(jnp.where(low, a, pltpu.roll(b, 64, 1)))
                out_ref[4 + fy * 2 + fz, at] = encode(jnp.where(low, pltpu.roll(a, 64, 1), b))


def conv_far(got, head):
    half = LAYERS * TAPS // 2
    steps = 3
    block = (half // steps, 2, 2, 32, 128)
    shape = (8, head.shape[1] + half, 32, 128)
    size = 8 * got[0].size
    return pl.pallas_call(
        conv_far_kernel,
        grid=(steps,),
        out_shape=jax.ShapeDtypeStruct(shape, BF16),
        in_specs=[pl.BlockSpec(block, lambda i: (i, 0, 0, 0, 0))] * 8
        + [pl.BlockSpec(block, lambda i: (i + steps, 0, 0, 0, 0))] * 8
        + [pl.BlockSpec(head.shape, lambda i: (0, 0, 0, 0))],
        out_specs=pl.BlockSpec(shape, lambda i: (0, 0, 0, 0)),
        compiler_params=params(8, "arbitrary"),
        cost_estimate=pl.CostEstimate(
            flops=8 * size, bytes_accessed=3 * size, transcendentals=size
        ),
        name="conv_far",
    )(*got, *got, head)


def finish_kernel(got_ref, conv_ref, head_ref):
    blocks = head_ref.shape[1] // 128
    for c in range(blocks):
        head_ref[:, c * 128 : (c + 1) * 128] = total_of(got_ref, c)
    half = LAYERS * TAPS // 2
    for t in range(half):
        total = total_of(got_ref, blocks + t)
        for tap, value in ((t, total), (t + half, pltpu.roll(total, 64, 1))):
            conv_ref[tap // TAPS, tap % TAPS] = value[:, :64]


def finish(got, scores):
    return pl.pallas_call(
        finish_kernel,
        out_shape=[
            jax.ShapeDtypeStruct((LAYERS, TAPS, 32, 64), F32),
            jax.ShapeDtypeStruct((32, scores // 8), F32),
        ],
        in_specs=[whole()],
        out_specs=[whole(), whole()],
        compiler_params=params(4),
        name="finish",
    )(got)


def swap(x):
    return lax.ppermute(x, AXES, other_core())


def on_device(student_in, teacher_rows, valid, conv_weight, head_weight, teacher_head_weight):
    _, frames, width = student_in.shape
    scores = head_weight.shape[1]
    loss_scale = scores / (3.0 * math.sqrt(READ * TM * frames))
    read, tm = (lax.axis_index(axis) for axis in AXES)
    core = read % 2
    even = 1 - core
    near_bits = (
        tm % 2 ^ read // 8 * even,
        tm // 4 ^ tm // 2 % 2 * even,
        read // 4 % 2 ^ read // 2 % 2 * even,
    )
    sc = jnp.stack([valid[0], tm, core, *near_bits])
    regrouped = regroup(student_in[0]).reshape(TM, frames // TM, width)
    student = exchange(regrouped, frame_groups()).reshape(frames, width)
    teacher = regroup(teacher_rows[0]).reshape(TM, frames // TM, -1)
    teacher = exchange(teacher, frame_groups()).reshape(frames, -1)

    saved, pre, hidden, h_mine, h_other = convolve(sc, student, conv_weight)
    h_got = swap(h_other)
    score, g = heads(
        sc, hidden, teacher, head_weight, teacher_head_weight, h_got, loss_scale
    )
    score_got = swap(score)
    send, mine = back(sc, g, saved, pre, conv_weight)
    got = swap(send)
    near = head_grad(sc, h_mine, h_got, score, score_got, mine)
    head_got = exchange(near.reshape(8, 4 * 32, scores // 4), near_groups())
    parts = conv_grad(sc, mine, send, got, near)
    conv_got = [parts[0]] + [near_swap(parts[i], i) for i in (7, 3, 5, 6, 1, 2, 4)]

    far = head_far(head_got.reshape(8, 2, 2, 32, scores // 4))
    far = conv_far(conv_got, far)
    return tuple(finish(exchange(far, far_groups()), scores))


def solution(mesh):
    return jax.shard_map(
        on_device,
        mesh=mesh,
        in_specs=(P("read", "tm", None), P("read", "tm", None), P("read"), P(), P(), P()),
        out_specs=(P(None, None, "read", "tm"), P("read", "tm")),
        check_vma=False,
    )
```

```python
import functools
import math

import jax
import jax.numpy as jnp
from jax import lax
from jax.experimental import pallas as pl
from jax.experimental.pallas import tpu as pltpu
from jax.sharding import PartitionSpec as P

LAYERS, TAPS = 4, 3
BASE_DILATION = 32
AXES = ("read", "tm")
READ, TM = 16, 8
CLASSES = BASE_DILATION // TM
PAD = CLASSES * 2 ** (LAYERS - 1)
BITS = [(a, b, c) for a in range(2) for b in range(2) for c in range(2)]
F32, BF16 = jnp.float32, jnp.bfloat16


def near_of(core, v):
    return (v // 2) ^ (v % 2) if core == 0 else v // 2


def far_of(core, v):
    return v // 2 if core == 0 else (v // 2) ^ (v % 2)


def high_low(core, near, far):
    return (far if core == 0 else near, near ^ far)


def device_index(x, y, z, core):
    return (((x % 2) * 4 + z) * 2 + core) * TM + y * 2 + x // 2


def groups_of(fixed, order):
    groups = {}
    for core in range(2):
        for x in range(4):
            for y in range(4):
                for z in range(4):
                    key = (core, fixed(core, x), fixed(core, y), fixed(core, z))
                    place = order(core, x) * 4 + order(core, y) * 2 + order(core, z)
                    groups.setdefault(key, [0] * 8)[place] = device_index(x, y, z, core)
    return list(groups.values())


def near_groups():
    def cube(core, v):
        return (v + core) % 4 // 2

    return groups_of(cube, near_of)


def near_swap(x, bits):
    pairs = [(group[i], group[i ^ bits]) for group in near_groups() for i in range(8)]
    return lax.ppermute(x, AXES, pairs)


def far_groups():
    return groups_of(near_of, far_of)


def other_core():
    return [(d, d ^ TM) for d in range(READ * TM)]


def frame_groups():
    return [[r * TM + t for t in range(TM)] for r in range(READ)]


def exchange(x, groups):
    return lax.all_to_all(x, AXES, 0, 0, tiled=True, axis_index_groups=groups)


def encode(x):
    return (x * jnp.abs(x)).astype(BF16)


def decode(y):
    y = y.astype(F32)
    return y * lax.rsqrt(jnp.maximum(jnp.abs(y), 1e-37))


def low_lanes(shape):
    return lax.broadcasted_iota(jnp.int32, shape, len(shape) - 1) < 64


def dot(a, b):
    return jnp.dot(a, b, preferred_element_type=F32)


def dot_nt(a, b):
    return lax.dot_general(a, b, (((1,), (1,)), ((), ())), preferred_element_type=F32)


def params(mib, *kinds):
    return pltpu.CompilerParams(dimension_semantics=kinds, vmem_limit_bytes=mib * 1024 * 1024)


def whole():
    return pl.BlockSpec(memory_space=pltpu.VMEM)


def in_hbm(x):
    return pltpu.with_memory_space_constraint(x, pltpu.HBM)


AFTER = pl.BlockSpec(memory_space=pl.ANY)


def frame_mask(sc_ref, frames):
    row = lax.broadcasted_iota(jnp.int32, (frames, 1), 0)
    position = row // CLASSES * BASE_DILATION + sc_ref[1] * CLASSES + row % CLASSES
    return (position < sc_ref[0]).astype(F32)


def regroup_kernel(x_ref, out_ref):
    frames = x_ref.shape[0]
    row = lax.broadcasted_iota(jnp.int32, (frames, frames), 0)
    col = lax.broadcasted_iota(jnp.int32, (frames, frames), 1)
    per = frames // TM
    source = (row % per) // CLASSES * BASE_DILATION + row // per * CLASSES + row % CLASSES
    select = jnp.where(col == source, 1.0, 0.0).astype(BF16)
    out_ref[...] = dot(select, x_ref[...]).astype(BF16)


def regroup(x):
    return pl.pallas_call(
        regroup_kernel,
        out_shape=jax.ShapeDtypeStruct(x.shape, BF16),
        in_specs=[whole()],
        out_specs=whole(),
        compiler_params=params(5),
        name="regroup",
    )(x)


def split_rows(core, ht_s, mine_ref, other_ref):
    for ref, owner in ((mine_ref, core), (other_ref, 1 - core)):
        for at, (nz, fz, xl) in enumerate(BITS):
            high = jnp.where(owner == 0, fz, nz)
            row = ((xl * 4 + high * 2 + (nz ^ fz)) * 2 + owner) * 32
            ref[at * 32 : (at + 1) * 32] = ht_s[pl.ds(pl.multiple_of(row, 32), 32)]


def conv_kernel(sc_ref, x_ref, w_ref, saved_ref, pre_ref, last_ref, mine_ref, other_ref, pad_s, tap_s, ht_s):
    layer = pl.program_id(0)
    frames = x_ref.shape[0]

    @pl.when(layer == 0)
    def _():
        pad_s[...] = jnp.zeros_like(pad_s)
        pad_s[PAD : PAD + frames] = x_ref[...].astype(F32)

    for at in range(LAYERS):

        @pl.when(layer == at)
        def _():
            reach = CLASSES * 2**at
            tap_s[0] = pad_s[PAD - reach : PAD - reach + frames].astype(BF16)
            tap_s[1] = pad_s[PAD + reach : PAD + reach + frames].astype(BF16)

    hidden = pad_s[PAD : PAD + frames]
    middle = hidden.astype(BF16)
    saved_ref[0] = middle
    pre = dot(tap_s[0], w_ref[0, 0]) + dot(middle, w_ref[0, 1]) + dot(tap_s[1], w_ref[0, 2])
    pre_ref[0] = pre
    new = (frame_mask(sc_ref, frames) * (hidden + jax.nn.silu(pre))).astype(BF16)
    pad_s[PAD : PAD + frames] = new.astype(F32)

    @pl.when(layer == LAYERS - 1)
    def _():
        last_ref[...] = new
        ht_s[...] = new.T
        split_rows(sc_ref[2], ht_s, mine_ref, other_ref)


def convolve(sc, x, weight):
    frames, width = x.shape
    one = pl.BlockSpec((1, frames, width), lambda i: (i, 0, 0))
    flat = pl.BlockSpec((frames, width), lambda i: (0, 0))
    rows = pl.BlockSpec((width // 2, frames), lambda i: (0, 0))
    return pl.pallas_call(
        conv_kernel,
        grid=(LAYERS,),
        in_specs=[
            pl.BlockSpec(memory_space=pltpu.SMEM),
            flat,
            pl.BlockSpec((1, TAPS, width, width), lambda i: (i, 0, 0, 0)),
        ],
        out_specs=[one, one, flat, rows, rows],
        out_shape=[
            jax.ShapeDtypeStruct((LAYERS, frames, width), BF16),
            pltpu.HBM((LAYERS, frames, width), F32),
            pltpu.HBM((frames, width), BF16),
            pltpu.HBM((width // 2, frames), BF16),
            pltpu.HBM((width // 2, frames), BF16),
        ],
        scratch_shapes=[
            pltpu.VMEM((frames + 2 * PAD, width), F32),
            pltpu.VMEM((2, frames, width), BF16),
            pltpu.VMEM((width, frames), BF16),
        ],
        compiler_params=params(14, "arbitrary"),
        cost_estimate=pl.CostEstimate(
            flops=2 * LAYERS * TAPS * frames * width * width,
            bytes_accessed=LAYERS * (TAPS * width * width * 2 + frames * width * 6),
            transcendentals=LAYERS * frames * width,
        ),
        name="convolve",
    )(sc, x, in_hbm(weight))


def head_kernel(scale, tiles, sc_ref, h_ref, t_ref, ws_ref, wt_ref, _, score_ref, g_ref,
                sq_s, et_s, sum_s):
    step = pl.program_id(0)
    frames, width = h_ref.shape
    tile = ws_ref.shape[1]
    sub = 256

    @pl.when(step == 0)
    def _():
        sum_s[...] = jnp.zeros_like(sum_s)

    @pl.when(step < tiles)
    def _():
        for c in range(tile // sub):
            cols = slice(c * sub, (c + 1) * sub)
            squash = jnp.tanh(dot(h_ref[...], ws_ref[:, cols]))
            exp_s = jnp.exp(5.0 * squash)
            sq_s[step, :, cols] = squash
            sum_s[0] += exp_s[:, :128] + exp_s[:, 128:]
            exp_t = jnp.exp(5.0 * jnp.tanh(dot(t_ref[...], wt_ref[:, cols])))
            et_s[step, :, cols] = exp_t
            sum_s[1] += exp_t[:, :128] + exp_t[:, 128:]

    @pl.when(step == tiles)
    def _():
        factor = scale * frame_mask(sc_ref, frames)
        for i in range(2):
            inverse = factor / jnp.sum(sum_s[i], axis=1, keepdims=True)
            sum_s[i] = jnp.broadcast_to(inverse, (frames, 128))
        g_ref[...] = jnp.zeros_like(g_ref)

    @pl.when(step >= tiles)
    def _():
        at = step - tiles
        for c in range(tile // 128):
            cols = slice(c * 128, (c + 1) * 128)
            squash = sq_s[at, :, cols]
            p = jnp.exp(5.0 * squash) * sum_s[0] - et_s[at, :, cols] * sum_s[1]
            score_ref[:, cols] = (p * (1.0 - squash * squash)).astype(BF16)
        g_ref[...] += dot_nt(score_ref[...], ws_ref[...])


def heads(sc, hidden, teacher_in, head_weight, teacher_head_weight, after, loss_scale):
    frames, width = hidden.shape
    wide = teacher_in.shape[1]
    scores = head_weight.shape[1]
    tiles = 4
    tile = scores // tiles
    big = pltpu.VMEM((tiles, frames, tile), F32)
    return pl.pallas_call(
        functools.partial(head_kernel, 5.0 * loss_scale, tiles),
        grid=(2 * tiles,),
        in_specs=[
            pl.BlockSpec(memory_space=pltpu.SMEM),
            pl.BlockSpec((frames, width), lambda i: (0, 0)),
            pl.BlockSpec((frames, wide), lambda i: (0, 0)),
            pl.BlockSpec((width, tile), lambda i: (0, i % tiles)),
            pl.BlockSpec((wide, tile), lambda i: (0, jnp.minimum(i, tiles - 1))),
            AFTER,
        ],
        out_specs=[
            pl.BlockSpec((frames, tile), lambda i: (0, jnp.maximum(i - tiles, 0))),
            pl.BlockSpec((frames, width), lambda i: (0, 0)),
        ],
        scratch_shapes=[
            big,
            big,
            pltpu.VMEM((2, frames, 128), F32),
        ],
        out_shape=[
            jax.ShapeDtypeStruct((frames, scores), BF16),
            jax.ShapeDtypeStruct((frames, width), F32),
        ],
        compiler_params=params(37, "arbitrary"),
        cost_estimate=pl.CostEstimate(
            flops=2 * frames * scores * (2 * width + wide),
            bytes_accessed=scores * (6 * width + 2 * wide),
            transcendentals=4 * frames * scores,
        ),
        name="heads",
    )(sc, in_hbm(hidden), teacher_in, in_hbm(head_weight), in_hbm(teacher_head_weight), after)


def head_grad_kernel(sc_ref, ha_ref, hb_ref, ga_ref, gb_ref, _, out_ref, res_s):
    half = ga_ref.shape[1] // 2
    first = sc_ref[2] == 0
    for c in range(half // 128):
        cols = [slice(x * half + c * 128, x * half + (c + 1) * 128) for x in range(2)]
        ga, gb = (jnp.concatenate([ref[:, at] for at in cols], axis=1) for ref in (ga_ref, gb_ref))
        res_s[c] = dot(ha_ref[...], ga) + dot(hb_ref[...], gb)
        for nx, nz, fz in BITS:
            for fx in range(2):
                row = ((nz * 2 + fz) * 2 + (nx ^ fx)) * 32
                rows = slice(row, row + 32)
                value = res_s[c, rows, fx * 128 : (fx + 1) * 128]
                if nx != fx:
                    value = jnp.where(first, value, res_s[c, rows, nx * 128 : (nx + 1) * 128])
                out_ref[nx, 0, nz, fz, 0, :, cols[fx]] = encode(value)


def head_grad(sc, h_mine, h_other, score_mine, score_other, after):
    rows, frames = h_mine.shape
    scores = score_mine.shape[1]
    tile = scores // 4

    def place(i, sc):
        high, low = i // 2, i % 2
        even = sc[2] == 0
        return (0, jnp.where(even, high ^ low, high), 0, 0, jnp.where(even, high, high ^ low), 0, 0)

    hidden = pl.BlockSpec((rows, frames), lambda i, sc: (0, 0))
    score = pl.BlockSpec((frames, tile), lambda i, sc: (0, i))
    return pl.pallas_call(
        head_grad_kernel,
        grid_spec=pltpu.PrefetchScalarGridSpec(
            num_scalar_prefetch=1,
            grid=(4,),
            in_specs=[hidden, hidden, score, score, AFTER],
            out_specs=pl.BlockSpec((2, 1, 2, 2, 1, 32, tile), place),
            scratch_shapes=[pltpu.VMEM((tile // 256, rows, 256), F32)],
        ),
        out_shape=jax.ShapeDtypeStruct((2, 2, 2, 2, 2, 32, tile), BF16),
        compiler_params=params(13, "arbitrary"),
        cost_estimate=pl.CostEstimate(
            flops=4 * rows * frames * scores,
            bytes_accessed=4 * frames * scores + 2 * rows * scores,
            transcendentals=0,
        ),
        name="head_grad",
    )(sc, h_mine, h_other, score_mine, score_other, in_hbm(after))


def back_kernel(sc_ref, g4_ref, h_ref, pre_ref, w_ref, send_ref, mine_ref, g_s, pad_s, tap_s, ht_s):
    step = pl.program_id(0)
    frames, width = g4_ref.shape

    @pl.when(step == 0)
    def _():
        g_s[...] = g4_ref[...]
        pad_s[...] = jnp.zeros_like(pad_s)

    g_act = frame_mask(sc_ref, frames) * g_s[...]
    pre = pre_ref[0]
    sigma = jax.nn.sigmoid(pre)
    g_pre = (g_act * sigma * (1.0 + pre * (1.0 - sigma))).astype(BF16)
    send_ref[0, :2] = g_pre.reshape(2, frames // 2, width)
    ht_s[...] = h_ref[0].T
    split_rows(sc_ref[2], ht_s, mine_ref.at[0], send_ref.at[0, 2])

    @pl.when(step < LAYERS - 1)
    def _():
        pad_s[PAD : PAD + frames] = g_pre.astype(F32)
        for at in range(LAYERS - 1, 0, -1):

            @pl.when(step == LAYERS - 1 - at)
            def _():
                reach = CLASSES * 2**at
                tap_s[0] = pad_s[PAD + reach : PAD + reach + frames].astype(BF16)
                tap_s[1] = pad_s[PAD - reach : PAD - reach + frames].astype(BF16)

        g_s[...] = (
            g_act
            + dot_nt(tap_s[0], w_ref[0, 0])
            + dot_nt(g_pre, w_ref[0, 1])
            + dot_nt(tap_s[1], w_ref[0, 2])
        )


def back(sc, g, saved, pre, weight):
    frames, width = g.shape

    def at(*block):
        return pl.BlockSpec((1, *block), lambda i: (LAYERS - 1 - i, *(0 for _ in block)))

    return pl.pallas_call(
        back_kernel,
        grid=(LAYERS,),
        in_specs=[
            pl.BlockSpec(memory_space=pltpu.SMEM),
            pl.BlockSpec((frames, width), lambda i: (0, 0)),
            at(frames, width),
            at(frames, width),
            pl.BlockSpec(
                (1, TAPS, width, width), lambda i: (jnp.maximum(LAYERS - 1 - i, 1), 0, 0, 0)
            ),
        ],
        out_specs=[at(3, frames // 2, width), at(width // 2, frames)],
        out_shape=[
            jax.ShapeDtypeStruct((LAYERS, 3, frames // 2, width), BF16),
            pltpu.HBM((LAYERS, width // 2, frames), BF16),
        ],
        scratch_shapes=[
            pltpu.VMEM((frames, width), F32),
            pltpu.VMEM((frames + 2 * PAD, width), F32),
            pltpu.VMEM((2, frames, width), BF16),
            pltpu.VMEM((width, frames), BF16),
        ],
        compiler_params=params(16, "arbitrary"),
        cost_estimate=pl.CostEstimate(
            flops=2 * (LAYERS - 1) * TAPS * frames * width * width,
            bytes_accessed=LAYERS * (TAPS * width * width * 2 + frames * width * 10),
            transcendentals=LAYERS * frames * width,
        ),
        name="back",
    )(sc, g, saved, pre, weight)


def conv_grad_kernel(sc_ref, mine_ref, send_ref, got_ref, _, *refs):
    outs, (pad_s, tap_s, res_s) = refs[:8], refs[8:]
    step = pl.program_id(0)
    rows, frames = mine_ref.shape[1:]
    width = send_ref.shape[3]

    @pl.when(step == 0)
    def _():
        pad_s[...] = jnp.zeros_like(pad_s)

    for side, ref in enumerate((send_ref, got_ref)):
        g_pre = ref[0, :2].reshape(frames, width)
        tap_s[1, side] = g_pre
        pad_s[side, PAD : PAD + frames] = g_pre.astype(F32)
    for at in range(LAYERS):

        @pl.when(step == at)
        def _():
            reach = CLASSES * 2**at
            for side in range(2):
                tap_s[0, side] = pad_s[side, PAD + reach : PAD + reach + frames].astype(BF16)
                tap_s[2, side] = pad_s[side, PAD - reach : PAD - reach + frames].astype(BF16)

    core, mx, my, mz = (sc_ref[i] for i in range(2, 6))
    side = lax.broadcasted_iota(jnp.int32, (32, 128), 1) // 64
    straight, crossed = side == mx, side != mx
    for tap in range(TAPS):
        res_s[tap] = dot(mine_ref[0], tap_s[tap, 0]) + dot(got_ref[0, 2], tap_s[tap, 1])
        for dy, dz, fz in BITS:
            for fy in range(2):
                ny, nz = my ^ dy, mz ^ dz
                high = jnp.where(core == 0, fy, ny)
                cols = pl.ds(pl.multiple_of((high * 2 + (ny ^ fy)) * 128, 128), 128)
                row = pl.multiple_of((nz * 2 + fz) * 64, 64)
                a = res_s[tap, pl.ds(row, 32), cols]
                b = pltpu.roll(res_s[tap, pl.ds(row + 32, 32), cols], 64 * core, 1)
                outs[dy * 2 + dz][tap, fz, fy] = encode(jnp.where(straight, a, b))
                outs[4 + dy * 2 + dz][tap, fz, fy] = encode(jnp.where(crossed, a, b))


def conv_grad(sc, mine, send, got, after):
    _, rows, frames = mine.shape
    width = send.shape[3]

    def at(*block):
        return pl.BlockSpec((1, *block), lambda i: (i, *(0 for _ in block)))

    out = pl.BlockSpec((TAPS, 2, 2, 32, width // 4), lambda i: (i, 0, 0, 0, 0))
    return pl.pallas_call(
        conv_grad_kernel,
        grid=(LAYERS,),
        in_specs=[
            pl.BlockSpec(memory_space=pltpu.SMEM),
            at(rows, frames),
            at(3, frames // 2, width),
            at(3, frames // 2, width),
            AFTER,
        ],
        out_specs=[out] * 8,
        out_shape=[jax.ShapeDtypeStruct((LAYERS * TAPS, 2, 2, 32, width // 4), BF16)] * 8,
        scratch_shapes=[
            pltpu.VMEM((2, frames + 2 * PAD, width), F32),
            pltpu.VMEM((TAPS, 2, frames, width), BF16),
            pltpu.VMEM((TAPS, rows, width), F32),
        ],
        compiler_params=params(18, "arbitrary"),
        cost_estimate=pl.CostEstimate(
            flops=4 * LAYERS * TAPS * rows * frames * width,
            bytes_accessed=LAYERS * (7 * rows * frames * 2 + TAPS * rows * width * 2),
            transcendentals=0,
        ),
        name="conv_grad",
    )(sc, mine, send, got, in_hbm(after))


def total_of(ref, *at):
    total = decode(ref[(0, *at)])
    for i in range(1, 8):
        total = total + decode(ref[(i, *at)])
    return total


def head_far_kernel(got_ref, out_ref):
    half = got_ref.shape[-1] // 2
    for fz, fy, fx in BITS:
        for c in range(half // 128):
            lanes = slice(fx * half + c * 128, fx * half + (c + 1) * 128)
            out_ref[fx * 4 + fy * 2 + fz, c] = encode(total_of(got_ref, fz, fy, slice(None), lanes))


def head_far(got):
    tile = got.shape[-1]
    return pl.pallas_call(
        head_far_kernel,
        out_shape=jax.ShapeDtypeStruct((8, tile // 256, 32, 128), BF16),
        in_specs=[whole()],
        out_specs=whole(),
        compiler_params=params(8),
        cost_estimate=pl.CostEstimate(
            flops=8 * got.size, bytes_accessed=3 * got.size, transcendentals=got.size
        ),
        name="head_far",
    )(in_hbm(got))


def conv_far_kernel(*refs):
    first, second, (head_ref, out_ref) = refs[:8], refs[8:16], refs[16:]
    step = pl.program_id(0)
    blocks, each = head_ref.shape[1], first[0].shape[0]
    low = low_lanes((32, 128))

    @pl.when(step == 0)
    def _():
        out_ref[:, :blocks] = head_ref[...]

    for t in range(each):
        at = blocks + step * each + t
        for fz in range(2):
            for fy in range(2):
                a = sum(decode(ref[t, fz, fy]) for ref in first)
                b = sum(decode(ref[t, fz, fy]) for ref in second)
                out_ref[fy * 2 + fz, at] = encode(jnp.where(low, a, pltpu.roll(b, 64, 1)))
                out_ref[4 + fy * 2 + fz, at] = encode(jnp.where(low, pltpu.roll(a, 64, 1), b))


def conv_far(got, head):
    half = LAYERS * TAPS // 2
    steps = 3
    block = (half // steps, 2, 2, 32, 128)
    shape = (8, head.shape[1] + half, 32, 128)
    size = 8 * got[0].size
    return pl.pallas_call(
        conv_far_kernel,
        grid=(steps,),
        out_shape=jax.ShapeDtypeStruct(shape, BF16),
        in_specs=[pl.BlockSpec(block, lambda i: (i, 0, 0, 0, 0))] * 8
        + [pl.BlockSpec(block, lambda i: (i + steps, 0, 0, 0, 0))] * 8
        + [pl.BlockSpec(head.shape, lambda i: (0, 0, 0, 0))],
        out_specs=pl.BlockSpec(shape, lambda i: (0, 0, 0, 0)),
        compiler_params=params(8, "arbitrary"),
        cost_estimate=pl.CostEstimate(
            flops=8 * size, bytes_accessed=3 * size, transcendentals=size
        ),
        name="conv_far",
    )(*got, *got, head)


def finish_kernel(got_ref, conv_ref, head_ref):
    blocks = head_ref.shape[1] // 128
    for c in range(blocks):
        head_ref[:, c * 128 : (c + 1) * 128] = total_of(got_ref, c)
    half = LAYERS * TAPS // 2
    for t in range(half):
        total = total_of(got_ref, blocks + t)
        for tap, value in ((t, total), (t + half, pltpu.roll(total, 64, 1))):
            conv_ref[tap // TAPS, tap % TAPS] = value[:, :64]


def finish(got, scores):
    return pl.pallas_call(
        finish_kernel,
        out_shape=[
            jax.ShapeDtypeStruct((LAYERS, TAPS, 32, 64), F32),
            jax.ShapeDtypeStruct((32, scores // 8), F32),
        ],
        in_specs=[whole()],
        out_specs=[whole(), whole()],
        compiler_params=params(4),
        name="finish",
    )(got)


def swap(x):
    return lax.ppermute(x, AXES, other_core())


def on_device(student_in, teacher_rows, valid, conv_weight, head_weight, teacher_head_weight):
    _, frames, width = student_in.shape
    scores = head_weight.shape[1]
    loss_scale = scores / (3.0 * math.sqrt(READ * TM * frames))
    read, tm = (lax.axis_index(axis) for axis in AXES)
    core = read % 2
    even = 1 - core
    near_bits = (
        tm % 2 ^ read // 8 * even,
        tm // 4 ^ tm // 2 % 2 * even,
        read // 4 % 2 ^ read // 2 % 2 * even,
    )
    sc = jnp.stack([valid[0], tm, core, *near_bits])
    regrouped = regroup(student_in[0]).reshape(TM, frames // TM, width)
    student = exchange(regrouped, frame_groups()).reshape(frames, width)
    teacher = regroup(teacher_rows[0]).reshape(TM, frames // TM, -1)
    teacher = exchange(teacher, frame_groups()).reshape(frames, -1)

    saved, pre, hidden, h_mine, h_other = convolve(sc, student, conv_weight)
    h_got = swap(h_other)
    score, g = heads(
        sc, hidden, teacher, head_weight, teacher_head_weight, h_got, loss_scale
    )
    score_got = swap(score)
    send, mine = back(sc, g, saved, pre, conv_weight)
    got = swap(send)
    near = head_grad(sc, h_mine, h_got, score, score_got, mine)
    head_got = exchange(near.reshape(8, 4 * 32, scores // 4), near_groups())
    parts = conv_grad(sc, mine, send, got, near)
    conv_got = [parts[0]] + [near_swap(parts[i], i) for i in range(1, 8)]

    far = head_far(head_got.reshape(8, 2, 2, 32, scores // 4))
    far = conv_far(conv_got, far)
    return tuple(finish(exchange(far, far_groups()), scores))


def solution(mesh):
    return jax.shard_map(
        on_device,
        mesh=mesh,
        in_specs=(P("read", "tm", None), P("read", "tm", None), P("read"), P(), P(), P()),
        out_specs=(P(None, None, "read", "tm"), P("read", "tm")),
        check_vma=False,
    )
```

```python
import functools
import math

import jax
import jax.numpy as jnp
from jax import lax
from jax.experimental import pallas as pl
from jax.experimental.pallas import tpu as pltpu
from jax.sharding import PartitionSpec as P

LAYERS, TAPS = 4, 3
BASE_DILATION = 32
AXES = ("read", "tm")
READ, TM = 16, 8
CLASSES = BASE_DILATION // TM
PAD = CLASSES * 2 ** (LAYERS - 1)
BITS = [(a, b, c) for a in range(2) for b in range(2) for c in range(2)]
F32, BF16 = jnp.float32, jnp.bfloat16


def near_of(core, v):
    return (v // 2) ^ (v % 2) if core == 0 else v // 2


def far_of(core, v):
    return v // 2 if core == 0 else (v // 2) ^ (v % 2)


def high_low(core, near, far):
    return (far if core == 0 else near, near ^ far)


def device_index(x, y, z, core):
    return (((x % 2) * 4 + z) * 2 + core) * TM + y * 2 + x // 2


def groups_of(fixed, order):
    groups = {}
    for core in range(2):
        for x in range(4):
            for y in range(4):
                for z in range(4):
                    key = (core, fixed(core, x), fixed(core, y), fixed(core, z))
                    place = order(core, x) * 4 + order(core, y) * 2 + order(core, z)
                    groups.setdefault(key, [0] * 8)[place] = device_index(x, y, z, core)
    return list(groups.values())


def near_groups():
    def cube(core, v):
        return (v + core) % 4 // 2

    return groups_of(cube, near_of)


def near_swap(x, bits):
    pairs = [(group[i], group[i ^ bits]) for group in near_groups() for i in range(8)]
    return lax.ppermute(x, AXES, pairs)


def far_groups():
    return groups_of(near_of, far_of)


def other_core():
    return [(d, d ^ TM) for d in range(READ * TM)]


def frame_groups():
    return [[r * TM + t for t in range(TM)] for r in range(READ)]


def exchange(x, groups):
    return lax.all_to_all(x, AXES, 0, 0, tiled=True, axis_index_groups=groups)


def encode(x):
    return (x * jnp.abs(x)).astype(BF16)


def decode(y):
    y = y.astype(F32)
    return y * lax.rsqrt(jnp.maximum(jnp.abs(y), 1e-37))


def low_lanes(shape):
    return lax.broadcasted_iota(jnp.int32, shape, len(shape) - 1) < 64


def dot(a, b):
    return jnp.dot(a, b, preferred_element_type=F32)


def dot_nt(a, b):
    return lax.dot_general(a, b, (((1,), (1,)), ((), ())), preferred_element_type=F32)


def params(mib, *kinds):
    return pltpu.CompilerParams(dimension_semantics=kinds, vmem_limit_bytes=mib * 1024 * 1024)


def whole():
    return pl.BlockSpec(memory_space=pltpu.VMEM)


def in_hbm(x):
    return pltpu.with_memory_space_constraint(x, pltpu.HBM)


AFTER = pl.BlockSpec(memory_space=pl.ANY)


def frame_mask(sc_ref, frames):
    row = lax.broadcasted_iota(jnp.int32, (frames, 1), 0)
    position = row // CLASSES * BASE_DILATION + sc_ref[1] * CLASSES + row % CLASSES
    return (position < sc_ref[0]).astype(F32)


def regroup_kernel(x_ref, out_ref):
    frames = x_ref.shape[0]
    row = lax.broadcasted_iota(jnp.int32, (frames, frames), 0)
    col = lax.broadcasted_iota(jnp.int32, (frames, frames), 1)
    per = frames // TM
    source = (row % per) // CLASSES * BASE_DILATION + row // per * CLASSES + row % CLASSES
    select = jnp.where(col == source, 1.0, 0.0).astype(BF16)
    out_ref[...] = dot(select, x_ref[...]).astype(BF16)


def regroup(x):
    return pl.pallas_call(
        regroup_kernel,
        out_shape=jax.ShapeDtypeStruct(x.shape, BF16),
        in_specs=[whole()],
        out_specs=whole(),
        compiler_params=params(5),
        name="regroup",
    )(x)


def split_rows(core, ht_s, mine_ref, other_ref):
    for ref, owner in ((mine_ref, core), (other_ref, 1 - core)):
        for at, (nz, fz, xl) in enumerate(BITS):
            high = jnp.where(owner == 0, fz, nz)
            row = ((xl * 4 + high * 2 + (nz ^ fz)) * 2 + owner) * 32
            ref[at * 32 : (at + 1) * 32] = ht_s[pl.ds(pl.multiple_of(row, 32), 32)]


def conv_kernel(sc_ref, x_ref, w_ref, saved_ref, pre_ref, last_ref, mine_ref, other_ref, pad_s, tap_s, ht_s):
    layer = pl.program_id(0)
    frames = x_ref.shape[0]

    @pl.when(layer == 0)
    def _():
        pad_s[...] = jnp.zeros_like(pad_s)
        pad_s[PAD : PAD + frames] = x_ref[...].astype(F32)

    for at in range(LAYERS):

        @pl.when(layer == at)
        def _():
            reach = CLASSES * 2**at
            tap_s[0] = pad_s[PAD - reach : PAD - reach + frames].astype(BF16)
            tap_s[1] = pad_s[PAD + reach : PAD + reach + frames].astype(BF16)

    hidden = pad_s[PAD : PAD + frames]
    middle = hidden.astype(BF16)
    saved_ref[0] = middle
    pre = dot(tap_s[0], w_ref[0, 0]) + dot(middle, w_ref[0, 1]) + dot(tap_s[1], w_ref[0, 2])
    pre_ref[0] = pre
    new = (frame_mask(sc_ref, frames) * (hidden + jax.nn.silu(pre))).astype(BF16)
    pad_s[PAD : PAD + frames] = new.astype(F32)

    @pl.when(layer == LAYERS - 1)
    def _():
        last_ref[...] = new
        ht_s[...] = new.T
        split_rows(sc_ref[2], ht_s, mine_ref, other_ref)


def convolve(sc, x, weight):
    frames, width = x.shape
    one = pl.BlockSpec((1, frames, width), lambda i: (i, 0, 0))
    flat = pl.BlockSpec((frames, width), lambda i: (0, 0))
    rows = pl.BlockSpec((width // 2, frames), lambda i: (0, 0))
    return pl.pallas_call(
        conv_kernel,
        grid=(LAYERS,),
        in_specs=[
            pl.BlockSpec(memory_space=pltpu.SMEM),
            flat,
            pl.BlockSpec((1, TAPS, width, width), lambda i: (i, 0, 0, 0)),
        ],
        out_specs=[one, one, flat, rows, rows],
        out_shape=[
            jax.ShapeDtypeStruct((LAYERS, frames, width), BF16),
            pltpu.HBM((LAYERS, frames, width), F32),
            pltpu.HBM((frames, width), BF16),
            pltpu.HBM((width // 2, frames), BF16),
            pltpu.HBM((width // 2, frames), BF16),
        ],
        scratch_shapes=[
            pltpu.VMEM((frames + 2 * PAD, width), F32),
            pltpu.VMEM((2, frames, width), BF16),
            pltpu.VMEM((width, frames), BF16),
        ],
        compiler_params=params(14, "arbitrary"),
        cost_estimate=pl.CostEstimate(
            flops=2 * LAYERS * TAPS * frames * width * width,
            bytes_accessed=LAYERS * (TAPS * width * width * 2 + frames * width * 6),
            transcendentals=LAYERS * frames * width,
        ),
        name="convolve",
    )(sc, x, in_hbm(weight))


def head_kernel(scale, tiles, sc_ref, h_ref, t_ref, ws_ref, wt_ref, _, score_ref, g_ref,
                sq_s, et_s, sum_s):
    step = pl.program_id(0)
    frames, width = h_ref.shape
    tile = ws_ref.shape[1]
    sub = 256

    @pl.when(step == 0)
    def _():
        sum_s[...] = jnp.zeros_like(sum_s)

    @pl.when(step < tiles)
    def _():
        for c in range(tile // sub):
            cols = slice(c * sub, (c + 1) * sub)
            squash = jnp.tanh(dot(h_ref[...], ws_ref[:, cols]))
            exp_s = jnp.exp(5.0 * squash)
            sq_s[step, :, cols] = squash
            sum_s[0] += exp_s[:, :128] + exp_s[:, 128:]
            exp_t = jnp.exp(5.0 * jnp.tanh(dot(t_ref[...], wt_ref[:, cols])))
            et_s[step, :, cols] = exp_t
            sum_s[1] += exp_t[:, :128] + exp_t[:, 128:]

    @pl.when(step == tiles)
    def _():
        factor = scale * frame_mask(sc_ref, frames)
        for i in range(2):
            inverse = factor / jnp.sum(sum_s[i], axis=1, keepdims=True)
            sum_s[i] = jnp.broadcast_to(inverse, (frames, 128))
        g_ref[...] = jnp.zeros_like(g_ref)

    @pl.when(step >= tiles)
    def _():
        at = step - tiles
        for c in range(tile // 128):
            cols = slice(c * 128, (c + 1) * 128)
            squash = sq_s[at, :, cols]
            p = jnp.exp(5.0 * squash) * sum_s[0] - et_s[at, :, cols] * sum_s[1]
            score_ref[:, cols] = (p * (1.0 - squash * squash)).astype(BF16)
        g_ref[...] += dot_nt(score_ref[...], ws_ref[...])


def heads(sc, hidden, teacher_in, head_weight, teacher_head_weight, after, loss_scale):
    frames, width = hidden.shape
    wide = teacher_in.shape[1]
    scores = head_weight.shape[1]
    tiles = 4
    tile = scores // tiles
    big = pltpu.VMEM((tiles, frames, tile), F32)
    return pl.pallas_call(
        functools.partial(head_kernel, 5.0 * loss_scale, tiles),
        grid=(2 * tiles,),
        in_specs=[
            pl.BlockSpec(memory_space=pltpu.SMEM),
            pl.BlockSpec((frames, width), lambda i: (0, 0)),
            pl.BlockSpec((frames, wide), lambda i: (0, 0)),
            pl.BlockSpec((width, tile), lambda i: (0, i % tiles)),
            pl.BlockSpec((wide, tile), lambda i: (0, jnp.minimum(i, tiles - 1))),
            AFTER,
        ],
        out_specs=[
            pl.BlockSpec((frames, tile), lambda i: (0, jnp.maximum(i - tiles, 0))),
            pl.BlockSpec((frames, width), lambda i: (0, 0)),
        ],
        scratch_shapes=[
            big,
            big,
            pltpu.VMEM((2, frames, 128), F32),
        ],
        out_shape=[
            jax.ShapeDtypeStruct((frames, scores), BF16),
            jax.ShapeDtypeStruct((frames, width), F32),
        ],
        compiler_params=params(37, "arbitrary"),
        cost_estimate=pl.CostEstimate(
            flops=2 * frames * scores * (2 * width + wide),
            bytes_accessed=scores * (6 * width + 2 * wide),
            transcendentals=4 * frames * scores,
        ),
        name="heads",
    )(sc, in_hbm(hidden), teacher_in, in_hbm(head_weight), in_hbm(teacher_head_weight), after)


def head_grad_kernel(sc_ref, ha_ref, hb_ref, ga_ref, gb_ref, _, out_ref, res_s):
    half = ga_ref.shape[1] // 2
    first = sc_ref[2] == 0
    for c in range(half // 128):
        cols = [slice(x * half + c * 128, x * half + (c + 1) * 128) for x in range(2)]
        ga, gb = (jnp.concatenate([ref[:, at] for at in cols], axis=1) for ref in (ga_ref, gb_ref))
        res_s[c] = dot(ha_ref[...], ga) + dot(hb_ref[...], gb)
        for nx, nz, fz in BITS:
            for fx in range(2):
                row = ((nz * 2 + fz) * 2 + (nx ^ fx)) * 32
                rows = slice(row, row + 32)
                value = res_s[c, rows, fx * 128 : (fx + 1) * 128]
                if nx != fx:
                    value = jnp.where(first, value, res_s[c, rows, nx * 128 : (nx + 1) * 128])
                out_ref[nx, 0, nz, fz, 0, :, cols[fx]] = encode(value)


def head_grad(sc, h_mine, h_other, score_mine, score_other, after):
    rows, frames = h_mine.shape
    scores = score_mine.shape[1]
    tile = scores // 4

    def place(i, sc):
        high, low = i // 2, i % 2
        even = sc[2] == 0
        return (0, jnp.where(even, high ^ low, high), 0, 0, jnp.where(even, high, high ^ low), 0, 0)

    hidden = pl.BlockSpec((rows, frames), lambda i, sc: (0, 0))
    score = pl.BlockSpec((frames, tile), lambda i, sc: (0, i))
    return pl.pallas_call(
        head_grad_kernel,
        grid_spec=pltpu.PrefetchScalarGridSpec(
            num_scalar_prefetch=1,
            grid=(4,),
            in_specs=[hidden, hidden, score, score, AFTER],
            out_specs=pl.BlockSpec((2, 1, 2, 2, 1, 32, tile), place),
            scratch_shapes=[pltpu.VMEM((tile // 256, rows, 256), F32)],
        ),
        out_shape=jax.ShapeDtypeStruct((2, 2, 2, 2, 2, 32, tile), BF16),
        compiler_params=params(13, "arbitrary"),
        cost_estimate=pl.CostEstimate(
            flops=4 * rows * frames * scores,
            bytes_accessed=4 * frames * scores + 2 * rows * scores,
            transcendentals=0,
        ),
        name="head_grad",
    )(sc, h_mine, h_other, score_mine, score_other, in_hbm(after))


def back_kernel(sc_ref, g4_ref, h_ref, pre_ref, w_ref, send_ref, mine_ref, g_s, pad_s, tap_s, ht_s):
    step = pl.program_id(0)
    frames, width = g4_ref.shape

    @pl.when(step == 0)
    def _():
        g_s[...] = g4_ref[...]
        pad_s[...] = jnp.zeros_like(pad_s)

    g_act = frame_mask(sc_ref, frames) * g_s[...]
    pre = pre_ref[0]
    sigma = jax.nn.sigmoid(pre)
    g_pre = (g_act * sigma * (1.0 + pre * (1.0 - sigma))).astype(BF16)
    send_ref[0, :2] = g_pre.reshape(2, frames // 2, width)
    ht_s[...] = h_ref[0].T
    split_rows(sc_ref[2], ht_s, mine_ref.at[0], send_ref.at[0, 2])

    @pl.when(step < LAYERS - 1)
    def _():
        pad_s[PAD : PAD + frames] = g_pre.astype(F32)
        for at in range(LAYERS - 1, 0, -1):

            @pl.when(step == LAYERS - 1 - at)
            def _():
                reach = CLASSES * 2**at
                tap_s[0] = pad_s[PAD + reach : PAD + reach + frames].astype(BF16)
                tap_s[1] = pad_s[PAD - reach : PAD - reach + frames].astype(BF16)

        g_s[...] = (
            g_act
            + dot_nt(tap_s[0], w_ref[0, 0])
            + dot_nt(g_pre, w_ref[0, 1])
            + dot_nt(tap_s[1], w_ref[0, 2])
        )


def back(sc, g, saved, pre, weight):
    frames, width = g.shape

    def at(*block):
        return pl.BlockSpec((1, *block), lambda i: (LAYERS - 1 - i, *(0 for _ in block)))

    return pl.pallas_call(
        back_kernel,
        grid=(LAYERS,),
        in_specs=[
            pl.BlockSpec(memory_space=pltpu.SMEM),
            pl.BlockSpec((frames, width), lambda i: (0, 0)),
            at(frames, width),
            at(frames, width),
            pl.BlockSpec(
                (1, TAPS, width, width), lambda i: (jnp.maximum(LAYERS - 1 - i, 1), 0, 0, 0)
            ),
        ],
        out_specs=[at(3, frames // 2, width), at(width // 2, frames)],
        out_shape=[
            jax.ShapeDtypeStruct((LAYERS, 3, frames // 2, width), BF16),
            pltpu.HBM((LAYERS, width // 2, frames), BF16),
        ],
        scratch_shapes=[
            pltpu.VMEM((frames, width), F32),
            pltpu.VMEM((frames + 2 * PAD, width), F32),
            pltpu.VMEM((2, frames, width), BF16),
            pltpu.VMEM((width, frames), BF16),
        ],
        compiler_params=params(16, "arbitrary"),
        cost_estimate=pl.CostEstimate(
            flops=2 * (LAYERS - 1) * TAPS * frames * width * width,
            bytes_accessed=LAYERS * (TAPS * width * width * 2 + frames * width * 10),
            transcendentals=LAYERS * frames * width,
        ),
        name="back",
    )(sc, g, saved, pre, weight)


def conv_grad_kernel(sc_ref, mine_ref, send_ref, got_ref, _, *refs):
    outs, (pad_s, tap_s, left_s), results = refs[:8], refs[8:11], refs[11:]
    step = pl.program_id(0)
    frames = mine_ref.shape[2]
    width = send_ref.shape[3]

    @pl.when(step == 0)
    def _():
        pad_s[...] = jnp.zeros_like(pad_s)

    for side, ref in enumerate((send_ref, got_ref)):
        g_pre = ref[0, :2].reshape(frames, width)
        tap_s[1, side * frames : (side + 1) * frames] = g_pre
        pad_s[side, PAD : PAD + frames] = g_pre
    for at in range(LAYERS):

        @pl.when(step == at)
        def _():
            reach = CLASSES * 2**at
            for side in range(2):
                rows = slice(side * frames, (side + 1) * frames)
                tap_s[0, rows] = pad_s[side, PAD + reach : PAD + reach + frames]
                tap_s[2, rows] = pad_s[side, PAD - reach : PAD - reach + frames]

    core, mx, my, mz = (sc_ref[i] for i in range(2, 6))
    side = lax.broadcasted_iota(jnp.int32, (32, 128), 1) // 64
    straight, crossed = side == mx, side != mx
    left_s[:, :frames] = mine_ref[0]
    left_s[:, frames:] = got_ref[0, 2]
    for tap, res_s in enumerate(results):
        res_s[...] = dot(left_s[...], tap_s[tap])
        for dy, dz, fz in BITS:
            for fy in range(2):
                ny, nz = my ^ dy, mz ^ dz
                high = jnp.where(core == 0, fy, ny)
                cols = pl.ds(pl.multiple_of((high * 2 + (ny ^ fy)) * 128, 128), 128)
                row = pl.multiple_of((nz * 2 + fz) * 64, 64)
                a = res_s[pl.ds(row, 32), cols]
                b = pltpu.roll(res_s[pl.ds(row + 32, 32), cols], 64 * core, 1)
                outs[dy * 2 + dz][tap, fz, fy] = encode(jnp.where(straight, a, b))
                outs[4 + dy * 2 + dz][tap, fz, fy] = encode(jnp.where(crossed, a, b))


def conv_grad(sc, mine, send, got, after):
    _, rows, frames = mine.shape
    width = send.shape[3]

    def at(*block):
        return pl.BlockSpec((1, *block), lambda i: (i, *(0 for _ in block)))

    out = pl.BlockSpec((TAPS, 2, 2, 32, width // 4), lambda i: (i, 0, 0, 0, 0))
    return pl.pallas_call(
        conv_grad_kernel,
        grid=(LAYERS,),
        in_specs=[
            pl.BlockSpec(memory_space=pltpu.SMEM),
            at(rows, frames),
            at(3, frames // 2, width),
            at(3, frames // 2, width),
            AFTER,
        ],
        out_specs=[out] * 8,
        out_shape=[jax.ShapeDtypeStruct((LAYERS * TAPS, 2, 2, 32, width // 4), BF16)] * 8,
        scratch_shapes=[
            pltpu.VMEM((2, frames + 2 * PAD, width), BF16),
            pltpu.VMEM((TAPS, 2 * frames, width), BF16),
            pltpu.VMEM((rows, 2 * frames), BF16),
        ]
        + [pltpu.VMEM((rows, width), F32)] * TAPS,
        compiler_params=params(18, "arbitrary"),
        cost_estimate=pl.CostEstimate(
            flops=4 * LAYERS * TAPS * rows * frames * width,
            bytes_accessed=LAYERS * (7 * rows * frames * 2 + TAPS * rows * width * 2),
            transcendentals=0,
        ),
        name="conv_grad",
    )(sc, mine, send, got, in_hbm(after))


def total_of(ref, *at):
    total = decode(ref[(0, *at)])
    for i in range(1, 8):
        total = total + decode(ref[(i, *at)])
    return total


def head_far_kernel(got_ref, out_ref):
    half = got_ref.shape[-1] // 2
    for fz, fy, fx in BITS:
        for c in range(half // 128):
            lanes = slice(fx * half + c * 128, fx * half + (c + 1) * 128)
            out_ref[fx * 4 + fy * 2 + fz, c] = encode(total_of(got_ref, fz, fy, slice(None), lanes))


def head_far(got):
    tile = got.shape[-1]
    return pl.pallas_call(
        head_far_kernel,
        out_shape=jax.ShapeDtypeStruct((8, tile // 256, 32, 128), BF16),
        in_specs=[whole()],
        out_specs=whole(),
        compiler_params=params(8),
        cost_estimate=pl.CostEstimate(
            flops=8 * got.size, bytes_accessed=3 * got.size, transcendentals=got.size
        ),
        name="head_far",
    )(in_hbm(got))


def conv_far_kernel(*refs):
    first, second, (head_ref, out_ref) = refs[:8], refs[8:16], refs[16:]
    step = pl.program_id(0)
    blocks, each = head_ref.shape[1], first[0].shape[0]
    low = low_lanes((32, 128))

    @pl.when(step == 0)
    def _():
        out_ref[:, :blocks] = head_ref[...]

    for t in range(each):
        at = blocks + step * each + t
        for fz in range(2):
            for fy in range(2):
                a = sum(decode(ref[t, fz, fy]) for ref in first)
                b = sum(decode(ref[t, fz, fy]) for ref in second)
                out_ref[fy * 2 + fz, at] = encode(jnp.where(low, a, pltpu.roll(b, 64, 1)))
                out_ref[4 + fy * 2 + fz, at] = encode(jnp.where(low, pltpu.roll(a, 64, 1), b))


def conv_far(got, head):
    half = LAYERS * TAPS // 2
    steps = 3
    block = (half // steps, 2, 2, 32, 128)
    shape = (8, head.shape[1] + half, 32, 128)
    size = 8 * got[0].size
    return pl.pallas_call(
        conv_far_kernel,
        grid=(steps,),
        out_shape=jax.ShapeDtypeStruct(shape, BF16),
        in_specs=[pl.BlockSpec(block, lambda i: (i, 0, 0, 0, 0))] * 8
        + [pl.BlockSpec(block, lambda i: (i + steps, 0, 0, 0, 0))] * 8
        + [pl.BlockSpec(head.shape, lambda i: (0, 0, 0, 0))],
        out_specs=pl.BlockSpec(shape, lambda i: (0, 0, 0, 0)),
        compiler_params=params(8, "arbitrary"),
        cost_estimate=pl.CostEstimate(
            flops=8 * size, bytes_accessed=3 * size, transcendentals=size
        ),
        name="conv_far",
    )(*got, *got, head)


def finish_kernel(got_ref, conv_ref, head_ref):
    blocks = head_ref.shape[1] // 128
    for c in range(blocks):
        head_ref[:, c * 128 : (c + 1) * 128] = total_of(got_ref, c)
    half = LAYERS * TAPS // 2
    for t in range(half):
        total = total_of(got_ref, blocks + t)
        for tap, value in ((t, total), (t + half, pltpu.roll(total, 64, 1))):
            conv_ref[tap // TAPS, tap % TAPS] = value[:, :64]


def finish(got, scores):
    return pl.pallas_call(
        finish_kernel,
        out_shape=[
            jax.ShapeDtypeStruct((LAYERS, TAPS, 32, 64), F32),
            jax.ShapeDtypeStruct((32, scores // 8), F32),
        ],
        in_specs=[whole()],
        out_specs=[whole(), whole()],
        compiler_params=params(4),
        name="finish",
    )(got)


def swap(x):
    return lax.ppermute(x, AXES, other_core())


def on_device(student_in, teacher_rows, valid, conv_weight, head_weight, teacher_head_weight):
    _, frames, width = student_in.shape
    scores = head_weight.shape[1]
    loss_scale = scores / (3.0 * math.sqrt(READ * TM * frames))
    read, tm = (lax.axis_index(axis) for axis in AXES)
    core = read % 2
    even = 1 - core
    near_bits = (
        tm % 2 ^ read // 8 * even,
        tm // 4 ^ tm // 2 % 2 * even,
        read // 4 % 2 ^ read // 2 % 2 * even,
    )
    sc = jnp.stack([valid[0], tm, core, *near_bits])
    regrouped = regroup(student_in[0]).reshape(TM, frames // TM, width)
    student = exchange(regrouped, frame_groups()).reshape(frames, width)
    teacher = regroup(teacher_rows[0]).reshape(TM, frames // TM, -1)
    teacher = exchange(teacher, frame_groups()).reshape(frames, -1)

    saved, pre, hidden, h_mine, h_other = convolve(sc, student, conv_weight)
    h_got = swap(h_other)
    score, g = heads(
        sc, hidden, teacher, head_weight, teacher_head_weight, h_got, loss_scale
    )
    score_got = swap(score)
    send, mine = back(sc, g, saved, pre, conv_weight)
    got = swap(send)
    near = head_grad(sc, h_mine, h_got, score, score_got, mine)
    head_got = exchange(near.reshape(8, 4 * 32, scores // 4), near_groups())
    parts = conv_grad(sc, mine, send, got, near)
    conv_got = [parts[0]] + [near_swap(parts[i], i) for i in range(1, 8)]

    far = head_far(head_got.reshape(8, 2, 2, 32, scores // 4))
    far = conv_far(conv_got, far)
    return tuple(finish(exchange(far, far_groups()), scores))


def solution(mesh):
    return jax.shard_map(
        on_device,
        mesh=mesh,
        in_specs=(P("read", "tm", None), P("read", "tm", None), P("read"), P(), P(), P()),
        out_specs=(P(None, None, "read", "tm"), P("read", "tm")),
        check_vma=False,
    )
```

```python
import functools
import math

import jax
import jax.numpy as jnp
from jax import lax
from jax.experimental import pallas as pl
from jax.experimental.pallas import tpu as pltpu
from jax.sharding import PartitionSpec as P

LAYERS, TAPS = 4, 3
BASE_DILATION = 32
AXES = ("read", "tm")
READ, TM = 16, 8
CLASSES = BASE_DILATION // TM
PAD = CLASSES * 2 ** (LAYERS - 1)
BITS = [(a, b, c) for a in range(2) for b in range(2) for c in range(2)]
F32, BF16 = jnp.float32, jnp.bfloat16


def near_of(core, v):
    return (v // 2) ^ (v % 2) if core == 0 else v // 2


def far_of(core, v):
    return v // 2 if core == 0 else (v // 2) ^ (v % 2)


def high_low(core, near, far):
    return (far if core == 0 else near, near ^ far)


def device_index(x, y, z, core):
    return (((x % 2) * 4 + z) * 2 + core) * TM + y * 2 + x // 2


def groups_of(fixed, order):
    groups = {}
    for core in range(2):
        for x in range(4):
            for y in range(4):
                for z in range(4):
                    key = (core, fixed(core, x), fixed(core, y), fixed(core, z))
                    place = order(core, x) * 4 + order(core, y) * 2 + order(core, z)
                    groups.setdefault(key, [0] * 8)[place] = device_index(x, y, z, core)
    return list(groups.values())


def near_groups():
    def cube(core, v):
        return (v + core) % 4 // 2

    return groups_of(cube, near_of)


def near_swap(x, bits):
    pairs = [(group[i], group[i ^ bits]) for group in near_groups() for i in range(8)]
    return lax.ppermute(x, AXES, pairs)


def far_groups():
    return groups_of(near_of, far_of)


def other_core():
    return [(d, d ^ TM) for d in range(READ * TM)]


def frame_groups():
    return [[r * TM + t for t in range(TM)] for r in range(READ)]


def exchange(x, groups):
    return lax.all_to_all(x, AXES, 0, 0, tiled=True, axis_index_groups=groups)


def encode(x):
    return (x * jnp.abs(x)).astype(BF16)


def decode(y):
    y = y.astype(F32)
    return y * lax.rsqrt(jnp.maximum(jnp.abs(y), 1e-37))


def low_lanes(shape):
    return lax.broadcasted_iota(jnp.int32, shape, len(shape) - 1) < 64


def dot(a, b):
    return jnp.dot(a, b, preferred_element_type=F32)


def dot_nt(a, b):
    return lax.dot_general(a, b, (((1,), (1,)), ((), ())), preferred_element_type=F32)


def params(mib, *kinds):
    return pltpu.CompilerParams(dimension_semantics=kinds, vmem_limit_bytes=mib * 1024 * 1024)


def whole():
    return pl.BlockSpec(memory_space=pltpu.VMEM)


def in_hbm(x):
    return pltpu.with_memory_space_constraint(x, pltpu.HBM)


AFTER = pl.BlockSpec(memory_space=pl.ANY)


def frame_mask(sc_ref, frames):
    row = lax.broadcasted_iota(jnp.int32, (frames, 1), 0)
    position = row // CLASSES * BASE_DILATION + sc_ref[1] * CLASSES + row % CLASSES
    return (position < sc_ref[0]).astype(F32)


def regroup_kernel(x_ref, out_ref):
    frames = x_ref.shape[0]
    row = lax.broadcasted_iota(jnp.int32, (frames, frames), 0)
    col = lax.broadcasted_iota(jnp.int32, (frames, frames), 1)
    per = frames // TM
    source = (row % per) // CLASSES * BASE_DILATION + row // per * CLASSES + row % CLASSES
    select = jnp.where(col == source, 1.0, 0.0).astype(BF16)
    out_ref[...] = dot(select, x_ref[...]).astype(BF16)


def regroup(x):
    return pl.pallas_call(
        regroup_kernel,
        out_shape=jax.ShapeDtypeStruct(x.shape, BF16),
        in_specs=[whole()],
        out_specs=whole(),
        compiler_params=params(5),
        name="regroup",
    )(x)


def split_rows(core, ht_s, mine_ref, other_ref):
    for ref, owner in ((mine_ref, core), (other_ref, 1 - core)):
        for at, (nz, fz, xl) in enumerate(BITS):
            high = jnp.where(owner == 0, fz, nz)
            row = ((xl * 4 + high * 2 + (nz ^ fz)) * 2 + owner) * 32
            ref[at * 32 : (at + 1) * 32] = ht_s[pl.ds(pl.multiple_of(row, 32), 32)]


def conv_kernel(sc_ref, x_ref, w_ref, saved_ref, pre_ref, last_ref, mine_ref, other_ref, pad_s, tap_s, ht_s):
    layer = pl.program_id(0)
    frames, width = x_ref.shape

    @pl.when(layer == 0)
    def _():
        pad_s[...] = jnp.zeros_like(pad_s)
        pad_s[PAD : PAD + frames] = x_ref[...]

    for at in range(LAYERS):

        @pl.when(layer == at)
        def _():
            reach = CLASSES * 2**at
            tap_s[:, :width] = pad_s[PAD - reach : PAD - reach + frames]
            tap_s[:, 2 * width :] = pad_s[PAD + reach : PAD + reach + frames]

    middle = pad_s[PAD : PAD + frames]
    saved_ref[0] = middle
    tap_s[:, width : 2 * width] = middle
    pre = dot(tap_s[...], w_ref[0].reshape(TAPS * width, width))
    pre_ref[0] = pre
    new = (frame_mask(sc_ref, frames) * (middle.astype(F32) + jax.nn.silu(pre))).astype(BF16)
    pad_s[PAD : PAD + frames] = new

    @pl.when(layer == LAYERS - 1)
    def _():
        last_ref[...] = new
        ht_s[...] = new.T
        split_rows(sc_ref[2], ht_s, mine_ref, other_ref)


def convolve(sc, x, weight):
    frames, width = x.shape
    one = pl.BlockSpec((1, frames, width), lambda i: (i, 0, 0))
    flat = pl.BlockSpec((frames, width), lambda i: (0, 0))
    rows = pl.BlockSpec((width // 2, frames), lambda i: (0, 0))
    return pl.pallas_call(
        conv_kernel,
        grid=(LAYERS,),
        in_specs=[
            pl.BlockSpec(memory_space=pltpu.SMEM),
            flat,
            pl.BlockSpec((1, TAPS, width, width), lambda i: (i, 0, 0, 0)),
        ],
        out_specs=[one, one, flat, rows, rows],
        out_shape=[
            jax.ShapeDtypeStruct((LAYERS, frames, width), BF16),
            pltpu.HBM((LAYERS, frames, width), F32),
            pltpu.HBM((frames, width), BF16),
            pltpu.HBM((width // 2, frames), BF16),
            pltpu.HBM((width // 2, frames), BF16),
        ],
        scratch_shapes=[
            pltpu.VMEM((frames + 2 * PAD, width), BF16),
            pltpu.VMEM((frames, TAPS * width), BF16),
            pltpu.VMEM((width, frames), BF16),
        ],
        compiler_params=params(14, "arbitrary"),
        cost_estimate=pl.CostEstimate(
            flops=2 * LAYERS * TAPS * frames * width * width,
            bytes_accessed=LAYERS * (TAPS * width * width * 2 + frames * width * 6),
            transcendentals=LAYERS * frames * width,
        ),
        name="convolve",
    )(sc, x, in_hbm(weight))


def head_kernel(scale, tiles, sc_ref, h_ref, t_ref, ws_ref, wt_ref, _, score_ref, g_ref,
                sq_s, et_s, sum_s):
    step = pl.program_id(0)
    frames, width = h_ref.shape
    tile = ws_ref.shape[1]
    sub = 256

    @pl.when(step == 0)
    def _():
        sum_s[...] = jnp.zeros_like(sum_s)

    @pl.when(step < tiles)
    def _():
        for c in range(tile // sub):
            cols = slice(c * sub, (c + 1) * sub)
            squash = jnp.tanh(dot(h_ref[...], ws_ref[:, cols]))
            exp_s = jnp.exp(5.0 * squash)
            sq_s[step, :, cols] = squash
            sum_s[0] += exp_s[:, :128] + exp_s[:, 128:]
            exp_t = jnp.exp(5.0 * jnp.tanh(dot(t_ref[...], wt_ref[:, cols])))
            et_s[step, :, cols] = exp_t
            sum_s[1] += exp_t[:, :128] + exp_t[:, 128:]

    @pl.when(step == tiles)
    def _():
        factor = scale * frame_mask(sc_ref, frames)
        for i in range(2):
            inverse = factor / jnp.sum(sum_s[i], axis=1, keepdims=True)
            sum_s[i] = jnp.broadcast_to(inverse, (frames, 128))
        g_ref[...] = jnp.zeros_like(g_ref)

    @pl.when(step >= tiles)
    def _():
        at = step - tiles
        for c in range(tile // 128):
            cols = slice(c * 128, (c + 1) * 128)
            squash = sq_s[at, :, cols]
            p = jnp.exp(5.0 * squash) * sum_s[0] - et_s[at, :, cols] * sum_s[1]
            score_ref[:, cols] = (p * (1.0 - squash * squash)).astype(BF16)
        g_ref[...] += dot_nt(score_ref[...], ws_ref[...])


def heads(sc, hidden, teacher_in, head_weight, teacher_head_weight, after, loss_scale):
    frames, width = hidden.shape
    wide = teacher_in.shape[1]
    scores = head_weight.shape[1]
    tiles = 4
    tile = scores // tiles
    big = pltpu.VMEM((tiles, frames, tile), F32)
    return pl.pallas_call(
        functools.partial(head_kernel, 5.0 * loss_scale, tiles),
        grid=(2 * tiles,),
        in_specs=[
            pl.BlockSpec(memory_space=pltpu.SMEM),
            pl.BlockSpec((frames, width), lambda i: (0, 0)),
            pl.BlockSpec((frames, wide), lambda i: (0, 0)),
            pl.BlockSpec((width, tile), lambda i: (0, i % tiles)),
            pl.BlockSpec((wide, tile), lambda i: (0, jnp.minimum(i, tiles - 1))),
            AFTER,
        ],
        out_specs=[
            pl.BlockSpec((frames, tile), lambda i: (0, jnp.maximum(i - tiles, 0))),
            pl.BlockSpec((frames, width), lambda i: (0, 0)),
        ],
        scratch_shapes=[
            big,
            big,
            pltpu.VMEM((2, frames, 128), F32),
        ],
        out_shape=[
            jax.ShapeDtypeStruct((frames, scores), BF16),
            jax.ShapeDtypeStruct((frames, width), F32),
        ],
        compiler_params=params(37, "arbitrary"),
        cost_estimate=pl.CostEstimate(
            flops=2 * frames * scores * (2 * width + wide),
            bytes_accessed=scores * (6 * width + 2 * wide),
            transcendentals=4 * frames * scores,
        ),
        name="heads",
    )(sc, in_hbm(hidden), teacher_in, in_hbm(head_weight), in_hbm(teacher_head_weight), after)


def head_grad_kernel(sc_ref, ha_ref, hb_ref, ga_ref, gb_ref, _, out_ref, res_s):
    half = ga_ref.shape[1] // 2
    first = sc_ref[2] == 0
    for c in range(half // 128):
        cols = [slice(x * half + c * 128, x * half + (c + 1) * 128) for x in range(2)]
        ga, gb = (jnp.concatenate([ref[:, at] for at in cols], axis=1) for ref in (ga_ref, gb_ref))
        res_s[c] = dot(ha_ref[...], ga) + dot(hb_ref[...], gb)
        for nx, nz, fz in BITS:
            for fx in range(2):
                row = ((nz * 2 + fz) * 2 + (nx ^ fx)) * 32
                rows = slice(row, row + 32)
                value = res_s[c, rows, fx * 128 : (fx + 1) * 128]
                if nx != fx:
                    value = jnp.where(first, value, res_s[c, rows, nx * 128 : (nx + 1) * 128])
                out_ref[nx, 0, nz, fz, 0, :, cols[fx]] = encode(value)


def head_grad(sc, h_mine, h_other, score_mine, score_other, after):
    rows, frames = h_mine.shape
    scores = score_mine.shape[1]
    tile = scores // 4

    def place(i, sc):
        high, low = i // 2, i % 2
        even = sc[2] == 0
        return (0, jnp.where(even, high ^ low, high), 0, 0, jnp.where(even, high, high ^ low), 0, 0)

    hidden = pl.BlockSpec((rows, frames), lambda i, sc: (0, 0))
    score = pl.BlockSpec((frames, tile), lambda i, sc: (0, i))
    return pl.pallas_call(
        head_grad_kernel,
        grid_spec=pltpu.PrefetchScalarGridSpec(
            num_scalar_prefetch=1,
            grid=(4,),
            in_specs=[hidden, hidden, score, score, AFTER],
            out_specs=pl.BlockSpec((2, 1, 2, 2, 1, 32, tile), place),
            scratch_shapes=[pltpu.VMEM((tile // 256, rows, 256), F32)],
        ),
        out_shape=jax.ShapeDtypeStruct((2, 2, 2, 2, 2, 32, tile), BF16),
        compiler_params=params(13, "arbitrary"),
        cost_estimate=pl.CostEstimate(
            flops=4 * rows * frames * scores,
            bytes_accessed=4 * frames * scores + 2 * rows * scores,
            transcendentals=0,
        ),
        name="head_grad",
    )(sc, h_mine, h_other, score_mine, score_other, in_hbm(after))


def back_kernel(sc_ref, g4_ref, h_ref, pre_ref, w_ref, send_ref, mine_ref, g_s, pad_s, tap_s, ht_s):
    step = pl.program_id(0)
    frames, width = g4_ref.shape

    @pl.when(step == 0)
    def _():
        g_s[...] = g4_ref[...]
        pad_s[...] = jnp.zeros_like(pad_s)

    g_act = frame_mask(sc_ref, frames) * g_s[...]
    pre = pre_ref[0]
    sigma = jax.nn.sigmoid(pre)
    g_pre = (g_act * sigma * (1.0 + pre * (1.0 - sigma))).astype(BF16)
    send_ref[0, :2] = g_pre.reshape(2, frames // 2, width)
    ht_s[...] = h_ref[0].T
    split_rows(sc_ref[2], ht_s, mine_ref.at[0], send_ref.at[0, 2])

    @pl.when(step < LAYERS - 1)
    def _():
        pad_s[PAD : PAD + frames] = g_pre
        for at in range(LAYERS - 1, 0, -1):

            @pl.when(step == LAYERS - 1 - at)
            def _():
                reach = CLASSES * 2**at
                tap_s[0] = pad_s[PAD + reach : PAD + reach + frames]
                tap_s[1] = pad_s[PAD - reach : PAD - reach + frames]

        g_s[...] = (
            g_act
            + dot_nt(tap_s[0], w_ref[0, 0])
            + dot_nt(g_pre, w_ref[0, 1])
            + dot_nt(tap_s[1], w_ref[0, 2])
        )


def back(sc, g, saved, pre, weight):
    frames, width = g.shape

    def at(*block):
        return pl.BlockSpec((1, *block), lambda i: (LAYERS - 1 - i, *(0 for _ in block)))

    return pl.pallas_call(
        back_kernel,
        grid=(LAYERS,),
        in_specs=[
            pl.BlockSpec(memory_space=pltpu.SMEM),
            pl.BlockSpec((frames, width), lambda i: (0, 0)),
            at(frames, width),
            at(frames, width),
            pl.BlockSpec(
                (1, TAPS, width, width), lambda i: (jnp.maximum(LAYERS - 1 - i, 1), 0, 0, 0)
            ),
        ],
        out_specs=[at(3, frames // 2, width), at(width // 2, frames)],
        out_shape=[
            jax.ShapeDtypeStruct((LAYERS, 3, frames // 2, width), BF16),
            pltpu.HBM((LAYERS, width // 2, frames), BF16),
        ],
        scratch_shapes=[
            pltpu.VMEM((frames, width), F32),
            pltpu.VMEM((frames + 2 * PAD, width), BF16),
            pltpu.VMEM((2, frames, width), BF16),
            pltpu.VMEM((width, frames), BF16),
        ],
        compiler_params=params(16, "arbitrary"),
        cost_estimate=pl.CostEstimate(
            flops=2 * (LAYERS - 1) * TAPS * frames * width * width,
            bytes_accessed=LAYERS * (TAPS * width * width * 2 + frames * width * 10),
            transcendentals=LAYERS * frames * width,
        ),
        name="back",
    )(sc, g, saved, pre, weight)


def conv_grad_kernel(sc_ref, mine_ref, send_ref, got_ref, _, *refs):
    outs, (pad_s, tap_s, left_s), results = refs[:8], refs[8:11], refs[11:]
    step = pl.program_id(0)
    frames = mine_ref.shape[2]
    width = send_ref.shape[3]

    @pl.when(step == 0)
    def _():
        pad_s[...] = jnp.zeros_like(pad_s)

    for side, ref in enumerate((send_ref, got_ref)):
        g_pre = ref[0, :2].reshape(frames, width)
        tap_s[1, side * frames : (side + 1) * frames] = g_pre
        pad_s[side, PAD : PAD + frames] = g_pre
    for at in range(LAYERS):

        @pl.when(step == at)
        def _():
            reach = CLASSES * 2**at
            for side in range(2):
                rows = slice(side * frames, (side + 1) * frames)
                tap_s[0, rows] = pad_s[side, PAD + reach : PAD + reach + frames]
                tap_s[2, rows] = pad_s[side, PAD - reach : PAD - reach + frames]

    core, mx, my, mz = (sc_ref[i] for i in range(2, 6))
    side = lax.broadcasted_iota(jnp.int32, (32, 128), 1) // 64
    straight, crossed = side == mx, side != mx
    left_s[:, :frames] = mine_ref[0]
    left_s[:, frames:] = got_ref[0, 2]
    for tap, res_s in enumerate(results):
        res_s[...] = dot(left_s[...], tap_s[tap])
        for dy, dz, fz in BITS:
            for fy in range(2):
                ny, nz = my ^ dy, mz ^ dz
                high = jnp.where(core == 0, fy, ny)
                cols = pl.ds(pl.multiple_of((high * 2 + (ny ^ fy)) * 128, 128), 128)
                row = pl.multiple_of((nz * 2 + fz) * 64, 64)
                a = res_s[pl.ds(row, 32), cols]
                b = pltpu.roll(res_s[pl.ds(row + 32, 32), cols], 64 * core, 1)
                outs[dy * 2 + dz][tap, fz, fy] = encode(jnp.where(straight, a, b))
                outs[4 + dy * 2 + dz][tap, fz, fy] = encode(jnp.where(crossed, a, b))


def conv_grad(sc, mine, send, got, after):
    _, rows, frames = mine.shape
    width = send.shape[3]

    def at(*block):
        return pl.BlockSpec((1, *block), lambda i: (i, *(0 for _ in block)))

    out = pl.BlockSpec((TAPS, 2, 2, 32, width // 4), lambda i: (i, 0, 0, 0, 0))
    return pl.pallas_call(
        conv_grad_kernel,
        grid=(LAYERS,),
        in_specs=[
            pl.BlockSpec(memory_space=pltpu.SMEM),
            at(rows, frames),
            at(3, frames // 2, width),
            at(3, frames // 2, width),
            AFTER,
        ],
        out_specs=[out] * 8,
        out_shape=[jax.ShapeDtypeStruct((LAYERS * TAPS, 2, 2, 32, width // 4), BF16)] * 8,
        scratch_shapes=[
            pltpu.VMEM((2, frames + 2 * PAD, width), BF16),
            pltpu.VMEM((TAPS, 2 * frames, width), BF16),
            pltpu.VMEM((rows, 2 * frames), BF16),
        ]
        + [pltpu.VMEM((rows, width), F32)] * TAPS,
        compiler_params=params(18, "arbitrary"),
        cost_estimate=pl.CostEstimate(
            flops=4 * LAYERS * TAPS * rows * frames * width,
            bytes_accessed=LAYERS * (7 * rows * frames * 2 + TAPS * rows * width * 2),
            transcendentals=0,
        ),
        name="conv_grad",
    )(sc, mine, send, got, in_hbm(after))


def total_of(ref, *at):
    total = decode(ref[(0, *at)])
    for i in range(1, 8):
        total = total + decode(ref[(i, *at)])
    return total


def head_far_kernel(got_ref, out_ref):
    half = got_ref.shape[-1] // 2
    for fz, fy, fx in BITS:
        for c in range(half // 128):
            lanes = slice(fx * half + c * 128, fx * half + (c + 1) * 128)
            out_ref[fx * 4 + fy * 2 + fz, c] = encode(total_of(got_ref, fz, fy, slice(None), lanes))


def head_far(got):
    tile = got.shape[-1]
    return pl.pallas_call(
        head_far_kernel,
        out_shape=jax.ShapeDtypeStruct((8, tile // 256, 32, 128), BF16),
        in_specs=[whole()],
        out_specs=whole(),
        compiler_params=params(8),
        cost_estimate=pl.CostEstimate(
            flops=8 * got.size, bytes_accessed=3 * got.size, transcendentals=got.size
        ),
        name="head_far",
    )(in_hbm(got))


def conv_far_kernel(*refs):
    first, second, (head_ref, out_ref) = refs[:8], refs[8:16], refs[16:]
    step = pl.program_id(0)
    blocks, each = head_ref.shape[1], first[0].shape[0]
    low = low_lanes((32, 128))

    @pl.when(step == 0)
    def _():
        out_ref[:, :blocks] = head_ref[...]

    for t in range(each):
        at = blocks + step * each + t
        for fz in range(2):
            for fy in range(2):
                a = sum(decode(ref[t, fz, fy]) for ref in first)
                b = sum(decode(ref[t, fz, fy]) for ref in second)
                out_ref[fy * 2 + fz, at] = encode(jnp.where(low, a, pltpu.roll(b, 64, 1)))
                out_ref[4 + fy * 2 + fz, at] = encode(jnp.where(low, pltpu.roll(a, 64, 1), b))


def conv_far(got, head):
    half = LAYERS * TAPS // 2
    steps = 3
    block = (half // steps, 2, 2, 32, 128)
    shape = (8, head.shape[1] + half, 32, 128)
    size = 8 * got[0].size
    return pl.pallas_call(
        conv_far_kernel,
        grid=(steps,),
        out_shape=jax.ShapeDtypeStruct(shape, BF16),
        in_specs=[pl.BlockSpec(block, lambda i: (i, 0, 0, 0, 0))] * 8
        + [pl.BlockSpec(block, lambda i: (i + steps, 0, 0, 0, 0))] * 8
        + [pl.BlockSpec(head.shape, lambda i: (0, 0, 0, 0))],
        out_specs=pl.BlockSpec(shape, lambda i: (0, 0, 0, 0)),
        compiler_params=params(8, "arbitrary"),
        cost_estimate=pl.CostEstimate(
            flops=8 * size, bytes_accessed=3 * size, transcendentals=size
        ),
        name="conv_far",
    )(*got, *got, head)


def finish_kernel(got_ref, conv_ref, head_ref):
    blocks = head_ref.shape[1] // 128
    for c in range(blocks):
        head_ref[:, c * 128 : (c + 1) * 128] = total_of(got_ref, c)
    half = LAYERS * TAPS // 2
    for t in range(half):
        total = total_of(got_ref, blocks + t)
        for tap, value in ((t, total), (t + half, pltpu.roll(total, 64, 1))):
            conv_ref[tap // TAPS, tap % TAPS] = value[:, :64]


def finish(got, scores):
    return pl.pallas_call(
        finish_kernel,
        out_shape=[
            jax.ShapeDtypeStruct((LAYERS, TAPS, 32, 64), F32),
            jax.ShapeDtypeStruct((32, scores // 8), F32),
        ],
        in_specs=[whole()],
        out_specs=[whole(), whole()],
        compiler_params=params(4),
        name="finish",
    )(got)


def swap(x):
    return lax.ppermute(x, AXES, other_core())


def on_device(student_in, teacher_rows, valid, conv_weight, head_weight, teacher_head_weight):
    _, frames, width = student_in.shape
    scores = head_weight.shape[1]
    loss_scale = scores / (3.0 * math.sqrt(READ * TM * frames))
    read, tm = (lax.axis_index(axis) for axis in AXES)
    core = read % 2
    even = 1 - core
    near_bits = (
        tm % 2 ^ read // 8 * even,
        tm // 4 ^ tm // 2 % 2 * even,
        read // 4 % 2 ^ read // 2 % 2 * even,
    )
    sc = jnp.stack([valid[0], tm, core, *near_bits])
    regrouped = regroup(student_in[0]).reshape(TM, frames // TM, width)
    student = exchange(regrouped, frame_groups()).reshape(frames, width)
    teacher = regroup(teacher_rows[0]).reshape(TM, frames // TM, -1)
    teacher = exchange(teacher, frame_groups()).reshape(frames, -1)

    saved, pre, hidden, h_mine, h_other = convolve(sc, student, conv_weight)
    h_got = swap(h_other)
    score, g = heads(
        sc, hidden, teacher, head_weight, teacher_head_weight, h_got, loss_scale
    )
    score_got = swap(score)
    send, mine = back(sc, g, saved, pre, conv_weight)
    got = swap(send)
    near = head_grad(sc, h_mine, h_got, score, score_got, mine)
    head_got = exchange(near.reshape(8, 4 * 32, scores // 4), near_groups())
    parts = conv_grad(sc, mine, send, got, near)
    conv_got = [parts[0]] + [near_swap(parts[i], i) for i in range(1, 8)]

    far = head_far(head_got.reshape(8, 2, 2, 32, scores // 4))
    far = conv_far(conv_got, far)
    return tuple(finish(exchange(far, far_groups()), scores))


def solution(mesh):
    return jax.shard_map(
        on_device,
        mesh=mesh,
        in_specs=(P("read", "tm", None), P("read", "tm", None), P("read"), P(), P(), P()),
        out_specs=(P(None, None, "read", "tm"), P("read", "tm")),
        check_vma=False,
    )
```

```python
import functools
import math

import jax
import jax.numpy as jnp
from jax import lax
from jax.experimental import pallas as pl
from jax.experimental.pallas import tpu as pltpu
from jax.sharding import PartitionSpec as P

LAYERS, TAPS = 4, 3
BASE_DILATION = 32
AXES = ("read", "tm")
READ, TM = 16, 8
CLASSES = BASE_DILATION // TM
PAD = CLASSES * 2 ** (LAYERS - 1)
BITS = [(a, b, c) for a in range(2) for b in range(2) for c in range(2)]
F32, BF16 = jnp.float32, jnp.bfloat16


def near_of(core, v):
    return (v // 2) ^ (v % 2) if core == 0 else v // 2


def far_of(core, v):
    return v // 2 if core == 0 else (v // 2) ^ (v % 2)


def high_low(core, near, far):
    return (far if core == 0 else near, near ^ far)


def device_index(x, y, z, core):
    return (((x % 2) * 4 + z) * 2 + core) * TM + y * 2 + x // 2


def groups_of(fixed, order):
    groups = {}
    for core in range(2):
        for x in range(4):
            for y in range(4):
                for z in range(4):
                    key = (core, fixed(core, x), fixed(core, y), fixed(core, z))
                    place = order(core, x) * 4 + order(core, y) * 2 + order(core, z)
                    groups.setdefault(key, [0] * 8)[place] = device_index(x, y, z, core)
    return list(groups.values())


def near_groups():
    def cube(core, v):
        return (v + core) % 4 // 2

    return groups_of(cube, near_of)


def near_swap(x, bits):
    pairs = [(group[i], group[i ^ bits]) for group in near_groups() for i in range(8)]
    return lax.ppermute(x, AXES, pairs)


def far_groups():
    return groups_of(near_of, far_of)


def other_core():
    return [(d, d ^ TM) for d in range(READ * TM)]


def frame_groups():
    return [[r * TM + t for t in range(TM)] for r in range(READ)]


def exchange(x, groups):
    return lax.all_to_all(x, AXES, 0, 0, tiled=True, axis_index_groups=groups)


def encode(x):
    return (x * jnp.abs(x)).astype(BF16)


def decode(y):
    y = y.astype(F32)
    return y * lax.rsqrt(jnp.maximum(jnp.abs(y), 1e-37))


def low_lanes(shape):
    return lax.broadcasted_iota(jnp.int32, shape, len(shape) - 1) < 64


def dot(a, b):
    return jnp.dot(a, b, preferred_element_type=F32)


def dot_nt(a, b):
    return lax.dot_general(a, b, (((1,), (1,)), ((), ())), preferred_element_type=F32)


def params(mib, *kinds):
    return pltpu.CompilerParams(dimension_semantics=kinds, vmem_limit_bytes=mib * 1024 * 1024)


def whole():
    return pl.BlockSpec(memory_space=pltpu.VMEM)


def in_hbm(x):
    return pltpu.with_memory_space_constraint(x, pltpu.HBM)


AFTER = pl.BlockSpec(memory_space=pl.ANY)


def frame_mask(sc_ref, frames):
    row = lax.broadcasted_iota(jnp.int32, (frames, 1), 0)
    position = row // CLASSES * BASE_DILATION + sc_ref[1] * CLASSES + row % CLASSES
    return (position < sc_ref[0]).astype(F32)


def regroup_kernel(x_ref, out_ref):
    frames = x_ref.shape[0]
    row = lax.broadcasted_iota(jnp.int32, (frames, frames), 0)
    col = lax.broadcasted_iota(jnp.int32, (frames, frames), 1)
    per = frames // TM
    source = (row % per) // CLASSES * BASE_DILATION + row // per * CLASSES + row % CLASSES
    select = jnp.where(col == source, 1.0, 0.0).astype(BF16)
    out_ref[...] = dot(select, x_ref[...]).astype(BF16)


def regroup(x):
    return pl.pallas_call(
        regroup_kernel,
        out_shape=jax.ShapeDtypeStruct(x.shape, BF16),
        in_specs=[whole()],
        out_specs=whole(),
        compiler_params=params(5),
        name="regroup",
    )(x)


def split_rows(core, ht_s, mine_ref, other_ref):
    for ref, owner in ((mine_ref, core), (other_ref, 1 - core)):
        for at, (nz, fz, xl) in enumerate(BITS):
            high = jnp.where(owner == 0, fz, nz)
            row = ((xl * 4 + high * 2 + (nz ^ fz)) * 2 + owner) * 32
            ref[at * 32 : (at + 1) * 32] = ht_s[pl.ds(pl.multiple_of(row, 32), 32)]


def conv_kernel(sc_ref, x_ref, w_ref, saved_ref, pre_ref, last_ref, mine_ref, other_ref, pad_s, tap_s, ht_s):
    layer = pl.program_id(0)
    frames = x_ref.shape[0]

    @pl.when(layer == 0)
    def _():
        pad_s[...] = jnp.zeros_like(pad_s)
        pad_s[PAD : PAD + frames] = x_ref[...].astype(F32)

    for at in range(LAYERS):

        @pl.when(layer == at)
        def _():
            reach = CLASSES * 2**at
            tap_s[0] = pad_s[PAD - reach : PAD - reach + frames].astype(BF16)
            tap_s[1] = pad_s[PAD + reach : PAD + reach + frames].astype(BF16)

    hidden = pad_s[PAD : PAD + frames]
    middle = hidden.astype(BF16)
    saved_ref[0] = middle
    pre = dot(tap_s[0], w_ref[0, 0]) + dot(middle, w_ref[0, 1]) + dot(tap_s[1], w_ref[0, 2])
    pre_ref[0] = pre
    new = (frame_mask(sc_ref, frames) * (hidden + jax.nn.silu(pre))).astype(BF16)
    pad_s[PAD : PAD + frames] = new.astype(F32)

    @pl.when(layer == LAYERS - 1)
    def _():
        last_ref[...] = new
        ht_s[...] = new.T
        split_rows(sc_ref[2], ht_s, mine_ref, other_ref)


def convolve(sc, x, weight):
    frames, width = x.shape
    one = pl.BlockSpec((1, frames, width), lambda i: (i, 0, 0))
    flat = pl.BlockSpec((frames, width), lambda i: (0, 0))
    rows = pl.BlockSpec((width // 2, frames), lambda i: (0, 0))
    return pl.pallas_call(
        conv_kernel,
        grid=(LAYERS,),
        in_specs=[
            pl.BlockSpec(memory_space=pltpu.SMEM),
            flat,
            pl.BlockSpec((1, TAPS, width, width), lambda i: (i, 0, 0, 0)),
        ],
        out_specs=[one, one, flat, rows, rows],
        out_shape=[
            jax.ShapeDtypeStruct((LAYERS, frames, width), BF16),
            pltpu.HBM((LAYERS, frames, width), F32),
            pltpu.HBM((frames, width), BF16),
            pltpu.HBM((width // 2, frames), BF16),
            pltpu.HBM((width // 2, frames), BF16),
        ],
        scratch_shapes=[
            pltpu.VMEM((frames + 2 * PAD, width), F32),
            pltpu.VMEM((2, frames, width), BF16),
            pltpu.VMEM((width, frames), BF16),
        ],
        compiler_params=params(14, "arbitrary"),
        cost_estimate=pl.CostEstimate(
            flops=2 * LAYERS * TAPS * frames * width * width,
            bytes_accessed=LAYERS * (TAPS * width * width * 2 + frames * width * 6),
            transcendentals=LAYERS * frames * width,
        ),
        name="convolve",
    )(sc, x, in_hbm(weight))


def head_kernel(scale, tiles, sc_ref, h_ref, t_ref, ws_ref, wt_ref, _, score_ref, g_ref,
                sq_s, et_s, sum_s):
    step = pl.program_id(0)
    frames, width = h_ref.shape
    tile = ws_ref.shape[1]
    sub = 256

    @pl.when(step == 0)
    def _():
        sum_s[...] = jnp.zeros_like(sum_s)

    @pl.when(step < tiles)
    def _():
        for c in range(tile // sub):
            cols = slice(c * sub, (c + 1) * sub)
            squash = jnp.tanh(dot(h_ref[...], ws_ref[:, cols]))
            exp_s = jnp.exp(5.0 * squash)
            sq_s[step, :, cols] = squash
            sum_s[0] += exp_s[:, :128] + exp_s[:, 128:]
            exp_t = jnp.exp(5.0 * jnp.tanh(dot(t_ref[...], wt_ref[:, cols])))
            et_s[step, :, cols] = exp_t
            sum_s[1] += exp_t[:, :128] + exp_t[:, 128:]

    @pl.when(step == tiles)
    def _():
        factor = scale * frame_mask(sc_ref, frames)
        for i in range(2):
            inverse = factor / jnp.sum(sum_s[i], axis=1, keepdims=True)
            sum_s[i] = jnp.broadcast_to(inverse, (frames, 128))
        g_ref[...] = jnp.zeros_like(g_ref)

    @pl.when(step >= tiles)
    def _():
        at = step - tiles
        for c in range(tile // 128):
            cols = slice(c * 128, (c + 1) * 128)
            squash = sq_s[at, :, cols]
            p = jnp.exp(5.0 * squash) * sum_s[0] - et_s[at, :, cols] * sum_s[1]
            score_ref[:, cols] = (p * (1.0 - squash * squash)).astype(BF16)
        g_ref[...] += dot_nt(score_ref[...], ws_ref[...])


def heads(sc, hidden, teacher_in, head_weight, teacher_head_weight, after, loss_scale):
    frames, width = hidden.shape
    wide = teacher_in.shape[1]
    scores = head_weight.shape[1]
    tiles = 4
    tile = scores // tiles
    big = pltpu.VMEM((tiles, frames, tile), F32)
    return pl.pallas_call(
        functools.partial(head_kernel, 5.0 * loss_scale, tiles),
        grid=(2 * tiles,),
        in_specs=[
            pl.BlockSpec(memory_space=pltpu.SMEM),
            pl.BlockSpec((frames, width), lambda i: (0, 0)),
            pl.BlockSpec((frames, wide), lambda i: (0, 0)),
            pl.BlockSpec((width, tile), lambda i: (0, i % tiles)),
            pl.BlockSpec((wide, tile), lambda i: (0, jnp.minimum(i, tiles - 1))),
            AFTER,
        ],
        out_specs=[
            pl.BlockSpec((frames, tile), lambda i: (0, jnp.maximum(i - tiles, 0))),
            pl.BlockSpec((frames, width), lambda i: (0, 0)),
        ],
        scratch_shapes=[
            big,
            big,
            pltpu.VMEM((2, frames, 128), F32),
        ],
        out_shape=[
            jax.ShapeDtypeStruct((frames, scores), BF16),
            jax.ShapeDtypeStruct((frames, width), F32),
        ],
        compiler_params=params(37, "arbitrary"),
        cost_estimate=pl.CostEstimate(
            flops=2 * frames * scores * (2 * width + wide),
            bytes_accessed=scores * (6 * width + 2 * wide),
            transcendentals=4 * frames * scores,
        ),
        name="heads",
    )(sc, in_hbm(hidden), teacher_in, in_hbm(head_weight), in_hbm(teacher_head_weight), after)


def head_grad_kernel(sc_ref, ha_ref, hb_ref, ga_ref, gb_ref, _, out_ref, res_s):
    half = ga_ref.shape[1] // 2
    first = sc_ref[2] == 0
    for c in range(half // 128):
        cols = [slice(x * half + c * 128, x * half + (c + 1) * 128) for x in range(2)]
        ga, gb = (jnp.concatenate([ref[:, at] for at in cols], axis=1) for ref in (ga_ref, gb_ref))
        res_s[c] = dot(ha_ref[...], ga) + dot(hb_ref[...], gb)
        for nx, nz, fz in BITS:
            for fx in range(2):
                row = ((nz * 2 + fz) * 2 + (nx ^ fx)) * 32
                rows = slice(row, row + 32)
                value = res_s[c, rows, fx * 128 : (fx + 1) * 128]
                if nx != fx:
                    value = jnp.where(first, value, res_s[c, rows, nx * 128 : (nx + 1) * 128])
                out_ref[nx, 0, nz, fz, 0, :, cols[fx]] = encode(value)


def head_grad(sc, h_mine, h_other, score_mine, score_other, after):
    rows, frames = h_mine.shape
    scores = score_mine.shape[1]
    tile = scores // 4

    def place(i, sc):
        high, low = i // 2, i % 2
        even = sc[2] == 0
        return (0, jnp.where(even, high ^ low, high), 0, 0, jnp.where(even, high, high ^ low), 0, 0)

    hidden = pl.BlockSpec((rows, frames), lambda i, sc: (0, 0))
    score = pl.BlockSpec((frames, tile), lambda i, sc: (0, i))
    return pl.pallas_call(
        head_grad_kernel,
        grid_spec=pltpu.PrefetchScalarGridSpec(
            num_scalar_prefetch=1,
            grid=(4,),
            in_specs=[hidden, hidden, score, score, AFTER],
            out_specs=pl.BlockSpec((2, 1, 2, 2, 1, 32, tile), place),
            scratch_shapes=[pltpu.VMEM((tile // 256, rows, 256), F32)],
        ),
        out_shape=jax.ShapeDtypeStruct((2, 2, 2, 2, 2, 32, tile), BF16),
        compiler_params=params(13, "arbitrary"),
        cost_estimate=pl.CostEstimate(
            flops=4 * rows * frames * scores,
            bytes_accessed=4 * frames * scores + 2 * rows * scores,
            transcendentals=0,
        ),
        name="head_grad",
    )(sc, h_mine, h_other, score_mine, score_other, in_hbm(after))


def back_kernel(sc_ref, g4_ref, h_ref, pre_ref, w_ref, send_ref, mine_ref, g_s, pad_s, tap_s, ht_s):
    step = pl.program_id(0)
    frames, width = g4_ref.shape

    @pl.when(step == 0)
    def _():
        g_s[...] = g4_ref[...]
        pad_s[...] = jnp.zeros_like(pad_s)

    g_act = frame_mask(sc_ref, frames) * g_s[...]
    pre = pre_ref[0]
    sigma = jax.nn.sigmoid(pre)
    g_pre = (g_act * sigma * (1.0 + pre * (1.0 - sigma))).astype(BF16)
    send_ref[0, :2] = g_pre.reshape(2, frames // 2, width)
    ht_s[...] = h_ref[0].T
    split_rows(sc_ref[2], ht_s, mine_ref.at[0], send_ref.at[0, 2])

    @pl.when(step < LAYERS - 1)
    def _():
        pad_s[PAD : PAD + frames] = g_pre.astype(F32)
        for at in range(LAYERS - 1, 0, -1):

            @pl.when(step == LAYERS - 1 - at)
            def _():
                reach = CLASSES * 2**at
                tap_s[0] = pad_s[PAD + reach : PAD + reach + frames].astype(BF16)
                tap_s[1] = pad_s[PAD - reach : PAD - reach + frames].astype(BF16)

        g_s[...] = (
            g_act
            + dot_nt(tap_s[0], w_ref[0, 0])
            + dot_nt(g_pre, w_ref[0, 1])
            + dot_nt(tap_s[1], w_ref[0, 2])
        )


def back(sc, g, saved, pre, weight):
    frames, width = g.shape

    def at(*block):
        return pl.BlockSpec((1, *block), lambda i: (LAYERS - 1 - i, *(0 for _ in block)))

    return pl.pallas_call(
        back_kernel,
        grid=(LAYERS,),
        in_specs=[
            pl.BlockSpec(memory_space=pltpu.SMEM),
            pl.BlockSpec((frames, width), lambda i: (0, 0)),
            at(frames, width),
            at(frames, width),
            pl.BlockSpec(
                (1, TAPS, width, width), lambda i: (jnp.maximum(LAYERS - 1 - i, 1), 0, 0, 0)
            ),
        ],
        out_specs=[at(3, frames // 2, width), at(width // 2, frames)],
        out_shape=[
            jax.ShapeDtypeStruct((LAYERS, 3, frames // 2, width), BF16),
            pltpu.HBM((LAYERS, width // 2, frames), BF16),
        ],
        scratch_shapes=[
            pltpu.VMEM((frames, width), F32),
            pltpu.VMEM((frames + 2 * PAD, width), F32),
            pltpu.VMEM((2, frames, width), BF16),
            pltpu.VMEM((width, frames), BF16),
        ],
        compiler_params=params(16, "arbitrary"),
        cost_estimate=pl.CostEstimate(
            flops=2 * (LAYERS - 1) * TAPS * frames * width * width,
            bytes_accessed=LAYERS * (TAPS * width * width * 2 + frames * width * 10),
            transcendentals=LAYERS * frames * width,
        ),
        name="back",
    )(sc, g, saved, pre, weight)


def conv_grad_kernel(sc_ref, mine_ref, send_ref, got_ref, _, *refs):
    outs, (pad_s, tap_s, left_s), results = refs[:8], refs[8:11], refs[11:]
    step = pl.program_id(0)
    frames = mine_ref.shape[2]
    width = send_ref.shape[3]

    @pl.when(step == 0)
    def _():
        pad_s[...] = jnp.zeros_like(pad_s)

    for side, ref in enumerate((send_ref, got_ref)):
        g_pre = ref[0, :2].reshape(frames, width)
        tap_s[1, side * frames : (side + 1) * frames] = g_pre
        pad_s[side, PAD : PAD + frames] = g_pre
    for at in range(LAYERS):

        @pl.when(step == at)
        def _():
            reach = CLASSES * 2**at
            for side in range(2):
                rows = slice(side * frames, (side + 1) * frames)
                tap_s[0, rows] = pad_s[side, PAD + reach : PAD + reach + frames]
                tap_s[2, rows] = pad_s[side, PAD - reach : PAD - reach + frames]

    core, mx, my, mz = (sc_ref[i] for i in range(2, 6))
    side = lax.broadcasted_iota(jnp.int32, (32, 128), 1) // 64
    straight, crossed = side == mx, side != mx
    left_s[:, :frames] = mine_ref[0]
    left_s[:, frames:] = got_ref[0, 2]
    for tap, res_s in enumerate(results):
        res_s[...] = dot(left_s[...], tap_s[tap])
        for dy, dz, fz in BITS:
            for fy in range(2):
                ny, nz = my ^ dy, mz ^ dz
                high = jnp.where(core == 0, fy, ny)
                cols = pl.ds(pl.multiple_of((high * 2 + (ny ^ fy)) * 128, 128), 128)
                row = pl.multiple_of((nz * 2 + fz) * 64, 64)
                a = res_s[pl.ds(row, 32), cols]
                b = pltpu.roll(res_s[pl.ds(row + 32, 32), cols], 64 * core, 1)
                outs[dy * 2 + dz][tap, fz, fy] = encode(jnp.where(straight, a, b))
                outs[4 + dy * 2 + dz][tap, fz, fy] = encode(jnp.where(crossed, a, b))


def conv_grad(sc, mine, send, got, after):
    _, rows, frames = mine.shape
    width = send.shape[3]

    def at(*block):
        return pl.BlockSpec((1, *block), lambda i: (i, *(0 for _ in block)))

    out = pl.BlockSpec((TAPS, 2, 2, 32, width // 4), lambda i: (i, 0, 0, 0, 0))
    return pl.pallas_call(
        conv_grad_kernel,
        grid=(LAYERS,),
        in_specs=[
            pl.BlockSpec(memory_space=pltpu.SMEM),
            at(rows, frames),
            at(3, frames // 2, width),
            at(3, frames // 2, width),
            AFTER,
        ],
        out_specs=[out] * 8,
        out_shape=[jax.ShapeDtypeStruct((LAYERS * TAPS, 2, 2, 32, width // 4), BF16)] * 8,
        scratch_shapes=[
            pltpu.VMEM((2, frames + 2 * PAD, width), BF16),
            pltpu.VMEM((TAPS, 2 * frames, width), BF16),
            pltpu.VMEM((rows, 2 * frames), BF16),
        ]
        + [pltpu.VMEM((rows, width), F32)] * TAPS,
        compiler_params=params(18, "arbitrary"),
        cost_estimate=pl.CostEstimate(
            flops=4 * LAYERS * TAPS * rows * frames * width,
            bytes_accessed=LAYERS * (7 * rows * frames * 2 + TAPS * rows * width * 2),
            transcendentals=0,
        ),
        name="conv_grad",
    )(sc, mine, send, got, in_hbm(after))


def total_of(ref, *at):
    total = decode(ref[(0, *at)])
    for i in range(1, 8):
        total = total + decode(ref[(i, *at)])
    return total


def head_far_kernel(got_ref, out_ref):
    half = got_ref.shape[-1] // 2
    for fz, fy, fx in BITS:
        for c in range(half // 128):
            lanes = slice(fx * half + c * 128, fx * half + (c + 1) * 128)
            out_ref[fx * 4 + fy * 2 + fz, c] = encode(total_of(got_ref, fz, fy, slice(None), lanes))


def head_far(got):
    tile = got.shape[-1]
    return pl.pallas_call(
        head_far_kernel,
        out_shape=jax.ShapeDtypeStruct((8, tile // 256, 32, 128), BF16),
        in_specs=[whole()],
        out_specs=whole(),
        compiler_params=params(8),
        cost_estimate=pl.CostEstimate(
            flops=8 * got.size, bytes_accessed=3 * got.size, transcendentals=got.size
        ),
        name="head_far",
    )(in_hbm(got))


def conv_far_kernel(*refs):
    first, second, (head_ref, out_ref) = refs[:8], refs[8:16], refs[16:]
    step = pl.program_id(0)
    blocks, each = head_ref.shape[1], first[0].shape[0]
    low = low_lanes((32, 128))

    @pl.when(step == 0)
    def _():
        out_ref[:, :blocks] = head_ref[...]

    for t in range(each):
        at = blocks + step * each + t
        for fz in range(2):
            for fy in range(2):
                a = sum(decode(ref[t, fz, fy]) for ref in first)
                b = sum(decode(ref[t, fz, fy]) for ref in second)
                out_ref[fy * 2 + fz, at] = encode(jnp.where(low, a, pltpu.roll(b, 64, 1)))
                out_ref[4 + fy * 2 + fz, at] = encode(jnp.where(low, pltpu.roll(a, 64, 1), b))


def conv_far(got, head):
    half = LAYERS * TAPS // 2
    steps = 3
    block = (half // steps, 2, 2, 32, 128)
    shape = (8, head.shape[1] + half, 32, 128)
    size = 8 * got[0].size
    return pl.pallas_call(
        conv_far_kernel,
        grid=(steps,),
        out_shape=jax.ShapeDtypeStruct(shape, BF16),
        in_specs=[pl.BlockSpec(block, lambda i: (i, 0, 0, 0, 0))] * 8
        + [pl.BlockSpec(block, lambda i: (i + steps, 0, 0, 0, 0))] * 8
        + [pl.BlockSpec(head.shape, lambda i: (0, 0, 0, 0))],
        out_specs=pl.BlockSpec(shape, lambda i: (0, 0, 0, 0)),
        compiler_params=params(8, "arbitrary"),
        cost_estimate=pl.CostEstimate(
            flops=8 * size, bytes_accessed=3 * size, transcendentals=size
        ),
        name="conv_far",
    )(*got, *got, head)


def finish_kernel(got_ref, conv_ref, head_ref):
    blocks = head_ref.shape[1] // 128
    for c in range(blocks):
        head_ref[:, c * 128 : (c + 1) * 128] = total_of(got_ref, c)
    half = LAYERS * TAPS // 2
    for t in range(half):
        total = total_of(got_ref, blocks + t)
        for tap, value in ((t, total), (t + half, pltpu.roll(total, 64, 1))):
            conv_ref[tap // TAPS, tap % TAPS] = value[:, :64]


def finish(got, scores):
    return pl.pallas_call(
        finish_kernel,
        out_shape=[
            jax.ShapeDtypeStruct((LAYERS, TAPS, 32, 64), F32),
            jax.ShapeDtypeStruct((32, scores // 8), F32),
        ],
        in_specs=[whole()],
        out_specs=[whole(), whole()],
        compiler_params=params(4),
        name="finish",
    )(got)


def swap(x):
    return lax.ppermute(x, AXES, other_core())


def on_device(student_in, teacher_rows, valid, conv_weight, head_weight, teacher_head_weight):
    _, frames, width = student_in.shape
    scores = head_weight.shape[1]
    loss_scale = scores / (3.0 * math.sqrt(READ * TM * frames))
    read, tm = (lax.axis_index(axis) for axis in AXES)
    core = read % 2
    even = 1 - core
    near_bits = (
        tm % 2 ^ read // 8 * even,
        tm // 4 ^ tm // 2 % 2 * even,
        read // 4 % 2 ^ read // 2 % 2 * even,
    )
    sc = jnp.stack([valid[0], tm, core, *near_bits])
    regrouped = regroup(student_in[0]).reshape(TM, frames // TM, width)
    student = exchange(regrouped, frame_groups()).reshape(frames, width)
    teacher = regroup(teacher_rows[0]).reshape(TM, frames // TM, -1)
    teacher = exchange(teacher, frame_groups()).reshape(frames, -1)

    saved, pre, hidden, h_mine, h_other = convolve(sc, student, conv_weight)
    h_got = swap(h_other)
    score, g = heads(
        sc, hidden, teacher, head_weight, teacher_head_weight, h_got, loss_scale
    )
    score_got = swap(score)
    send, mine = back(sc, g, saved, pre, conv_weight)
    got = swap(send)
    near = head_grad(sc, h_mine, h_got, score, score_got, mine)
    head_got = exchange(near.reshape(8, 4 * 32, scores // 4), near_groups())
    parts = conv_grad(sc, mine, send, got, near)
    conv_got = [parts[0]] + [near_swap(parts[i], i) for i in (1, 2, 7, 6, 5, 3, 4)]

    far = head_far(head_got.reshape(8, 2, 2, 32, scores // 4))
    far = conv_far(conv_got, far)
    return tuple(finish(exchange(far, far_groups()), scores))


def solution(mesh):
    return jax.shard_map(
        on_device,
        mesh=mesh,
        in_specs=(P("read", "tm", None), P("read", "tm", None), P("read"), P(), P(), P()),
        out_specs=(P(None, None, "read", "tm"), P("read", "tm")),
        check_vma=False,
    )
```

```python
import functools
import math

import jax
import jax.numpy as jnp
from jax import lax
from jax.experimental import pallas as pl
from jax.experimental.pallas import tpu as pltpu
from jax.sharding import PartitionSpec as P

LAYERS, TAPS = 4, 3
BASE_DILATION = 32
AXES = ("read", "tm")
READ, TM = 16, 8
CLASSES = BASE_DILATION // TM
PAD = CLASSES * 2 ** (LAYERS - 1)
BITS = [(a, b, c) for a in range(2) for b in range(2) for c in range(2)]
F32, BF16 = jnp.float32, jnp.bfloat16


def near_of(core, v):
    return (v // 2) ^ (v % 2) if core == 0 else v // 2


def far_of(core, v):
    return v // 2 if core == 0 else (v // 2) ^ (v % 2)


def high_low(core, near, far):
    return (far if core == 0 else near, near ^ far)


def device_index(x, y, z, core):
    return (((x % 2) * 4 + z) * 2 + core) * TM + y * 2 + x // 2


def groups_of(fixed, order):
    groups = {}
    for core in range(2):
        for x in range(4):
            for y in range(4):
                for z in range(4):
                    key = (core, fixed(core, x), fixed(core, y), fixed(core, z))
                    place = order(core, x) * 4 + order(core, y) * 2 + order(core, z)
                    groups.setdefault(key, [0] * 8)[place] = device_index(x, y, z, core)
    return list(groups.values())


def near_groups():
    def cube(core, v):
        return (v + core) % 4 // 2

    return groups_of(cube, near_of)


def near_swap(x, bits):
    pairs = [(group[i], group[i ^ bits]) for group in near_groups() for i in range(8)]
    return lax.ppermute(x, AXES, pairs)


def far_groups():
    return groups_of(near_of, far_of)


def other_core():
    return [(d, d ^ TM) for d in range(READ * TM)]


def frame_groups():
    return [[r * TM + t for t in range(TM)] for r in range(READ)]


def exchange(x, groups):
    return lax.all_to_all(x, AXES, 0, 0, tiled=True, axis_index_groups=groups)


def encode(x):
    return (x * jnp.abs(x)).astype(BF16)


def decode(y):
    y = y.astype(F32)
    return y * lax.rsqrt(jnp.maximum(jnp.abs(y), 1e-37))


def low_lanes(shape):
    return lax.broadcasted_iota(jnp.int32, shape, len(shape) - 1) < 64


def dot(a, b):
    return jnp.dot(a, b, preferred_element_type=F32)


def dot_nt(a, b):
    return lax.dot_general(a, b, (((1,), (1,)), ((), ())), preferred_element_type=F32)


def params(mib, *kinds):
    return pltpu.CompilerParams(dimension_semantics=kinds, vmem_limit_bytes=mib * 1024 * 1024)


def whole():
    return pl.BlockSpec(memory_space=pltpu.VMEM)


def in_hbm(x):
    return pltpu.with_memory_space_constraint(x, pltpu.HBM)


AFTER = pl.BlockSpec(memory_space=pl.ANY)


def frame_mask(sc_ref, frames):
    row = lax.broadcasted_iota(jnp.int32, (frames, 1), 0)
    position = row // CLASSES * BASE_DILATION + sc_ref[1] * CLASSES + row % CLASSES
    return (position < sc_ref[0]).astype(F32)


def regroup_kernel(x_ref, out_ref):
    frames = x_ref.shape[0]
    row = lax.broadcasted_iota(jnp.int32, (frames, frames), 0)
    col = lax.broadcasted_iota(jnp.int32, (frames, frames), 1)
    per = frames // TM
    source = (row % per) // CLASSES * BASE_DILATION + row // per * CLASSES + row % CLASSES
    select = jnp.where(col == source, 1.0, 0.0).astype(BF16)
    out_ref[...] = dot(select, x_ref[...]).astype(BF16)


def regroup(x):
    return pl.pallas_call(
        regroup_kernel,
        out_shape=jax.ShapeDtypeStruct(x.shape, BF16),
        in_specs=[whole()],
        out_specs=whole(),
        compiler_params=params(5),
        name="regroup",
    )(x)


def split_rows(core, ht_s, mine_ref, other_ref):
    for ref, owner in ((mine_ref, core), (other_ref, 1 - core)):
        for at, (nz, fz, xl) in enumerate(BITS):
            high = jnp.where(owner == 0, fz, nz)
            row = ((xl * 4 + high * 2 + (nz ^ fz)) * 2 + owner) * 32
            ref[at * 32 : (at + 1) * 32] = ht_s[pl.ds(pl.multiple_of(row, 32), 32)]


def conv_kernel(sc_ref, x_ref, w_ref, saved_ref, pre_ref, last_ref, mine_ref, other_ref, pad_s, tap_s, ht_s):
    layer = pl.program_id(0)
    frames, width = x_ref.shape

    @pl.when(layer == 0)
    def _():
        pad_s[...] = jnp.zeros_like(pad_s)
        pad_s[PAD : PAD + frames] = x_ref[...]

    for at in range(LAYERS):

        @pl.when(layer == at)
        def _():
            reach = CLASSES * 2**at
            tap_s[:, :width] = pad_s[PAD - reach : PAD - reach + frames]
            tap_s[:, 2 * width :] = pad_s[PAD + reach : PAD + reach + frames]

    middle = pad_s[PAD : PAD + frames]
    saved_ref[0] = middle
    tap_s[:, width : 2 * width] = middle
    pre = dot(tap_s[...], w_ref[0].reshape(TAPS * width, width))
    pre_ref[0] = pre
    new = (frame_mask(sc_ref, frames) * (middle.astype(F32) + jax.nn.silu(pre))).astype(BF16)
    pad_s[PAD : PAD + frames] = new

    @pl.when(layer == LAYERS - 1)
    def _():
        last_ref[...] = new
        ht_s[...] = new.T
        split_rows(sc_ref[2], ht_s, mine_ref, other_ref)


def convolve(sc, x, weight):
    frames, width = x.shape
    one = pl.BlockSpec((1, frames, width), lambda i: (i, 0, 0))
    flat = pl.BlockSpec((frames, width), lambda i: (0, 0))
    rows = pl.BlockSpec((width // 2, frames), lambda i: (0, 0))
    return pl.pallas_call(
        conv_kernel,
        grid=(LAYERS,),
        in_specs=[
            pl.BlockSpec(memory_space=pltpu.SMEM),
            flat,
            pl.BlockSpec((1, TAPS, width, width), lambda i: (i, 0, 0, 0)),
        ],
        out_specs=[one, one, flat, rows, rows],
        out_shape=[
            jax.ShapeDtypeStruct((LAYERS, frames, width), BF16),
            pltpu.HBM((LAYERS, frames, width), F32),
            pltpu.HBM((frames, width), BF16),
            pltpu.HBM((width // 2, frames), BF16),
            pltpu.HBM((width // 2, frames), BF16),
        ],
        scratch_shapes=[
            pltpu.VMEM((frames + 2 * PAD, width), BF16),
            pltpu.VMEM((frames, TAPS * width), BF16),
            pltpu.VMEM((width, frames), BF16),
        ],
        compiler_params=params(14, "arbitrary"),
        cost_estimate=pl.CostEstimate(
            flops=2 * LAYERS * TAPS * frames * width * width,
            bytes_accessed=LAYERS * (TAPS * width * width * 2 + frames * width * 6),
            transcendentals=LAYERS * frames * width,
        ),
        name="convolve",
    )(sc, x, in_hbm(weight))


def head_kernel(scale, tiles, sc_ref, h_ref, t_ref, ws_ref, wt_ref, _, score_ref, g_ref,
                sq_s, et_s, sum_s):
    step = pl.program_id(0)
    frames, width = h_ref.shape
    tile = ws_ref.shape[1]
    sub = 256

    @pl.when(step == 0)
    def _():
        sum_s[...] = jnp.zeros_like(sum_s)

    @pl.when(step < tiles)
    def _():
        for c in range(tile // sub):
            cols = slice(c * sub, (c + 1) * sub)
            squash = jnp.tanh(dot(h_ref[...], ws_ref[:, cols]))
            exp_s = jnp.exp(5.0 * squash)
            sq_s[step, :, cols] = squash
            sum_s[0] += exp_s[:, :128] + exp_s[:, 128:]
            exp_t = jnp.exp(5.0 * jnp.tanh(dot(t_ref[...], wt_ref[:, cols])))
            et_s[step, :, cols] = exp_t
            sum_s[1] += exp_t[:, :128] + exp_t[:, 128:]

    @pl.when(step == tiles)
    def _():
        factor = scale * frame_mask(sc_ref, frames)
        for i in range(2):
            inverse = factor / jnp.sum(sum_s[i], axis=1, keepdims=True)
            sum_s[i] = jnp.broadcast_to(inverse, (frames, 128))
        g_ref[...] = jnp.zeros_like(g_ref)

    @pl.when(step >= tiles)
    def _():
        at = step - tiles
        for c in range(tile // 128):
            cols = slice(c * 128, (c + 1) * 128)
            squash = sq_s[at, :, cols]
            p = jnp.exp(5.0 * squash) * sum_s[0] - et_s[at, :, cols] * sum_s[1]
            score_ref[:, cols] = (p * (1.0 - squash * squash)).astype(BF16)
        g_ref[...] += dot_nt(score_ref[...], ws_ref[...])


def heads(sc, hidden, teacher_in, head_weight, teacher_head_weight, after, loss_scale):
    frames, width = hidden.shape
    wide = teacher_in.shape[1]
    scores = head_weight.shape[1]
    tiles = 4
    tile = scores // tiles
    big = pltpu.VMEM((tiles, frames, tile), F32)
    return pl.pallas_call(
        functools.partial(head_kernel, 5.0 * loss_scale, tiles),
        grid=(2 * tiles,),
        in_specs=[
            pl.BlockSpec(memory_space=pltpu.SMEM),
            pl.BlockSpec((frames, width), lambda i: (0, 0)),
            pl.BlockSpec((frames, wide), lambda i: (0, 0)),
            pl.BlockSpec((width, tile), lambda i: (0, i % tiles)),
            pl.BlockSpec((wide, tile), lambda i: (0, jnp.minimum(i, tiles - 1))),
            AFTER,
        ],
        out_specs=[
            pl.BlockSpec((frames, tile), lambda i: (0, jnp.maximum(i - tiles, 0))),
            pl.BlockSpec((frames, width), lambda i: (0, 0)),
        ],
        scratch_shapes=[
            big,
            big,
            pltpu.VMEM((2, frames, 128), F32),
        ],
        out_shape=[
            jax.ShapeDtypeStruct((frames, scores), BF16),
            jax.ShapeDtypeStruct((frames, width), F32),
        ],
        compiler_params=params(37, "arbitrary"),
        cost_estimate=pl.CostEstimate(
            flops=2 * frames * scores * (2 * width + wide),
            bytes_accessed=scores * (6 * width + 2 * wide),
            transcendentals=4 * frames * scores,
        ),
        name="heads",
    )(sc, in_hbm(hidden), teacher_in, in_hbm(head_weight), in_hbm(teacher_head_weight), after)


def head_grad_kernel(sc_ref, ha_ref, hb_ref, ga_ref, gb_ref, _, out_ref, res_s):
    half = ga_ref.shape[1] // 2
    first = sc_ref[2] == 0
    for c in range(half // 128):
        cols = [slice(x * half + c * 128, x * half + (c + 1) * 128) for x in range(2)]
        ga, gb = (jnp.concatenate([ref[:, at] for at in cols], axis=1) for ref in (ga_ref, gb_ref))
        res_s[c] = dot(ha_ref[...], ga) + dot(hb_ref[...], gb)
        for nx, nz, fz in BITS:
            for fx in range(2):
                row = ((nz * 2 + fz) * 2 + (nx ^ fx)) * 32
                rows = slice(row, row + 32)
                value = res_s[c, rows, fx * 128 : (fx + 1) * 128]
                if nx != fx:
                    value = jnp.where(first, value, res_s[c, rows, nx * 128 : (nx + 1) * 128])
                out_ref[nx, 0, nz, fz, 0, :, cols[fx]] = encode(value)


def head_grad(sc, h_mine, h_other, score_mine, score_other, after):
    rows, frames = h_mine.shape
    scores = score_mine.shape[1]
    tile = scores // 4

    def place(i, sc):
        high, low = i // 2, i % 2
        even = sc[2] == 0
        return (0, jnp.where(even, high ^ low, high), 0, 0, jnp.where(even, high, high ^ low), 0, 0)

    hidden = pl.BlockSpec((rows, frames), lambda i, sc: (0, 0))
    score = pl.BlockSpec((frames, tile), lambda i, sc: (0, i))
    return pl.pallas_call(
        head_grad_kernel,
        grid_spec=pltpu.PrefetchScalarGridSpec(
            num_scalar_prefetch=1,
            grid=(4,),
            in_specs=[hidden, hidden, score, score, AFTER],
            out_specs=pl.BlockSpec((2, 1, 2, 2, 1, 32, tile), place),
            scratch_shapes=[pltpu.VMEM((tile // 256, rows, 256), F32)],
        ),
        out_shape=jax.ShapeDtypeStruct((2, 2, 2, 2, 2, 32, tile), BF16),
        compiler_params=params(13, "arbitrary"),
        cost_estimate=pl.CostEstimate(
            flops=4 * rows * frames * scores,
            bytes_accessed=4 * frames * scores + 2 * rows * scores,
            transcendentals=0,
        ),
        name="head_grad",
    )(sc, h_mine, h_other, score_mine, score_other, in_hbm(after))


def back_kernel(sc_ref, g4_ref, h_ref, pre_ref, w_ref, send_ref, mine_ref, g_s, pad_s, tap_s, ht_s):
    step = pl.program_id(0)
    frames, width = g4_ref.shape

    @pl.when(step == 0)
    def _():
        g_s[...] = g4_ref[...]
        pad_s[...] = jnp.zeros_like(pad_s)

    g_act = frame_mask(sc_ref, frames) * g_s[...]
    pre = pre_ref[0]
    sigma = jax.nn.sigmoid(pre)
    g_pre = (g_act * sigma * (1.0 + pre * (1.0 - sigma))).astype(BF16)
    send_ref[0, :2] = g_pre.reshape(2, frames // 2, width)
    ht_s[...] = h_ref[0].T
    split_rows(sc_ref[2], ht_s, mine_ref.at[0], send_ref.at[0, 2])

    @pl.when(step < LAYERS - 1)
    def _():
        pad_s[PAD : PAD + frames] = g_pre
        for at in range(LAYERS - 1, 0, -1):

            @pl.when(step == LAYERS - 1 - at)
            def _():
                reach = CLASSES * 2**at
                tap_s[0] = pad_s[PAD + reach : PAD + reach + frames]
                tap_s[1] = pad_s[PAD - reach : PAD - reach + frames]

        g_s[...] = (
            g_act
            + dot_nt(tap_s[0], w_ref[0, 0])
            + dot_nt(g_pre, w_ref[0, 1])
            + dot_nt(tap_s[1], w_ref[0, 2])
        )


def back(sc, g, saved, pre, weight):
    frames, width = g.shape

    def at(*block):
        return pl.BlockSpec((1, *block), lambda i: (LAYERS - 1 - i, *(0 for _ in block)))

    return pl.pallas_call(
        back_kernel,
        grid=(LAYERS,),
        in_specs=[
            pl.BlockSpec(memory_space=pltpu.SMEM),
            pl.BlockSpec((frames, width), lambda i: (0, 0)),
            at(frames, width),
            at(frames, width),
            pl.BlockSpec(
                (1, TAPS, width, width), lambda i: (jnp.maximum(LAYERS - 1 - i, 1), 0, 0, 0)
            ),
        ],
        out_specs=[at(3, frames // 2, width), at(width // 2, frames)],
        out_shape=[
            jax.ShapeDtypeStruct((LAYERS, 3, frames // 2, width), BF16),
            pltpu.HBM((LAYERS, width // 2, frames), BF16),
        ],
        scratch_shapes=[
            pltpu.VMEM((frames, width), F32),
            pltpu.VMEM((frames + 2 * PAD, width), BF16),
            pltpu.VMEM((2, frames, width), BF16),
            pltpu.VMEM((width, frames), BF16),
        ],
        compiler_params=params(16, "arbitrary"),
        cost_estimate=pl.CostEstimate(
            flops=2 * (LAYERS - 1) * TAPS * frames * width * width,
            bytes_accessed=LAYERS * (TAPS * width * width * 2 + frames * width * 10),
            transcendentals=LAYERS * frames * width,
        ),
        name="back",
    )(sc, g, saved, pre, weight)


def conv_grad_kernel(sc_ref, mine_ref, send_ref, got_ref, _, *refs):
    outs, (pad_s, tap_s, left_s), results = refs[:8], refs[8:11], refs[11:]
    step = pl.program_id(0)
    frames = mine_ref.shape[2]
    width = send_ref.shape[3]

    @pl.when(step == 0)
    def _():
        pad_s[...] = jnp.zeros_like(pad_s)

    for side, ref in enumerate((send_ref, got_ref)):
        g_pre = ref[0, :2].reshape(frames, width)
        tap_s[1, side * frames : (side + 1) * frames] = g_pre
        pad_s[side, PAD : PAD + frames] = g_pre
    for at in range(LAYERS):

        @pl.when(step == at)
        def _():
            reach = CLASSES * 2**at
            for side in range(2):
                rows = slice(side * frames, (side + 1) * frames)
                tap_s[0, rows] = pad_s[side, PAD + reach : PAD + reach + frames]
                tap_s[2, rows] = pad_s[side, PAD - reach : PAD - reach + frames]

    core, mx, my, mz = (sc_ref[i] for i in range(2, 6))
    side = lax.broadcasted_iota(jnp.int32, (32, 128), 1) // 64
    straight, crossed = side == mx, side != mx
    left_s[:, :frames] = mine_ref[0]
    left_s[:, frames:] = got_ref[0, 2]
    for tap, res_s in enumerate(results):
        res_s[...] = dot(left_s[...], tap_s[tap])
        for dy, dz, fz in BITS:
            for fy in range(2):
                ny, nz = my ^ dy, mz ^ dz
                high = jnp.where(core == 0, fy, ny)
                cols = pl.ds(pl.multiple_of((high * 2 + (ny ^ fy)) * 128, 128), 128)
                row = pl.multiple_of((nz * 2 + fz) * 64, 64)
                a = res_s[pl.ds(row, 32), cols]
                b = pltpu.roll(res_s[pl.ds(row + 32, 32), cols], 64 * core, 1)
                outs[dy * 2 + dz][tap, fz, fy] = encode(jnp.where(straight, a, b))
                outs[4 + dy * 2 + dz][tap, fz, fy] = encode(jnp.where(crossed, a, b))


def conv_grad(sc, mine, send, got, after):
    _, rows, frames = mine.shape
    width = send.shape[3]

    def at(*block):
        return pl.BlockSpec((1, *block), lambda i: (i, *(0 for _ in block)))

    out = pl.BlockSpec((TAPS, 2, 2, 32, width // 4), lambda i: (i, 0, 0, 0, 0))
    return pl.pallas_call(
        conv_grad_kernel,
        grid=(LAYERS,),
        in_specs=[
            pl.BlockSpec(memory_space=pltpu.SMEM),
            at(rows, frames),
            at(3, frames // 2, width),
            at(3, frames // 2, width),
            AFTER,
        ],
        out_specs=[out] * 8,
        out_shape=[jax.ShapeDtypeStruct((LAYERS * TAPS, 2, 2, 32, width // 4), BF16)] * 8,
        scratch_shapes=[
            pltpu.VMEM((2, frames + 2 * PAD, width), BF16),
            pltpu.VMEM((TAPS, 2 * frames, width), BF16),
            pltpu.VMEM((rows, 2 * frames), BF16),
        ]
        + [pltpu.VMEM((rows, width), F32)] * TAPS,
        compiler_params=params(18, "arbitrary"),
        cost_estimate=pl.CostEstimate(
            flops=4 * LAYERS * TAPS * rows * frames * width,
            bytes_accessed=LAYERS * (7 * rows * frames * 2 + TAPS * rows * width * 2),
            transcendentals=0,
        ),
        name="conv_grad",
    )(sc, mine, send, got, in_hbm(after))


def total_of(ref, *at):
    total = decode(ref[(0, *at)])
    for i in range(1, 8):
        total = total + decode(ref[(i, *at)])
    return total


def head_far_kernel(got_ref, out_ref):
    half = got_ref.shape[-1] // 2
    for fz, fy, fx in BITS:
        for c in range(half // 128):
            lanes = slice(fx * half + c * 128, fx * half + (c + 1) * 128)
            out_ref[fx * 4 + fy * 2 + fz, c] = encode(total_of(got_ref, fz, fy, slice(None), lanes))


def head_far(got):
    tile = got.shape[-1]
    return pl.pallas_call(
        head_far_kernel,
        out_shape=jax.ShapeDtypeStruct((8, tile // 256, 32, 128), BF16),
        in_specs=[whole()],
        out_specs=whole(),
        compiler_params=params(8),
        cost_estimate=pl.CostEstimate(
            flops=8 * got.size, bytes_accessed=3 * got.size, transcendentals=got.size
        ),
        name="head_far",
    )(in_hbm(got))


def conv_far_kernel(*refs):
    first, second, (head_ref, out_ref) = refs[:8], refs[8:16], refs[16:]
    step = pl.program_id(0)
    blocks, each = head_ref.shape[1], first[0].shape[0]
    low = low_lanes((32, 128))

    @pl.when(step == 0)
    def _():
        out_ref[:, :blocks] = head_ref[...]

    for t in range(each):
        at = blocks + step * each + t
        for fz in range(2):
            for fy in range(2):
                a = sum(decode(ref[t, fz, fy]) for ref in first)
                b = sum(decode(ref[t, fz, fy]) for ref in second)
                out_ref[fy * 2 + fz, at] = encode(jnp.where(low, a, pltpu.roll(b, 64, 1)))
                out_ref[4 + fy * 2 + fz, at] = encode(jnp.where(low, pltpu.roll(a, 64, 1), b))


def conv_far(got, head):
    half = LAYERS * TAPS // 2
    steps = 3
    block = (half // steps, 2, 2, 32, 128)
    shape = (8, head.shape[1] + half, 32, 128)
    size = 8 * got[0].size
    return pl.pallas_call(
        conv_far_kernel,
        grid=(steps,),
        out_shape=jax.ShapeDtypeStruct(shape, BF16),
        in_specs=[pl.BlockSpec(block, lambda i: (i, 0, 0, 0, 0))] * 8
        + [pl.BlockSpec(block, lambda i: (i + steps, 0, 0, 0, 0))] * 8
        + [pl.BlockSpec(head.shape, lambda i: (0, 0, 0, 0))],
        out_specs=pl.BlockSpec(shape, lambda i: (0, 0, 0, 0)),
        compiler_params=params(8, "arbitrary"),
        cost_estimate=pl.CostEstimate(
            flops=8 * size, bytes_accessed=3 * size, transcendentals=size
        ),
        name="conv_far",
    )(*got, *got, head)


def finish_kernel(got_ref, conv_ref, head_ref):
    blocks = head_ref.shape[1] // 128
    for c in range(blocks):
        head_ref[:, c * 128 : (c + 1) * 128] = total_of(got_ref, c)
    half = LAYERS * TAPS // 2
    for t in range(half):
        total = total_of(got_ref, blocks + t)
        for tap, value in ((t, total), (t + half, pltpu.roll(total, 64, 1))):
            conv_ref[tap // TAPS, tap % TAPS] = value[:, :64]


def finish(got, scores):
    return pl.pallas_call(
        finish_kernel,
        out_shape=[
            jax.ShapeDtypeStruct((LAYERS, TAPS, 32, 64), F32),
            jax.ShapeDtypeStruct((32, scores // 8), F32),
        ],
        in_specs=[whole()],
        out_specs=[whole(), whole()],
        compiler_params=params(4),
        name="finish",
    )(got)


def swap(x):
    return lax.ppermute(x, AXES, other_core())


def on_device(student_in, teacher_rows, valid, conv_weight, head_weight, teacher_head_weight):
    _, frames, width = student_in.shape
    scores = head_weight.shape[1]
    loss_scale = scores / (3.0 * math.sqrt(READ * TM * frames))
    read, tm = (lax.axis_index(axis) for axis in AXES)
    core = read % 2
    even = 1 - core
    near_bits = (
        tm % 2 ^ read // 8 * even,
        tm // 4 ^ tm // 2 % 2 * even,
        read // 4 % 2 ^ read // 2 % 2 * even,
    )
    sc = jnp.stack([valid[0], tm, core, *near_bits])
    regrouped = regroup(student_in[0]).reshape(TM, frames // TM, width)
    student = exchange(regrouped, frame_groups()).reshape(frames, width)
    teacher = regroup(teacher_rows[0]).reshape(TM, frames // TM, -1)
    teacher = exchange(teacher, frame_groups()).reshape(frames, -1)

    saved, pre, hidden, h_mine, h_other = convolve(sc, student, conv_weight)
    h_got = swap(h_other)
    score, g = heads(
        sc, hidden, teacher, head_weight, teacher_head_weight, h_got, loss_scale
    )
    score_got = swap(score)
    send, mine = back(sc, g, saved, pre, conv_weight)
    got = swap(send)
    near = head_grad(sc, h_mine, h_got, score, score_got, mine)
    head_got = exchange(near.reshape(8, 4 * 32, scores // 4), near_groups())
    parts = conv_grad(sc, mine, send, got, near)
    conv_got = [parts[0]] + [near_swap(parts[i], i) for i in (1, 2, 7, 6, 5, 3, 4)]

    far = head_far(head_got.reshape(8, 2, 2, 32, scores // 4))
    far = conv_far(conv_got, far)
    return tuple(finish(exchange(far, far_groups()), scores))


def solution(mesh):
    return jax.shard_map(
        on_device,
        mesh=mesh,
        in_specs=(P("read", "tm", None), P("read", "tm", None), P("read"), P(), P(), P()),
        out_specs=(P(None, None, "read", "tm"), P("read", "tm")),
        check_vma=False,
    )
```
